256 devices in a mesh: epoch: 8 (over z_lo, core), prow: 8 (over z_hi, x), pcol: 4 (over y).
Axes of the slice: x: 4, y: 4, z: 8 (z_hi: 2, z_lo: 4; z = z_hi * 4 + z_lo), core: 2. Of those that a mesh axis runs over, the one named last changes fastest.
Arguments:
- steps: int32 [2, 16384], P(None, 'epoch'), may hold values from 0 to 47
- harmonic: int32 [4096], replicated, may hold values from 0 to 4095, each once
- col_scale: float32 [4096], replicated, may hold values from 0.3 to 3
- taps: float32 [256], replicated, may hold values from -0.375 to 0.375
- ridge: float32 [4096], P(('epoch', 'prow')), may hold values from 0.1 to 1
Outputs:
- panel: float32 [4096, 256], P(('epoch', 'prow'))
- schur: float32 [4096, 4096], P(('epoch', 'prow'), 'pcol')
The draws below stay inside these ranges and needn't reach their ends.
Inputs may be any that keep to these rules, and one draw needn't show every extreme that they name: `harmonic`: each of 0 to 4095 once.
All inputs are finite; a program needn't handle non-finite values.
Results may differ from the reference program's by a relative error of at most 0.0028.
Values may be sent and summed in bfloat16 or wider, within the bound.
A program may use at most 64 MiB of HBM per device.

```python
import math
import jax
import jax.numpy as jnp
from jax import lax

P_SIZE = 4096
B = 256
TAPS = 256
EPOCHS = 16384


def place_ends(drawn, own_key, least, top_value):
    dims = drawn.shape
    place = [jax.random.randint(jax.random.fold_in(own_key, axis), (), 0, dims[axis]) for axis in range(len(dims))]
    drawn = drawn.at[tuple(place)].set(least)
    longest = dims.index(max(dims))
    place[longest] = (place[longest] + 1) % dims[longest]
    return drawn.at[tuple(place)].set(top_value)


def block_levels(own_key, extent, shards, smallest, largest):
    level = 1.0
    for dim, blocks in shards:
        draws = jax.random.uniform(jax.random.fold_in(jax.random.fold_in(own_key, 6), dim), (blocks,), jnp.float32, smallest / len(shards), largest / len(shards))
        level = level * jnp.repeat(jnp.exp(draws), extent[dim] // blocks).reshape((-1,) + (1,) * (len(extent) - 1 - dim))
    return level


def normal_values(own_key, shape, spread, reach, kind=jnp.bfloat16):
    return jnp.clip(spread * jax.random.normal(own_key, shape, jnp.float32), -reach, reach).astype(kind)


def setup_inputs(seed: int = 0) -> dict:
    seeds = jax.random.split(jax.random.key(seed), 6)
    return {
        "steps": place_ends(jax.random.randint(seeds[0], (2, EPOCHS), 0, 48), jax.random.fold_in(seeds[0], 1), 0, 47).astype(jnp.int32),
        "harmonic": jax.random.permutation(seeds[1], P_SIZE).astype(jnp.int32),
        "col_scale": jnp.clip(jnp.exp(jax.random.uniform(seeds[2], (P_SIZE,), jnp.float32, math.log(0.3), math.log(3.0))), 0.3, 3.0),
        "taps": normal_values(seeds[3], (TAPS,), TAPS ** -0.5, 0.375, jnp.float32),
        "ridge": jnp.clip(jnp.exp(math.log(1.0) - 2.3025851 * jax.random.uniform(seeds[4], (P_SIZE,), jnp.float32) ** block_levels(seeds[4], (P_SIZE,), ((0, 64),), -0.2, 0.2)), 0.1, 1.0),
    }


phase_count = 4096
angle_step = 2.0 * math.pi / 4096.0

def toeplitz_pair(taps):
    count = taps.shape[0]
    pattern = jnp.concatenate([jnp.zeros((1,), jnp.float32), taps[::-1], jnp.zeros((count,), jnp.float32)])
    full = jnp.tile(pattern, count)[:2 * count * count].reshape(count, 2 * count).astype(jnp.bfloat16)
    return (full[:, :count], full[:, count:])

def harmonic_design(phase_first, phase_second, orders, degrees, scales):
    indices = (phase_first[:, None] * orders[None, :] + phase_second[:, None] * degrees[None, :]) % phase_count
    angle = indices.astype(jnp.float32) * angle_step
    return (jnp.cos(angle) + jnp.sin(angle)) * scales[None, :]

def reference(steps, harmonic, col_scale, taps, ridge):
    phase = (jnp.cumsum(steps, axis=1) % phase_count).astype(jnp.int32)
    orders = (harmonic // 64).astype(jnp.int32)
    degrees = (harmonic % 64).astype(jnp.int32)
    design = harmonic_design(phase[0], phase[1], orders, degrees, col_scale).astype(jnp.bfloat16)
    joined = jnp.concatenate([jnp.zeros((TAPS, P_SIZE), jnp.bfloat16), design], axis=0)
    blocks = EPOCHS // TAPS
    earlier_rows = joined[:EPOCHS].reshape(blocks, TAPS, P_SIZE).astype(jnp.float32)
    current_rows = joined[TAPS:].reshape(blocks, TAPS, P_SIZE).astype(jnp.float32)
    lower_part, upper_part = toeplitz_pair(taps)
    filtered = jnp.einsum('ij,bjc->bic', lower_part.astype(jnp.float32), earlier_rows)
    filtered = filtered + jnp.einsum('ij,bjc->bic', upper_part.astype(jnp.float32), current_rows)
    filtered = filtered.reshape(EPOCHS, P_SIZE).astype(jnp.bfloat16)
    normal = jnp.dot(filtered.T.astype(jnp.float32), filtered.astype(jnp.float32), preferred_element_type=jnp.float32) / EPOCHS
    normal = normal + jnp.diag(ridge)
    leading = jnp.linalg.cholesky(normal[:B, :B])
    panel = jax.scipy.linalg.solve_triangular(leading, normal[:, :B].T, lower=True).T
    schur = normal - jnp.dot(panel.astype(jnp.float32), panel.T.astype(jnp.float32), precision=lax.Precision.HIGHEST, preferred_element_type=jnp.float32)
    return (panel, schur)
```

```python
import functools

import jax
import jax.numpy as jnp
from jax import lax
from jax.experimental import pallas as pl
from jax.experimental.pallas import tpu as pltpu
from jax.sharding import PartitionSpec as P

F32 = jnp.float32
BF16 = jnp.bfloat16
MESH = pl.DeviceIdType.MESH
HIGH = lax.Precision.HIGHEST
B = 256
BLK = 256
PERIOD = 4096
NX = 4
WAVE = (8.88573567404434, -58.45953046181323, 115.03267724691959, -100.39492606524867)
ROUND = 12582912.0
VMEM = pl.BlockSpec(memory_space=pltpu.VMEM)


def place():
    e, p, y = (lax.axis_index(a) for a in ("epoch", "prow", "pcol"))
    core, z_lo = e % 2, e // 2
    x, z_hi = p % NX, p // NX
    return x, y, z_hi * 4 + z_lo, core


def device(x, z, core):
    return {"epoch": (z % 4) * 2 + core, "prow": (z // 4) * NX + x}


def phase_kernel(steps_ref, phase_ref, every, send, recv):
    e = lax.axis_index("epoch")
    n = 8
    barrier = pltpu.get_barrier_semaphore()
    for i in range(1, n):
        pl.semaphore_signal(barrier, inc=1, device_id={"epoch": (e + i) % n}, device_id_type=MESH)
    pl.semaphore_wait(barrier, n - 1)
    copies = []
    for i in range(1, n):
        copy = pltpu.make_async_remote_copy(
            src_ref=steps_ref,
            dst_ref=every.at[e],
            send_sem=send.at[i],
            recv_sem=recv.at[i],
            device_id={"epoch": (e + i) % n},
            device_id_type=MESH,
        )
        copy.start()
        copies.append(copy)
    every[e] = steps_ref[...]
    tiles = steps_ref.shape[1]
    rows = n * 2 * tiles
    upper = (
        lax.broadcasted_iota(jnp.int32, (128, 128), 0)
        <= lax.broadcasted_iota(jnp.int32, (128, 128), 1)
    ).astype(BF16)
    r = lax.broadcasted_iota(jnp.int32, (rows, rows), 0)
    s = lax.broadcasted_iota(jnp.int32, (rows, rows), 1)
    same = (r // tiles) % 2 == (s // tiles) % 2
    key_r = (r // (2 * tiles)) * tiles + r % tiles
    key_s = (s // (2 * tiles)) * tiles + s % tiles
    before = jnp.where(same & (key_s < key_r), 1.0, 0.0).astype(F32)
    for copy in copies:
        copy.wait()
    x = every[...].reshape(rows, 128).astype(F32).astype(BF16)
    inside = jnp.dot(x, upper, preferred_element_type=F32)
    totals = jnp.broadcast_to(inside[:, 127:128], (rows, 128))
    earlier = jnp.dot(before, totals, precision=HIGH, preferred_element_type=F32)
    whole = (inside + earlier).astype(jnp.int32)
    phase_ref[...] = (whole & (PERIOD - 1)).astype(F32) * (1.0 / PERIOD)


def wave(turn, scale):
    turn = turn - 0.125
    whole = (turn + ROUND) - ROUND
    z = 0.25 - jnp.abs(turn - whole)
    s = z * z
    poly = WAVE[3]
    for c in (WAVE[2], WAVE[1], WAVE[0]):
        poly = poly * s + c
    return poly * (z * scale)


def tile_kernel(
    phase_ref, harm_ref, scale_ref, taps_ref, lead_ref, own_ref,
    colf, rowf, lowt, lowr, dcol, drow, fcol, frow,
):
    x, y, z, core = place()
    group = ((z % 4) * 2 + core) * 2 + z // 4
    blocks = (phase_ref.shape[0] // 4) // NX
    n_rows = rowf.shape[1]
    n_lead = n_rows - 256
    n_tiles = colf.shape[1]
    cols_here = n_tiles - 2

    def features(k):
        h = harm_ref[pl.ds(k, 1), :]
        return (
            lax.shift_right_logical(h, 6).astype(F32),
            (h & 63).astype(F32),
            scale_ref[pl.ds(k, 1), :],
        )

    def down(row):
        return jnp.transpose(jnp.broadcast_to(row, (128, 128)))

    for jt in range(n_tiles):
        k = jt if jt < 2 else y * cols_here + (jt - 2)
        for f, v in enumerate(features(k)):
            colf[f, jt] = v
    for half in range(2):
        for f, v in enumerate(features(group * 2 + half)):
            rowf[f, half * 128 : half * 128 + 128, :] = down(v)
    per = 128 // n_lead
    for f, v in enumerate(features(group // per)):
        lowr[...] = down(v)
        rowf[f, 256:, :] = lowr[pl.ds(pl.multiple_of((group % per) * n_lead, n_lead), n_lead), :]

    base = jnp.concatenate([taps_ref[0:1, :], taps_ref[1:2, :], jnp.zeros((1, 256), F32)], axis=1)
    full = pltpu.roll(
        jnp.broadcast_to(base, (512, 512)), 256, 1, stride=1, stride_axis=0
    )[:, :256]
    low_up = jnp.transpose(full).astype(BF16)
    lowt[...] = full.astype(BF16)

    @pl.loop(0, blocks + 1)
    def _(b):
        at = x * blocks + b - 1
        present = at >= 0
        at = jnp.maximum(at, 0)
        row0 = (at // 8) * 32 + (at % 8) * 2
        for half in range(2):
            q0 = phase_ref[pl.ds(row0 + half, 1), :]
            q1 = phase_ref[pl.ds(row0 + 16 + half, 1), :]
            q0d, q1d = down(q0), down(q1)
            where_t = pl.multiple_of(b * BLK + half * 128, 128)
            for jt in range(n_tiles):
                d = wave(q0d * colf[0, jt] + q1d * colf[1, jt], colf[2, jt])
                d = jnp.where(present, d, 0.0)
                dcol[pl.ds(where_t, 128), jt * 128 : jt * 128 + 128] = d.astype(BF16)
            for r0 in range(0, n_rows, 128):
                r1 = min(r0 + 128, n_rows)
                d = wave(q0 * rowf[0, r0:r1, :] + q1 * rowf[1, r0:r1, :], rowf[2, r0:r1, :])
                d = jnp.where(present, d, 0.0)
                drow[r0:r1, pl.ds(where_t, 128)] = d.astype(BF16)

    lowr2 = low_up

    @pl.loop(0, blocks)
    def _(b):
        t0 = pl.multiple_of(b * BLK, BLK)
        for j0 in range(0, n_tiles * 128, 256):
            f = jnp.dot(
                lowr2, dcol[pl.ds(t0, 2 * BLK), j0 : j0 + 256], preferred_element_type=F32
            )
            fcol[pl.ds(t0, BLK), j0 : j0 + 256] = f.astype(BF16)
        f = jnp.dot(drow[:, pl.ds(t0, 2 * BLK)], lowt[...], preferred_element_type=F32)
        frow[:, pl.ds(t0, BLK)] = f.astype(BF16)

    total = 1.0 / (blocks * BLK * NX)
    for j0 in range(0, n_tiles * 128, 256):
        g = jnp.dot(frow[...], fcol[:, j0 : j0 + 256], preferred_element_type=F32) * total
        own_ref[:, :, j0 : j0 + 256] = g[:256].reshape(NX, 64, 256)
        lead_ref[:, :, j0 : j0 + 256] = g[256:].reshape(NX, n_lead // NX, 256)


def exchange_kernel(
    lead_ref, own_ref, ridge_ref, mine_ref, slab_ref,
    slab, got_lead, got_own, send_lead, recv_lead, send_own, recv_own,
    send_z, recv_z, send_x, recv_x, send_c, recv_c,
):
    x, y, z, core = place()
    nz = 8
    width = lead_ref.shape[2]
    barrier = pltpu.get_barrier_semaphore()
    peers = [device((x + i) % NX, z, core) for i in range(1, NX)]
    tall = [device(x, (z + i) % nz, core) for i in range(1, nz)]
    other = device(x, z, 1 - core)
    for peer in peers + tall + [other]:
        pl.semaphore_signal(barrier, inc=1, device_id=peer, device_id_type=MESH)
    pl.semaphore_wait(barrier, len(peers) + len(tall) + 1)

    def put(src, dst, send, recv, peer):
        copy = pltpu.make_async_remote_copy(
            src_ref=src, dst_ref=dst, send_sem=send, recv_sem=recv,
            device_id=peer, device_id_type=MESH,
        )
        copy.start()
        return copy

    first = [
        put(lead_ref.at[(x + i) % NX], got_lead.at[i - 1], send_lead.at[i - 1], recv_lead.at[i - 1], peers[i - 1])
        for i in range(1, NX)
    ]
    owns = [
        put(own_ref.at[(x + i) % NX], got_own.at[i - 1], send_own.at[i - 1], recv_own.at[i - 1], peers[i - 1])
        for i in range(1, NX)
    ]
    for copy in first:
        copy.wait()
    slab[x, core, z, :, :width] = lead_ref[x] + got_lead[0] + got_lead[1] + got_lead[2]
    slab[x, core, z, :, width:] = jnp.broadcast_to(ridge_ref[...], (lead_ref.shape[1], 128))
    second = [
        put(slab.at[x, core, z], slab.at[x, core, z], send_z.at[i - 1], recv_z.at[i - 1], tall[i - 1])
        for i in range(1, nz)
    ]
    for copy in second:
        copy.wait()
    third = [
        put(slab.at[x, core], slab.at[x, core], send_x.at[i - 1], recv_x.at[i - 1], peers[i - 1])
        for i in range(1, NX)
    ]
    fourth = [put(slab.at[x, core], slab.at[x, core], send_c.at[0], recv_c.at[0], other)]
    for i in range(1, NX):
        third[i - 1].wait()
        xx = (x + NX - i) % NX
        fourth.append(put(slab.at[xx, core], slab.at[xx, core], send_c.at[i], recv_c.at[i], other))
    for copy in fourth:
        copy.wait()
    slab_ref[...] = slab[...]
    for copy in owns:
        copy.wait()
    mine_ref[...] = own_ref[x] + got_own[0] + got_own[1] + got_own[2]


def dot(a, b, dims=((1,), (0,))):
    return lax.dot_general(a, b, (dims, ((), ())), precision=HIGH, preferred_element_type=F32)


def inverse_factor(a):
    n = 128
    sub = lax.broadcasted_iota(jnp.int32, (8, 1), 0)
    lane = lax.broadcasted_iota(jnp.int32, (8, n), 1)
    row8 = lax.broadcasted_iota(jnp.int32, (8, n), 0)
    left = [a[8 * k : 8 * k + 8, :] for k in range(n // 8)]
    right = [jnp.where(lane == row8 + 8 * k, 1.0, 0.0).astype(F32) for k in range(n // 8)]
    for i in range(n):
        k, s = divmod(i, 8)
        top_l = left[k][s : s + 1, :]
        top_r = right[k][s : s + 1, :]
        inv = 1.0 / top_l[:, i : i + 1]
        for m in range(k, n // 8):
            ratio = left[m][:, i : i + 1] * inv
            if m == k:
                ratio = jnp.where(sub > s, ratio, 0.0)
            left[m] = left[m] - ratio * top_l
            right[m] = right[m] - ratio * top_r
    out = []
    for k in range(n // 8):
        diag = jnp.sum(jnp.where(lane == row8 + 8 * k, left[k], 0.0), axis=1, keepdims=True)
        out.append(right[k] * lax.rsqrt(diag))
    return jnp.concatenate(out, axis=0)


def finish_kernel(mine_ref, slab_ref, ridge_ref, panel_ref, schur_ref, full, winv):
    x, y, z, core = place()
    e, p = lax.axis_index("epoch"), lax.axis_index("prow")
    width = slab_ref.shape[4] - 128
    cols = width - B
    for xx in range(NX):
        for zz in range(8):
            for cc in range(2):
                g = ((zz % 4) * 2 + cc) * 2 + zz // 4
                r0 = 16 * g + 4 * xx
                full[r0 : r0 + 4, :] = slab_ref[xx, cc, zz, :, :width]
    lane = lax.broadcasted_iota(jnp.int32, (64, B), 1)
    sub = lax.broadcasted_iota(jnp.int32, (64, B), 0)
    for k in range(4):
        row = jnp.broadcast_to(slab_ref[k, 0, 0, 0:1, width:], (128, 128))
        ridge = jnp.transpose(row)[:64, 0:1]
        add = jnp.where(lane == sub + 64 * k, ridge, 0.0)
        full[64 * k : 64 * k + 64, 0:B] += add
        full[64 * k : 64 * k + 64, B : 2 * B] += jnp.where(y == 0, add, 0.0)
    w1 = inverse_factor(full[0:128, 0:128])
    low = full[128:256, 0:128]
    s = dot(low, w1, ((1,), (1,)))
    rest = full[128:256, 128:256] - dot(s, s, ((1,), (1,)))
    sw = dot(s, w1)
    w2 = inverse_factor(rest)
    winv[0:128, 0:128] = w1
    winv[0:128, 128:256] = jnp.zeros((128, 128), F32)
    winv[128:256, 0:128] = -dot(w2, sw)
    winv[128:256, 128:256] = w2
    first = (e * 8 + p) * 64
    own_ridge = jnp.transpose(jnp.broadcast_to(ridge_ref[...], (128, 128)))[:64, 0:1]
    lead = mine_ref[:, 0:B] + jnp.where(lane == sub + first, own_ridge, 0.0)
    panel = dot(lead, winv[...], ((1,), (1,)))
    panel_ref[...] = panel
    for j0 in range(0, cols, 256):
        right = dot(winv[...], full[:, B + j0 : B + j0 + 256])
        here = mine_ref[:, B + j0 : B + j0 + 256]
        here = here + jnp.where(lane + (y * cols + j0) == sub + first, own_ridge, 0.0)
        schur_ref[:, j0 : j0 + 256] = here - dot(panel, right)


def on_device(steps, harmonic, col_scale, taps, ridge):
    params = harmonic.shape[0]
    cols = params // 4
    width = cols + B
    steps3 = steps.reshape(2, 16, 128)
    phase = pl.pallas_call(
        phase_kernel,
        out_shape=jax.ShapeDtypeStruct((256, 128), F32),
        in_specs=[VMEM],
        out_specs=VMEM,
        scratch_shapes=[
            pltpu.VMEM((8, 2, 16, 128), jnp.int32),
            pltpu.SemaphoreType.DMA((8,)),
            pltpu.SemaphoreType.DMA((8,)),
        ],
        compiler_params=pltpu.CompilerParams(collective_id=0, has_side_effects=True),
        name="phases",
    )(steps3)
    here = 4096
    n_rows = 272
    lead, own = pl.pallas_call(
        tile_kernel,
        out_shape=(
            jax.ShapeDtypeStruct((NX, 4, width), F32),
            jax.ShapeDtypeStruct((NX, 64, width), F32),
        ),
        in_specs=[VMEM] * 4,
        out_specs=(VMEM, VMEM),
        scratch_shapes=[
            pltpu.VMEM((3, width // 128, 1, 128), F32),
            pltpu.VMEM((3, n_rows, 128), F32),
            pltpu.VMEM((512, 256), BF16),
            pltpu.VMEM((128, 128), F32),
            pltpu.VMEM((here + BLK, width), BF16),
            pltpu.VMEM((n_rows, here + BLK), BF16),
            pltpu.VMEM((here, width), BF16),
            pltpu.VMEM((n_rows, here), BF16),
        ],
        compiler_params=pltpu.CompilerParams(vmem_limit_bytes=60 * 1024 * 1024),
        name="tile",
    )(phase, harmonic.reshape(-1, 128), col_scale.reshape(-1, 128), taps.reshape(2, 128))
    ridge_row = jnp.pad(ridge.reshape(1, -1), ((0, 0), (0, 128 - ridge.shape[0])))
    dma = pltpu.SemaphoreType.DMA
    mine, slab = pl.pallas_call(
        exchange_kernel,
        out_shape=(
            jax.ShapeDtypeStruct((64, width), F32),
            jax.ShapeDtypeStruct((NX, 2, 8, 4, width + 128), F32),
        ),
        in_specs=[VMEM] * 3,
        out_specs=(VMEM, VMEM),
        scratch_shapes=[
            pltpu.VMEM((NX, 2, 8, 4, width + 128), F32),
            pltpu.VMEM((NX - 1, 4, width), F32),
            pltpu.VMEM((NX - 1, 64, width), F32),
            dma((3,)), dma((3,)), dma((3,)), dma((3,)),
            dma((7,)), dma((7,)), dma((3,)), dma((3,)), dma((4,)), dma((4,)),
        ],
        compiler_params=pltpu.CompilerParams(collective_id=1, has_side_effects=True),
        name="exchange",
    )(lead, own, ridge_row)
    return pl.pallas_call(
        finish_kernel,
        out_shape=(
            jax.ShapeDtypeStruct((64, B), F32),
            jax.ShapeDtypeStruct((64, cols), F32),
        ),
        in_specs=[VMEM] * 3,
        out_specs=(VMEM, VMEM),
        scratch_shapes=[pltpu.VMEM((B, width), F32), pltpu.VMEM((B, B), F32)],
        name="finish",
    )(mine, slab, ridge_row)


def solution(mesh):
    row = P(("epoch", "prow"))
    return jax.shard_map(
        on_device,
        mesh=mesh,
        in_specs=(P(None, "epoch"), P(), P(), P(), row),
        out_specs=(P(("epoch", "prow"), None), P(("epoch", "prow"), "pcol")),
        check_vma=False,
    )
```

```python
import functools

import jax
import jax.numpy as jnp
from jax import lax
from jax.experimental import pallas as pl
from jax.experimental.pallas import tpu as pltpu
from jax.sharding import PartitionSpec as P

F32 = jnp.float32
BF16 = jnp.bfloat16
MESH = pl.DeviceIdType.MESH
HIGH = lax.Precision.HIGHEST
B = 256
BLK = 256
PERIOD = 4096
NX = 4
WAVE = (8.88573567404434, -58.45953046181323, 115.03267724691959, -100.39492606524867)
ROUND = 12582912.0
VMEM = pl.BlockSpec(memory_space=pltpu.VMEM)


def place():
    e, p, y = (lax.axis_index(a) for a in ("epoch", "prow", "pcol"))
    core, z_lo = e % 2, e // 2
    x, z_hi = p % NX, p // NX
    return x, y, z_hi * 4 + z_lo, core


def device(x, z, core):
    return {"epoch": (z % 4) * 2 + core, "prow": (z // 4) * NX + x}


def phase_kernel(steps_ref, ridge_ref, phase_ref, ridge0_ref, every, every_ridge, send, recv, send_r, recv_r):
    e = lax.axis_index("epoch")
    n = 8
    barrier = pltpu.get_barrier_semaphore()
    for i in range(1, n):
        pl.semaphore_signal(barrier, inc=1, device_id={"epoch": (e + i) % n}, device_id_type=MESH)
    pl.semaphore_wait(barrier, n - 1)
    copies = []
    for i in range(1, n):
        copy = pltpu.make_async_remote_copy(
            src_ref=steps_ref,
            dst_ref=every.at[e],
            send_sem=send.at[i],
            recv_sem=recv.at[i],
            device_id={"epoch": (e + i) % n},
            device_id_type=MESH,
        )
        copy.start()
        copies.append(copy)
        copy = pltpu.make_async_remote_copy(
            src_ref=ridge_ref,
            dst_ref=every_ridge.at[e],
            send_sem=send_r.at[i],
            recv_sem=recv_r.at[i],
            device_id={"epoch": (e + i) % n},
            device_id_type=MESH,
        )
        copy.start()
        copies.append(copy)
    every[e] = steps_ref[...]
    every_ridge[e] = ridge_ref[...]
    tiles = steps_ref.shape[1]
    rows = n * 2 * tiles
    upper = (
        lax.broadcasted_iota(jnp.int32, (128, 128), 0)
        <= lax.broadcasted_iota(jnp.int32, (128, 128), 1)
    ).astype(BF16)
    r = lax.broadcasted_iota(jnp.int32, (rows, rows), 0)
    s = lax.broadcasted_iota(jnp.int32, (rows, rows), 1)
    same = (r // tiles) % 2 == (s // tiles) % 2
    key_r = (r // (2 * tiles)) * tiles + r % tiles
    key_s = (s // (2 * tiles)) * tiles + s % tiles
    before = jnp.where(same & (key_s < key_r), 1.0, 0.0).astype(F32)
    for copy in copies:
        copy.wait()
    x = every[...].reshape(rows, 128).astype(F32).astype(BF16)
    inside = jnp.dot(x, upper, preferred_element_type=F32)
    totals = jnp.broadcast_to(inside[:, 127:128], (rows, 128))
    earlier = jnp.dot(before, totals, precision=HIGH, preferred_element_type=F32)
    ridge0_ref[...] = every_ridge[0]
    whole = (inside + earlier).astype(jnp.int32)
    phase_ref[...] = (whole & (PERIOD - 1)).astype(F32) * (1.0 / PERIOD)


def wave(turn, scale):
    turn = turn - 0.125
    whole = (turn + ROUND) - ROUND
    z = 0.25 - jnp.abs(turn - whole)
    s = z * z
    poly = WAVE[3]
    for c in (WAVE[2], WAVE[1], WAVE[0]):
        poly = poly * s + c
    return poly * (z * scale)


def tile_kernel(
    phase_ref, harm_ref, scale_ref, taps_ref,
    la_ref, lb_ref, oa_ref, ob_ref, oc_ref,
    colf, rowf, lowt, lowr, dcol, drow, fcol, frow, held,
):
    x, y, z, core = place()
    group = ((z % 4) * 2 + core) * 2 + z // 4
    blocks = (phase_ref.shape[0] // 4) // NX
    n_rows = rowf.shape[1]
    n_lead = n_rows - 256
    n_tiles = colf.shape[1]
    cols_here = n_tiles - 2

    def features(k):
        h = harm_ref[pl.ds(k, 1), :]
        return (
            lax.shift_right_logical(h, 6).astype(F32),
            (h & 63).astype(F32),
            scale_ref[pl.ds(k, 1), :],
        )

    def down(row):
        return jnp.transpose(jnp.broadcast_to(row, (128, 128)))

    for jt in range(n_tiles):
        k = jt if jt < 2 else y * cols_here + (jt - 2)
        for f, v in enumerate(features(k)):
            colf[f, jt] = v
    for half in range(2):
        for f, v in enumerate(features(group * 2 + half)):
            rowf[f, half * 128 : half * 128 + 128, :] = down(v)
    per = 128 // n_lead
    for f, v in enumerate(features(group // per)):
        lowr[...] = down(v)
        rowf[f, 256:, :] = lowr[pl.ds(pl.multiple_of((group % per) * n_lead, n_lead), n_lead), :]

    base = jnp.concatenate([taps_ref[0:1, :], taps_ref[1:2, :], jnp.zeros((1, 256), F32)], axis=1)
    full = pltpu.roll(
        jnp.broadcast_to(base, (512, 512)), 256, 1, stride=1, stride_axis=0
    )[:, :256]
    low_up = jnp.transpose(full).astype(BF16)
    lowt[...] = full.astype(BF16)

    @pl.loop(0, blocks + 1)
    def _(b):
        at = x * blocks + b - 1
        present = at >= 0
        at = jnp.maximum(at, 0)
        row0 = (at // 8) * 32 + (at % 8) * 2
        for half in range(2):
            q0 = phase_ref[pl.ds(row0 + half, 1), :]
            q1 = phase_ref[pl.ds(row0 + 16 + half, 1), :]
            q0d, q1d = down(q0), down(q1)
            where_t = pl.multiple_of(b * BLK + half * 128, 128)
            for jt in range(n_tiles):
                d = wave(q0d * colf[0, jt] + q1d * colf[1, jt], colf[2, jt])
                d = jnp.where(present, d, 0.0)
                dcol[pl.ds(where_t, 128), jt * 128 : jt * 128 + 128] = d.astype(BF16)
            for r0 in range(0, n_rows, 128):
                r1 = min(r0 + 128, n_rows)
                d = wave(q0 * rowf[0, r0:r1, :] + q1 * rowf[1, r0:r1, :], rowf[2, r0:r1, :])
                d = jnp.where(present, d, 0.0)
                drow[r0:r1, pl.ds(where_t, 128)] = d.astype(BF16)

    lowr2 = low_up

    @pl.loop(0, blocks)
    def _(b):
        t0 = pl.multiple_of(b * BLK, BLK)
        for j0 in range(0, n_tiles * 128, 256):
            f = jnp.dot(
                lowr2, dcol[pl.ds(t0, 2 * BLK), j0 : j0 + 256], preferred_element_type=F32
            )
            fcol[pl.ds(t0, BLK), j0 : j0 + 256] = f.astype(BF16)
        f = jnp.dot(drow[:, pl.ds(t0, 2 * BLK)], lowt[...], preferred_element_type=F32)
        frow[:, pl.ds(t0, BLK)] = f.astype(BF16)

    total = 1.0 / (blocks * BLK * NX)
    for j0 in range(0, n_tiles * 128, 256):
        g = jnp.dot(frow[...], fcol[:, j0 : j0 + 256], preferred_element_type=F32) * total
        if j0 == 0:
            oa_ref[...] = g[:256].reshape(NX, 64, 256)
            la_ref[...] = g[256:]
        else:
            held[...] = g[:256]
            ob_ref[:, :, j0 - 256 : j0] = g[:256].astype(BF16).reshape(NX, 64, 256)
            oc_ref[:, j0 - 256 : j0] = held[pl.ds(pl.multiple_of(x * 64, 64), 64), :]
            lb_ref[:, j0 - 256 : j0] = g[256:]


def dot(a, b, dims=((1,), (0,))):
    return lax.dot_general(a, b, (dims, ((), ())), precision=HIGH, preferred_element_type=F32)


def split3(v):
    hi = v.astype(BF16)
    v = v - hi.astype(F32)
    mid = v.astype(BF16)
    low = (v - mid.astype(F32)).astype(BF16)
    return hi, mid, low


NB = 32


def block_inverse(a):
    sub = lax.broadcasted_iota(jnp.int32, (NB, 1), 0)
    lane = lax.broadcasted_iota(jnp.int32, (NB, NB), 1)
    row = lax.broadcasted_iota(jnp.int32, (NB, NB), 0)
    eye = jnp.where(lane == row, 1.0, 0.0).astype(F32)
    m = jnp.concatenate([a, eye, jnp.zeros((NB, 128 - 2 * NB), F32)], axis=1)
    for i in range(NB):
        top = m[i : i + 1, :]
        scaled = top * (1.0 / top[:, i : i + 1])
        m = m - jnp.where(sub > i, m[:, i : i + 1], 0.0) * scaled
    diag = jnp.sum(m[:, :NB] * eye, axis=1, keepdims=True)
    return m[:, NB : 2 * NB] * lax.rsqrt(diag)


def final_kernel(
    la_ref, lb_ref, oa_ref, ob_ref, oc_ref, ridge0_ref, ridge_ref, panel_ref, schur_ref,
    slab_a, slab_b, got_la, got_lb, got_oa, got_ob, ridge4, ridge_far, mat,
    s_la, r_la, s_lb, r_lb, s_oa, r_oa, s_ob, r_ob, s_r, r_r, s_f, r_f,
    s_za, r_za, s_zb, r_zb, s_ca, r_ca, s_cb, r_cb,
):
    x, y, z, core = place()
    e, p = lax.axis_index("epoch"), lax.axis_index("prow")
    nz = 8

    def group(zz, cc):
        return ((zz % 4) * 2 + cc) * 2 + zz // 4

    g = group(z, core)
    barrier = pltpu.get_barrier_semaphore()
    peers = [device((x + i) % NX, z, core) for i in range(1, NX)]
    tall = [device(x, (z + i) % nz, core) for i in range(1, nz)]
    other = device(x, z, 1 - core)
    for peer in peers + tall + [other]:
        pl.semaphore_signal(barrier, inc=1, device_id=peer, device_id_type=MESH)
    pl.semaphore_wait(barrier, len(peers) + len(tall) + 1)

    def put(src, dst, send, recv, peer):
        copy = pltpu.make_async_remote_copy(
            src_ref=src, dst_ref=dst, send_sem=send, recv_sem=recv,
            device_id=peer, device_id_type=MESH,
        )
        copy.start()
        return copy

    def to_x(src, got, send, recv):
        return [put(src(i), got.at[i - 1], send.at[i - 1], recv.at[i - 1], peers[i - 1]) for i in range(1, NX)]

    def to_z(slab, send, recv):
        return [put(slab.at[g], slab.at[g], send.at[i - 1], recv.at[i - 1], tall[i - 1]) for i in range(1, nz)]

    def to_core(slab, send, recv, i):
        k = group((z + nz - i) % nz, core)
        return put(slab.at[k], slab.at[k], send.at[i], recv.at[i], other)

    lead_a = to_x(lambda i: la_ref, got_la, s_la, r_la)
    ridges = [
        put(ridge0_ref, ridge4.at[x], s_r.at[i - 1], r_r.at[i - 1], peers[i - 1])
        for i in range(1, NX)
    ]
    lead_b = to_x(lambda i: lb_ref, got_lb, s_lb, r_lb)
    ridge4[x] = ridge0_ref[...]
    for copy in lead_a:
        copy.wait()
    slab_a[g] = la_ref[...] + got_la[0] + got_la[1] + got_la[2]
    z_a = to_z(slab_a, s_za, r_za)
    c_a = [to_core(slab_a, s_ca, r_ca, 0)]
    for copy in ridges:
        copy.wait()
    far = put(ridge4, ridge_far, s_f, r_f, device(x, (z + 4) % nz, core))
    for copy in lead_b:
        copy.wait()
    slab_b[g] = lb_ref[...] + got_lb[0] + got_lb[1] + got_lb[2]
    z_b = to_z(slab_b, s_zb, r_zb)
    c_b = [to_core(slab_b, s_cb, r_cb, 0)]
    own_a = to_x(lambda i: oa_ref.at[(x + i) % NX], got_oa, s_oa, r_oa)
    own_b = to_x(lambda i: ob_ref.at[(x + i) % NX], got_ob, s_ob, r_ob)
    for i in range(1, nz):
        z_a[i - 1].wait()
        c_a.append(to_core(slab_a, s_ca, r_ca, i))
    far.wait()
    for copy in c_a:
        copy.wait()

    lane = lax.broadcasted_iota(jnp.int32, (64, B), 1)
    sub = lax.broadcasted_iota(jnp.int32, (64, B), 0)

    def column(row):
        return jnp.transpose(jnp.broadcast_to(row, (128, 128)))[:64, 0:1]

    lead_ridge = [column(jnp.where(z < 4, ridge4[k], ridge_far[k])) for k in range(4)]
    for k in range(4):
        rows = slab_a[4 * k : 4 * k + 4].reshape(64, B)
        mat[64 * k : 64 * k + 64, 0:B] = rows + jnp.where(lane == sub + 64 * k, lead_ridge[k], 0.0)
        mat[64 * k : 64 * k + 64, B:] = jnp.where(lane == sub + 64 * k, 1.0, 0.0).astype(F32)

    nxt = mat[0:NB, 0:NB]
    for j in range(B // NB):
        if j == B // NB // 2:
            for i in range(1, nz):
                z_b[i - 1].wait()
                c_b.append(to_core(slab_b, s_cb, r_cb, i))
        r0, r1 = NB * j, NB * j + NB
        w = block_inverse(nxt)
        rj = dot(w, mat[r0:r1, :])
        mat[r0:r1, :] = rj
        if r1 < B:
            hi, mid, low = split3(rj)
            left = jnp.concatenate([hi, hi, mid, hi, low, mid], axis=0)
            right = jnp.concatenate([hi, mid, hi, low, hi, mid], axis=0)
            dims = (((0,), (0,)), ((), ()))
            c0 = (r1 // 128) * 128
            at = lax.dot_general(left[:, c0:B], right[:, c0:B], dims, preferred_element_type=F32)
            nxt = mat[r1 : r1 + NB, r1 : r1 + NB] - at[r1 - c0 : r1 - c0 + NB, r1 - c0 : r1 - c0 + NB]
            mat[r1:B, c0:B] -= at[r1 - c0 :, :]
            w1 = B + ((r1 + 127) // 128) * 128
            aw = lax.dot_general(left[:, c0:B], right[:, B:w1], dims, preferred_element_type=F32)
            mat[r1:B, B:w1] -= aw[r1 - c0 :, :]

    for copy in own_a:
        copy.wait()
    first = (e * 8 + p) * 64
    own_ridge = column(ridge_ref[...])
    winv = mat[:, B:]
    lead = oa_ref[x] + got_oa[0] + got_oa[1] + got_oa[2]
    lead = lead + jnp.where(lane == sub + first, own_ridge, 0.0)
    panel = dot(lead, winv, ((1,), (1,)))
    panel_ref[...] = panel
    for copy in c_b:
        copy.wait()
    for copy in own_b:
        copy.wait()
    cols = lb_ref.shape[1]
    for j0 in range(0, cols, B):
        here = slab_b[:, :, j0 : j0 + B].reshape(B, B)
        if j0 == 0:
            add = [jnp.where((lane == sub + 64 * k) & (y == 0), lead_ridge[k], 0.0) for k in range(4)]
            here = here + jnp.concatenate(add, axis=0)
        right = dot(winv, here)
        at = slice(j0, j0 + B)
        tile = oc_ref[:, at] + got_ob[0, :, at].astype(F32)
        tile = tile + got_ob[1, :, at].astype(F32) + got_ob[2, :, at].astype(F32)
        tile = tile + jnp.where(lane + (y * cols + j0) == sub + first, own_ridge, 0.0)
        schur_ref[:, at] = tile - dot(panel, right)


def on_device(steps, harmonic, col_scale, taps, ridge):
    params = harmonic.shape[0]
    cols = params // 4
    width = cols + B
    dma = pltpu.SemaphoreType.DMA
    steps3 = steps.reshape(2, 16, 128)
    ridge_row = jnp.pad(ridge.reshape(1, -1), ((0, 0), (0, 128 - ridge.shape[0])))
    phase, ridge0 = pl.pallas_call(
        phase_kernel,
        out_shape=(
            jax.ShapeDtypeStruct((256, 128), F32),
            jax.ShapeDtypeStruct((1, 128), F32),
        ),
        in_specs=[VMEM] * 2,
        out_specs=(VMEM, VMEM),
        scratch_shapes=[
            pltpu.VMEM((8, 2, 16, 128), jnp.int32),
            pltpu.VMEM((8, 1, 128), F32),
            dma((8,)), dma((8,)), dma((8,)), dma((8,)),
        ],
        compiler_params=pltpu.CompilerParams(collective_id=0, has_side_effects=True),
        name="phases",
    )(steps3, ridge_row)
    here = 4096
    n_rows = 272
    parts = pl.pallas_call(
        tile_kernel,
        out_shape=(
            jax.ShapeDtypeStruct((16, B), F32),
            jax.ShapeDtypeStruct((16, cols), F32),
            jax.ShapeDtypeStruct((NX, 64, B), F32),
            jax.ShapeDtypeStruct((NX, 64, cols), BF16),
            jax.ShapeDtypeStruct((64, cols), F32),
        ),
        in_specs=[VMEM] * 4,
        out_specs=(VMEM,) * 5,
        scratch_shapes=[
            pltpu.VMEM((3, width // 128, 1, 128), F32),
            pltpu.VMEM((3, n_rows, 128), F32),
            pltpu.VMEM((512, 256), BF16),
            pltpu.VMEM((128, 128), F32),
            pltpu.VMEM((here + BLK, width), BF16),
            pltpu.VMEM((n_rows, here + BLK), BF16),
            pltpu.VMEM((here, width), BF16),
            pltpu.VMEM((n_rows, here), BF16),
            pltpu.VMEM((256, 256), F32),
        ],
        compiler_params=pltpu.CompilerParams(vmem_limit_bytes=60 * 1024 * 1024),
        name="tile",
    )(phase, harmonic.reshape(-1, 128), col_scale.reshape(-1, 128), taps.reshape(2, 128))
    return pl.pallas_call(
        final_kernel,
        out_shape=(
            jax.ShapeDtypeStruct((64, B), F32),
            jax.ShapeDtypeStruct((64, cols), F32),
        ),
        in_specs=[VMEM] * 7,
        out_specs=(VMEM, VMEM),
        scratch_shapes=[
            pltpu.VMEM((16, 16, B), F32),
            pltpu.VMEM((16, 16, cols), F32),
            pltpu.VMEM((NX - 1, 16, B), F32),
            pltpu.VMEM((NX - 1, 16, cols), F32),
            pltpu.VMEM((NX - 1, 64, B), F32),
            pltpu.VMEM((NX - 1, 64, cols), BF16),
            pltpu.VMEM((NX, 1, 128), F32),
            pltpu.VMEM((NX, 1, 128), F32),
            pltpu.VMEM((B, 2 * B), F32),
            *([dma((3,))] * 10), dma, dma, *([dma((7,))] * 4), *([dma((8,))] * 4),
        ],
        compiler_params=pltpu.CompilerParams(collective_id=1, has_side_effects=True),
        name="final",
    )(*parts, ridge0, ridge_row)


def solution(mesh):
    row = P(("epoch", "prow"))
    return jax.shard_map(
        on_device,
        mesh=mesh,
        in_specs=(P(None, "epoch"), P(), P(), P(), row),
        out_specs=(P(("epoch", "prow"), None), P(("epoch", "prow"), "pcol")),
        check_vma=False,
    )
```

```python
import functools

import jax
import jax.numpy as jnp
from jax import lax
from jax.experimental import pallas as pl
from jax.experimental.pallas import tpu as pltpu
from jax.sharding import PartitionSpec as P

F32 = jnp.float32
BF16 = jnp.bfloat16
MESH = pl.DeviceIdType.MESH
HIGH = lax.Precision.HIGHEST
B = 256
BLK = 256
PERIOD = 4096
NX = 4
WAVE = (8.88573567404434, -58.45953046181323, 115.03267724691959, -100.39492606524867)
ROUND = 12582912.0
VMEM = pl.BlockSpec(memory_space=pltpu.VMEM)


def place():
    e, p, y = (lax.axis_index(a) for a in ("epoch", "prow", "pcol"))
    core, z_lo = e % 2, e // 2
    x, z_hi = p % NX, p // NX
    return x, y, z_hi * 4 + z_lo, core


def device(x, z, core):
    return {"epoch": (z % 4) * 2 + core, "prow": (z // 4) * NX + x}


def phase_kernel(steps_ref, ridge_ref, phase_ref, ridge0_ref, every, every_ridge, send, recv, send_r, recv_r):
    e = lax.axis_index("epoch")
    n = 8
    barrier = pltpu.get_barrier_semaphore()
    for i in range(1, n):
        pl.semaphore_signal(barrier, inc=1, device_id={"epoch": (e + i) % n}, device_id_type=MESH)
    pl.semaphore_wait(barrier, n - 1)
    copies = []
    for i in range(1, n):
        copy = pltpu.make_async_remote_copy(
            src_ref=steps_ref,
            dst_ref=every.at[e],
            send_sem=send.at[i],
            recv_sem=recv.at[i],
            device_id={"epoch": (e + i) % n},
            device_id_type=MESH,
        )
        copy.start()
        copies.append(copy)
        copy = pltpu.make_async_remote_copy(
            src_ref=ridge_ref,
            dst_ref=every_ridge.at[e],
            send_sem=send_r.at[i],
            recv_sem=recv_r.at[i],
            device_id={"epoch": (e + i) % n},
            device_id_type=MESH,
        )
        copy.start()
        copies.append(copy)
    every[e] = steps_ref[...]
    every_ridge[e] = ridge_ref[...]
    tiles = steps_ref.shape[1]
    rows = n * 2 * tiles
    upper = (
        lax.broadcasted_iota(jnp.int32, (128, 128), 0)
        <= lax.broadcasted_iota(jnp.int32, (128, 128), 1)
    ).astype(BF16)
    r = lax.broadcasted_iota(jnp.int32, (rows, rows), 0)
    s = lax.broadcasted_iota(jnp.int32, (rows, rows), 1)
    same = (r // tiles) % 2 == (s // tiles) % 2
    key_r = (r // (2 * tiles)) * tiles + r % tiles
    key_s = (s // (2 * tiles)) * tiles + s % tiles
    before = jnp.where(same & (key_s < key_r), 1.0, 0.0).astype(F32)
    for copy in copies:
        copy.wait()
    x = every[...].reshape(rows, 128).astype(F32).astype(BF16)
    inside = jnp.dot(x, upper, preferred_element_type=F32)
    totals = jnp.broadcast_to(inside[:, 127:128], (rows, 128))
    earlier = jnp.dot(before, totals, precision=HIGH, preferred_element_type=F32)
    ridge0_ref[...] = every_ridge[0]
    whole = (inside + earlier).astype(jnp.int32)
    phase_ref[...] = (whole & (PERIOD - 1)).astype(F32) * (1.0 / PERIOD)


def wave(turn, scale):
    whole = (turn + ROUND) - ROUND
    z = 0.25 - jnp.abs(turn - whole)
    s = z * z
    poly = WAVE[3]
    for c in (WAVE[2], WAVE[1], WAVE[0]):
        poly = poly * s + c
    return poly * (z * scale)


def halves(v):
    hi = jnp.floor(v * 64.0) * (1.0 / 64.0)
    return hi, v - hi


def tile_kernel(
    phase_ref, harm_ref, scale_ref, taps_ref,
    la_ref, lb_ref, oa_ref, ob_ref, oc_ref,
    colf, cols_s, rowf, rows_s, lowt, lowr, d0, d1, d2, e0, e1, e2, fcol, frow, held,
):
    x, y, z, core = place()
    group = ((z % 4) * 2 + core) * 2 + z // 4
    blocks = (phase_ref.shape[0] // 4) // NX
    n_rows = rows_s.shape[0]
    n_lead = n_rows - 256
    n_tiles = colf.shape[1] // 128
    cols_here = n_tiles - 2
    dcol, drow = (d0, d1, d2), (e0, e1, e2)

    def features(k):
        h = harm_ref[pl.ds(k, 1), :]
        order = lax.shift_right_logical(h, 6).astype(F32)
        degree = (h & 63).astype(F32)
        shift = jnp.full((1, 128), -0.125, F32)
        rows = jnp.concatenate(
            [order, order, degree, degree, shift, jnp.zeros((11, 128), F32)], axis=0
        )
        return rows, scale_ref[pl.ds(k, 1), :]

    def down(row):
        return jnp.transpose(jnp.broadcast_to(row, (128, 128)))

    for jt in range(n_tiles):
        k = jt if jt < 2 else y * cols_here + (jt - 2)
        rows, scale = features(k)
        colf[:, jt * 128 : jt * 128 + 128] = rows.astype(BF16)
        cols_s[:, jt * 128 : jt * 128 + 128] = scale
    for half in range(2):
        rows, scale = features(group * 2 + half)
        rowf[half * 128 : half * 128 + 128, :] = jnp.transpose(rows).astype(BF16)
        rows_s[half * 128 : half * 128 + 128, :] = down(scale)
    per = 128 // n_lead
    rows, scale = features(group // per)
    piece = pl.ds(pl.multiple_of((group % per) * n_lead, n_lead), n_lead)
    lowr[...] = down(scale)
    rows_s[256:, :] = lowr[piece, :]
    lowr[:, 0:16] = jnp.transpose(rows)
    rowf[256:, :] = lowr[piece, 0:16].astype(BF16)

    base = jnp.concatenate([taps_ref[0:1, :], taps_ref[1:2, :], jnp.zeros((1, 256), F32)], axis=1)
    full = pltpu.roll(
        jnp.broadcast_to(base, (512, 512)), 256, 1, stride=1, stride_axis=0
    )[:, :256]
    lowt[...] = full.astype(BF16)
    low_up = jnp.transpose(full).astype(BF16)

    def phases_of(b):
        at = jnp.maximum(x * blocks + b - 1, 0)
        row0 = (at // 8) * 32 + (at % 8) * 2
        parts = []
        for a in range(2):
            q = jnp.concatenate(
                [phase_ref[pl.ds(row0 + 16 * a + half, 1), :] for half in range(2)], axis=1
            )
            parts += list(halves(q))
        parts += [jnp.ones((1, BLK), F32), jnp.zeros((11, BLK), F32)]
        return jnp.concatenate(parts, axis=0).astype(BF16)

    def design(qf, slot, j0):
        turn = lax.dot_general(
            qf, colf[:, j0 : j0 + 256], (((0,), (0,)), ((), ())), preferred_element_type=F32
        )
        d = wave(turn, cols_s[:, j0 : j0 + 256])
        dcol[slot][:, j0 : j0 + 256] = d.astype(BF16)

    def design_rows(qf, slot):
        turn = jnp.dot(rowf[...], qf, preferred_element_type=F32)
        scale = rows_s[...]
        d = wave(turn, jnp.concatenate([scale, scale], axis=1))
        drow[slot][...] = d.astype(BF16)

    def filter_cols(b, s0, s1, j0):
        f = jnp.dot(low_up[:, :BLK], dcol[s0][:, j0 : j0 + 256], preferred_element_type=F32)
        f = f + jnp.dot(low_up[:, BLK:], dcol[s1][:, j0 : j0 + 256], preferred_element_type=F32)
        fcol[pl.ds(pl.multiple_of(b * BLK, BLK), BLK), j0 : j0 + 256] = f.astype(BF16)

    def filter_rows(b, s0, s1):
        f = jnp.dot(drow[s0][...], lowt[:BLK, :], preferred_element_type=F32)
        f = f + jnp.dot(drow[s1][...], lowt[BLK:, :], preferred_element_type=F32)
        frow[:, pl.ds(pl.multiple_of(b * BLK, BLK), BLK)] = f.astype(BF16)

    wide = range(0, n_tiles * 128, 256)
    for b in range(2):
        qf = phases_of(b)
        for j0 in wide:
            design(qf, b, j0)
        design_rows(qf, b)

    @pl.when(x == 0)
    def _():
        d0[...] = jnp.zeros_like(d0)
        e0[...] = jnp.zeros_like(e0)

    @pl.loop(0, blocks // 3)
    def _(step):
        for s in range(3):
            b = step * 3 + s
            qf = phases_of(b + 2)
            for j0 in wide:
                filter_cols(b, s, (s + 1) % 3, j0)
                design(qf, (s + 2) % 3, j0)
            filter_rows(b, s, (s + 1) % 3)
            design_rows(qf, (s + 2) % 3)

    for b in range(blocks // 3 * 3, blocks):
        for j0 in wide:
            filter_cols(b, b % 3, (b + 1) % 3, j0)
        filter_rows(b, b % 3, (b + 1) % 3)

    total = 1.0 / (blocks * BLK * NX)
    for j0 in wide:
        g = jnp.dot(frow[...], fcol[:, j0 : j0 + 256], preferred_element_type=F32) * total
        if j0 == 0:
            oa_ref[...] = g[:256].reshape(NX, 64, 256)
            la_ref[...] = g[256:]
        else:
            held[...] = g[:256]
            ob_ref[:, :, j0 - 256 : j0] = g[:256].astype(BF16).reshape(NX, 64, 256)
            oc_ref[:, j0 - 256 : j0] = held[pl.ds(pl.multiple_of(x * 64, 64), 64), :]
            lb_ref[:, j0 - 256 : j0] = g[256:]


def dot(a, b, dims=((1,), (0,))):
    return lax.dot_general(a, b, (dims, ((), ())), precision=HIGH, preferred_element_type=F32)


def split3(v):
    hi = v.astype(BF16)
    v = v - hi.astype(F32)
    mid = v.astype(BF16)
    low = (v - mid.astype(F32)).astype(BF16)
    return hi, mid, low


NB = 32


def block_inverse(a):
    sub = lax.broadcasted_iota(jnp.int32, (NB, 1), 0)
    lane = lax.broadcasted_iota(jnp.int32, (NB, NB), 1)
    row = lax.broadcasted_iota(jnp.int32, (NB, NB), 0)
    eye = jnp.where(lane == row, 1.0, 0.0).astype(F32)
    m = jnp.concatenate([a, eye, jnp.zeros((NB, 128 - 2 * NB), F32)], axis=1)
    for i in range(NB):
        top = m[i : i + 1, :]
        scaled = top * (1.0 / top[:, i : i + 1])
        m = m - jnp.where(sub > i, m[:, i : i + 1], 0.0) * scaled
    diag = jnp.sum(m[:, :NB] * eye, axis=1, keepdims=True)
    return m[:, NB : 2 * NB] * lax.rsqrt(diag)


def final_kernel(
    la_ref, lb_ref, oa_ref, ob_ref, oc_ref, ridge0_ref, ridge_ref, panel_ref, schur_ref,
    slab_a, slab_b, got_la, got_lb, got_oa, got_ob, ridge4, ridge_far, mat,
    s_la, r_la, s_lb, r_lb, s_oa, r_oa, s_ob, r_ob, s_r, r_r, s_f, r_f,
    s_za, r_za, s_zb, r_zb, s_ca, r_ca, s_cb, r_cb,
):
    x, y, z, core = place()
    e, p = lax.axis_index("epoch"), lax.axis_index("prow")
    nz = 8

    def group(zz, cc):
        return ((zz % 4) * 2 + cc) * 2 + zz // 4

    g = group(z, core)
    barrier = pltpu.get_barrier_semaphore()
    peers = [device((x + i) % NX, z, core) for i in range(1, NX)]
    tall = [device(x, (z + i) % nz, core) for i in range(1, nz)]
    other = device(x, z, 1 - core)
    for peer in peers + tall + [other]:
        pl.semaphore_signal(barrier, inc=1, device_id=peer, device_id_type=MESH)
    pl.semaphore_wait(barrier, len(peers) + len(tall) + 1)

    def put(src, dst, send, recv, peer):
        copy = pltpu.make_async_remote_copy(
            src_ref=src, dst_ref=dst, send_sem=send, recv_sem=recv,
            device_id=peer, device_id_type=MESH,
        )
        copy.start()
        return copy

    def to_x(src, got, send, recv):
        return [put(src(i), got.at[i - 1], send.at[i - 1], recv.at[i - 1], peers[i - 1]) for i in range(1, NX)]

    def to_z(slab, send, recv):
        return [put(slab.at[g], slab.at[g], send.at[i - 1], recv.at[i - 1], tall[i - 1]) for i in range(1, nz)]

    def to_core(slab, send, recv, i):
        k = group((z + nz - i) % nz, core)
        return put(slab.at[k], slab.at[k], send.at[i], recv.at[i], other)

    lead_a = to_x(lambda i: la_ref, got_la, s_la, r_la)
    ridges = [
        put(ridge0_ref, ridge4.at[x], s_r.at[i - 1], r_r.at[i - 1], peers[i - 1])
        for i in range(1, NX)
    ]
    lead_b = to_x(lambda i: lb_ref, got_lb, s_lb, r_lb)
    ridge4[x] = ridge0_ref[...]
    for copy in lead_a:
        copy.wait()
    slab_a[g] = la_ref[...] + got_la[0] + got_la[1] + got_la[2]
    z_a = to_z(slab_a, s_za, r_za)
    c_a = [to_core(slab_a, s_ca, r_ca, 0)]
    for copy in ridges:
        copy.wait()
    far = put(ridge4, ridge_far, s_f, r_f, device(x, (z + 4) % nz, core))
    for copy in lead_b:
        copy.wait()
    slab_b[g] = lb_ref[...] + got_lb[0] + got_lb[1] + got_lb[2]
    z_b = to_z(slab_b, s_zb, r_zb)
    c_b = [to_core(slab_b, s_cb, r_cb, 0)]
    own_a = to_x(lambda i: oa_ref.at[(x + i) % NX], got_oa, s_oa, r_oa)
    own_b = to_x(lambda i: ob_ref.at[(x + i) % NX], got_ob, s_ob, r_ob)
    for i in range(1, nz):
        z_a[i - 1].wait()
        c_a.append(to_core(slab_a, s_ca, r_ca, i))
    far.wait()
    for copy in c_a:
        copy.wait()

    lane = lax.broadcasted_iota(jnp.int32, (64, B), 1)
    sub = lax.broadcasted_iota(jnp.int32, (64, B), 0)

    def column(row):
        return jnp.transpose(jnp.broadcast_to(row, (128, 128)))[:64, 0:1]

    lead_ridge = [column(jnp.where(z < 4, ridge4[k], ridge_far[k])) for k in range(4)]
    for k in range(4):
        rows = slab_a[4 * k : 4 * k + 4].reshape(64, B)
        mat[64 * k : 64 * k + 64, 0:B] = rows + jnp.where(lane == sub + 64 * k, lead_ridge[k], 0.0)
        mat[64 * k : 64 * k + 64, B:] = jnp.where(lane == sub + 64 * k, 1.0, 0.0).astype(F32)

    nxt = mat[0:NB, 0:NB]
    for j in range(B // NB):
        if j == B // NB // 2:
            for i in range(1, nz):
                z_b[i - 1].wait()
                c_b.append(to_core(slab_b, s_cb, r_cb, i))
        r0, r1 = NB * j, NB * j + NB
        w = block_inverse(nxt)
        rj = dot(w, mat[r0:r1, :])
        mat[r0:r1, :] = rj
        if r1 < B:
            hi, mid, low = split3(rj)
            left = jnp.concatenate([hi, hi, mid, hi, low, mid], axis=0)
            right = jnp.concatenate([hi, mid, hi, low, hi, mid], axis=0)
            dims = (((0,), (0,)), ((), ()))
            c0 = (r1 // 128) * 128
            at = lax.dot_general(left[:, c0:B], right[:, c0:B], dims, preferred_element_type=F32)
            nxt = mat[r1 : r1 + NB, r1 : r1 + NB] - at[r1 - c0 : r1 - c0 + NB, r1 - c0 : r1 - c0 + NB]
            mat[r1:B, c0:B] -= at[r1 - c0 :, :]
            w1 = B + ((r1 + 127) // 128) * 128
            aw = lax.dot_general(left[:, c0:B], right[:, B:w1], dims, preferred_element_type=F32)
            mat[r1:B, B:w1] -= aw[r1 - c0 :, :]

    for copy in own_a:
        copy.wait()
    first = (e * 8 + p) * 64
    own_ridge = column(ridge_ref[...])
    winv = mat[:, B:]
    lead = oa_ref[x] + got_oa[0] + got_oa[1] + got_oa[2]
    lead = lead + jnp.where(lane == sub + first, own_ridge, 0.0)
    panel = dot(lead, winv, ((1,), (1,)))
    panel_ref[...] = panel
    for copy in c_b:
        copy.wait()
    for copy in own_b:
        copy.wait()
    cols = lb_ref.shape[1]
    for j0 in range(0, cols, B):
        here = slab_b[:, :, j0 : j0 + B].reshape(B, B)
        if j0 == 0:
            add = [jnp.where((lane == sub + 64 * k) & (y == 0), lead_ridge[k], 0.0) for k in range(4)]
            here = here + jnp.concatenate(add, axis=0)
        right = dot(winv, here)
        at = slice(j0, j0 + B)
        tile = oc_ref[:, at] + got_ob[0, :, at].astype(F32)
        tile = tile + got_ob[1, :, at].astype(F32) + got_ob[2, :, at].astype(F32)
        tile = tile + jnp.where(lane + (y * cols + j0) == sub + first, own_ridge, 0.0)
        schur_ref[:, at] = tile - dot(panel, right)


def on_device(steps, harmonic, col_scale, taps, ridge):
    params = harmonic.shape[0]
    cols = params // 4
    width = cols + B
    dma = pltpu.SemaphoreType.DMA
    steps3 = steps.reshape(2, 16, 128)
    ridge_row = jnp.pad(ridge.reshape(1, -1), ((0, 0), (0, 128 - ridge.shape[0])))
    phase, ridge0 = pl.pallas_call(
        phase_kernel,
        out_shape=(
            jax.ShapeDtypeStruct((256, 128), F32),
            jax.ShapeDtypeStruct((1, 128), F32),
        ),
        in_specs=[VMEM] * 2,
        out_specs=(VMEM, VMEM),
        scratch_shapes=[
            pltpu.VMEM((8, 2, 16, 128), jnp.int32),
            pltpu.VMEM((8, 1, 128), F32),
            dma((8,)), dma((8,)), dma((8,)), dma((8,)),
        ],
        compiler_params=pltpu.CompilerParams(collective_id=0, has_side_effects=True),
        name="phases",
    )(steps3, ridge_row)
    here = 4096
    n_rows = 272
    parts = pl.pallas_call(
        tile_kernel,
        out_shape=(
            jax.ShapeDtypeStruct((16, B), F32),
            jax.ShapeDtypeStruct((16, cols), F32),
            jax.ShapeDtypeStruct((NX, 64, B), F32),
            jax.ShapeDtypeStruct((NX, 64, cols), BF16),
            jax.ShapeDtypeStruct((64, cols), F32),
        ),
        in_specs=[VMEM] * 4,
        out_specs=(VMEM,) * 5,
        scratch_shapes=[
            pltpu.VMEM((16, width), BF16),
            pltpu.VMEM((1, width), F32),
            pltpu.VMEM((n_rows, 16), BF16),
            pltpu.VMEM((n_rows, 128), F32),
            pltpu.VMEM((512, 256), BF16),
            pltpu.VMEM((128, 128), F32),
            *([pltpu.VMEM((BLK, width), BF16)] * 3),
            *([pltpu.VMEM((n_rows, BLK), BF16)] * 3),
            pltpu.VMEM((here, width), BF16),
            pltpu.VMEM((n_rows, here), BF16),
            pltpu.VMEM((256, 256), F32),
        ],
        compiler_params=pltpu.CompilerParams(vmem_limit_bytes=60 * 1024 * 1024),
        name="tile",
    )(phase, harmonic.reshape(-1, 128), col_scale.reshape(-1, 128), taps.reshape(2, 128))
    return pl.pallas_call(
        final_kernel,
        out_shape=(
            jax.ShapeDtypeStruct((64, B), F32),
            jax.ShapeDtypeStruct((64, cols), F32),
        ),
        in_specs=[VMEM] * 7,
        out_specs=(VMEM, VMEM),
        scratch_shapes=[
            pltpu.VMEM((16, 16, B), F32),
            pltpu.VMEM((16, 16, cols), F32),
            pltpu.VMEM((NX - 1, 16, B), F32),
            pltpu.VMEM((NX - 1, 16, cols), F32),
            pltpu.VMEM((NX - 1, 64, B), F32),
            pltpu.VMEM((NX - 1, 64, cols), BF16),
            pltpu.VMEM((NX, 1, 128), F32),
            pltpu.VMEM((NX, 1, 128), F32),
            pltpu.VMEM((B, 2 * B), F32),
            *([dma((3,))] * 10), dma, dma, *([dma((7,))] * 4), *([dma((8,))] * 4),
        ],
        compiler_params=pltpu.CompilerParams(collective_id=1, has_side_effects=True),
        name="final",
    )(*parts, ridge0, ridge_row)


def solution(mesh):
    row = P(("epoch", "prow"))
    return jax.shard_map(
        on_device,
        mesh=mesh,
        in_specs=(P(None, "epoch"), P(), P(), P(), row),
        out_specs=(P(("epoch", "prow"), None), P(("epoch", "prow"), "pcol")),
        check_vma=False,
    )
```

```python
import functools

import jax
import jax.numpy as jnp
from jax import lax
from jax.experimental import pallas as pl
from jax.experimental.pallas import tpu as pltpu
from jax.sharding import PartitionSpec as P

F32 = jnp.float32
BF16 = jnp.bfloat16
MESH = pl.DeviceIdType.MESH
HIGH = lax.Precision.HIGHEST
B = 256
BLK = 256
CHUNK = 64
PERIOD = 4096
NX = 4
WAVE = (8.88573567404434, -58.45953046181323, 115.03267724691959, -100.39492606524867)
ROUND = 12582912.0
VMEM = pl.BlockSpec(memory_space=pltpu.VMEM)


def place():
    e, p, y = (lax.axis_index(a) for a in ("epoch", "prow", "pcol"))
    core, z_lo = e % 2, e // 2
    x, z_hi = p % NX, p // NX
    return x, y, z_hi * 4 + z_lo, core


def device(x, z, core):
    return {"epoch": (z % 4) * 2 + core, "prow": (z // 4) * NX + x}


def phase_kernel(steps_ref, ridge_ref, phase_ref, ridge0_ref, every, every_ridge, send, recv, send_r, recv_r):
    e = lax.axis_index("epoch")
    n = 8
    barrier = pltpu.get_barrier_semaphore()
    for i in range(1, n):
        pl.semaphore_signal(barrier, inc=1, device_id={"epoch": (e + i) % n}, device_id_type=MESH)
    pl.semaphore_wait(barrier, n - 1)
    copies = []
    for i in range(1, n):
        copy = pltpu.make_async_remote_copy(
            src_ref=steps_ref,
            dst_ref=every.at[e],
            send_sem=send.at[i],
            recv_sem=recv.at[i],
            device_id={"epoch": (e + i) % n},
            device_id_type=MESH,
        )
        copy.start()
        copies.append(copy)
        copy = pltpu.make_async_remote_copy(
            src_ref=ridge_ref,
            dst_ref=every_ridge.at[e],
            send_sem=send_r.at[i],
            recv_sem=recv_r.at[i],
            device_id={"epoch": (e + i) % n},
            device_id_type=MESH,
        )
        copy.start()
        copies.append(copy)
    every[e] = steps_ref[...]
    every_ridge[e] = ridge_ref[...]
    tiles = steps_ref.shape[1]
    rows = n * 2 * tiles
    upper = (
        lax.broadcasted_iota(jnp.int32, (128, 128), 0)
        <= lax.broadcasted_iota(jnp.int32, (128, 128), 1)
    ).astype(BF16)
    r = lax.broadcasted_iota(jnp.int32, (rows, rows), 0)
    s = lax.broadcasted_iota(jnp.int32, (rows, rows), 1)
    same = (r // tiles) % 2 == (s // tiles) % 2
    key_r = (r // (2 * tiles)) * tiles + r % tiles
    key_s = (s // (2 * tiles)) * tiles + s % tiles
    before = jnp.where(same & (key_s < key_r), 1.0, 0.0).astype(F32)
    for copy in copies:
        copy.wait()
    x = every[...].reshape(rows, 128).astype(F32).astype(BF16)
    inside = jnp.dot(x, upper, preferred_element_type=F32)
    totals = jnp.broadcast_to(inside[:, 127:128], (rows, 128))
    earlier = jnp.dot(before, totals, precision=HIGH, preferred_element_type=F32)
    ridge0_ref[...] = every_ridge[0]
    whole = (inside + earlier).astype(jnp.int32)
    phase_ref[...] = (whole & (PERIOD - 1)).astype(F32) * (1.0 / PERIOD)


def wave(turn, scale):
    whole = (turn + ROUND) - ROUND
    z = 0.25 - jnp.abs(turn - whole)
    s = z * z
    poly = s + WAVE[2] / WAVE[3]
    for c in (WAVE[1], WAVE[0]):
        poly = poly * s + c / WAVE[3]
    return poly * (z * scale)


def halves(v):
    hi = jnp.floor(v * 64.0) * (1.0 / 64.0)
    return hi, v - hi


def tile_kernel(
    phase_ref, harm_ref, scale_ref, taps_ref,
    la_ref, lb_ref, oa_ref, ob_ref, oc_ref,
    colf, cols_s, rowf, rows_s, lowt, lowr, d0, d1, d2, e0, e1, e2, fcol, frow, held,
):
    x, y, z, core = place()
    group = ((z % 4) * 2 + core) * 2 + z // 4
    blocks = (phase_ref.shape[0] // 4) // NX
    n_rows = rows_s.shape[0]
    n_lead = n_rows - 256
    n_tiles = colf.shape[1] // 128
    cols_here = n_tiles - 2
    dcol, drow = (d0, d1, d2), (e0, e1, e2)

    def features(k):
        h = harm_ref[pl.ds(k, 1), :]
        order = lax.shift_right_logical(h, 6).astype(F32)
        degree = (h & 63).astype(F32)
        shift = jnp.full((1, 128), -0.125, F32)
        rows = jnp.concatenate(
            [order, order, degree, degree, shift, jnp.zeros((11, 128), F32)], axis=0
        )
        return rows, scale_ref[pl.ds(k, 1), :] * WAVE[3]

    def down(row):
        return jnp.transpose(jnp.broadcast_to(row, (128, 128)))

    for jt in range(n_tiles):
        k = jt if jt < 2 else y * cols_here + (jt - 2)
        rows, scale = features(k)
        colf[:, jt * 128 : jt * 128 + 128] = rows.astype(BF16)
        cols_s[:, jt * 128 : jt * 128 + 128] = scale
    for half in range(2):
        rows, scale = features(group * 2 + half)
        rowf[half * 128 : half * 128 + 128, :] = jnp.transpose(rows).astype(BF16)
        rows_s[half * 128 : half * 128 + 128, :] = down(scale)
    per = 128 // n_lead
    rows, scale = features(group // per)
    piece = pl.ds(pl.multiple_of((group % per) * n_lead, n_lead), n_lead)
    lowr[...] = down(scale)
    rows_s[256:, :] = lowr[piece, :]
    lowr[:, 0:16] = jnp.transpose(rows)
    rowf[256:, :] = lowr[piece, 0:16].astype(BF16)

    base = jnp.concatenate([taps_ref[0:1, :], taps_ref[1:2, :], jnp.zeros((1, 256), F32)], axis=1)
    full = pltpu.roll(
        jnp.broadcast_to(base, (512, 512)), 256, 1, stride=1, stride_axis=0
    )[:, :256]
    lowt[...] = full.astype(BF16)
    low_up = jnp.transpose(full).astype(BF16)

    def phases_of(b):
        at = jnp.maximum(x * blocks + b - 1, 0)
        row0 = (at // 8) * 32 + (at % 8) * 2
        parts = []
        for a in range(2):
            q = jnp.concatenate(
                [phase_ref[pl.ds(row0 + 16 * a + half, 1), :] for half in range(2)], axis=1
            )
            parts += list(halves(q))
        parts += [jnp.ones((1, BLK), F32), jnp.zeros((11, BLK), F32)]
        rows = jnp.concatenate(parts, axis=0)
        return rows.astype(BF16), jnp.transpose(rows).astype(BF16)

    def design(qt, slot, j0):
        scale = cols_s[:, j0 : j0 + 256]
        for r0 in range(0, BLK, CHUNK):
            turn = jnp.dot(
                qt[r0 : r0 + CHUNK, :], colf[:, j0 : j0 + 256], preferred_element_type=F32
            )
            dcol[slot][r0 : r0 + CHUNK, j0 : j0 + 256] = wave(turn, scale).astype(BF16)

    def design_rows(qf, slot):
        for r0 in range(0, n_rows, CHUNK):
            r1 = min(r0 + CHUNK, n_rows)
            turn = jnp.dot(rowf[r0:r1, :], qf, preferred_element_type=F32)
            scale = rows_s[r0:r1, :]
            d = wave(turn, jnp.concatenate([scale, scale], axis=1))
            drow[slot][r0:r1, :] = d.astype(BF16)

    def filter_cols(b, s0, s1, j0):
        both = jnp.concatenate(
            [dcol[s0][:, j0 : j0 + 256], dcol[s1][:, j0 : j0 + 256]], axis=0
        )
        f = jnp.dot(low_up, both, preferred_element_type=F32)
        fcol[pl.ds(pl.multiple_of(b * BLK, BLK), BLK), j0 : j0 + 256] = f.astype(BF16)

    def filter_rows(b, s0, s1):
        both = jnp.concatenate([drow[s0][...], drow[s1][...]], axis=1)
        f = jnp.dot(both, lowt[...], preferred_element_type=F32)
        frow[:, pl.ds(pl.multiple_of(b * BLK, BLK), BLK)] = f.astype(BF16)

    wide = range(0, n_tiles * 128, 256)
    for b in range(2):
        qf, qt = phases_of(b)
        for j0 in wide:
            design(qt, b, j0)
        design_rows(qf, b)

    @pl.when(x == 0)
    def _():
        d0[...] = jnp.zeros_like(d0)
        e0[...] = jnp.zeros_like(e0)

    @pl.loop(0, blocks // 3)
    def _(step):
        for s in range(3):
            b = step * 3 + s
            qf, qt = phases_of(b + 2)
            for j0 in wide:
                filter_cols(b, s, (s + 1) % 3, j0)
                design(qt, (s + 2) % 3, j0)
            filter_rows(b, s, (s + 1) % 3)
            design_rows(qf, (s + 2) % 3)

    for b in range(blocks // 3 * 3, blocks):
        for j0 in wide:
            filter_cols(b, b % 3, (b + 1) % 3, j0)
        filter_rows(b, b % 3, (b + 1) % 3)

    total = 1.0 / (blocks * BLK * NX)
    for j0 in wide:
        g = jnp.dot(frow[...], fcol[:, j0 : j0 + 256], preferred_element_type=F32) * total
        if j0 == 0:
            oa_ref[...] = g[:256].reshape(NX, 64, 256)
            la_ref[...] = g[256:]
        else:
            held[...] = g[:256]
            ob_ref[:, :, j0 - 256 : j0] = g[:256].astype(BF16).reshape(NX, 64, 256)
            oc_ref[:, j0 - 256 : j0] = held[pl.ds(pl.multiple_of(x * 64, 64), 64), :]
            lb_ref[:, j0 - 256 : j0] = g[256:]


def dot(a, b, dims=((1,), (0,))):
    return lax.dot_general(a, b, (dims, ((), ())), precision=HIGH, preferred_element_type=F32)


def split3(v):
    hi = v.astype(BF16)
    v = v - hi.astype(F32)
    mid = v.astype(BF16)
    low = (v - mid.astype(F32)).astype(BF16)
    return hi, mid, low


NB = 32


def block_inverse(a):
    groups = NB // 8
    full = (8, 128)
    sub = lax.broadcasted_iota(jnp.int32, full, 0)
    lane = lax.broadcasted_iota(jnp.int32, full, 1)

    def spread(v, s):
        return jnp.broadcast_to(v[s : s + 1, :], full)

    col = [
        {k: jnp.broadcast_to(a[8 * k : 8 * k + 8, c : c + 1], full) for k in range(c // 8, groups)}
        for c in range(NB)
    ]
    inv = [jnp.where(lane == sub + 8 * k, 1.0, 0.0).astype(F32) for k in range(groups)]
    root = [jnp.zeros(full, F32) for _ in range(groups)]
    for i in range(NB):
        k0, s = divmod(i, 8)
        pivot = spread(col[i][k0], s)
        over = 1.0 / pivot
        root[k0] = jnp.where(sub == s, lax.rsqrt(pivot), root[k0])
        ratio = {k: col[i][k] * over for k in range(k0, groups)}
        ratio[k0] = jnp.where(sub > s, ratio[k0], 0.0)
        for c in range(i + 1, NB):
            kc, sc = divmod(c, 8)
            top = spread(col[i][kc], sc)
            for k in range(kc, groups):
                col[c][k] = col[c][k] - ratio[k] * top
        top = spread(inv[k0], s)
        for k in range(k0, groups):
            inv[k] = inv[k] - ratio[k] * top
    return jnp.concatenate([inv[k] * root[k] for k in range(groups)], axis=0)


def final_kernel(
    la_ref, lb_ref, oa_ref, ob_ref, oc_ref, ridge0_ref, ridge_ref, panel_ref, schur_ref,
    slab_a, slab_b, got_la, got_lb, got_oa, got_ob, ridge4, ridge_far, mat, nxt_ref,
    s_la, r_la, s_lb, r_lb, s_oa, r_oa, s_ob, r_ob, s_r, r_r, s_f, r_f,
    s_za, r_za, s_zb, r_zb, s_ca, r_ca, s_cb, r_cb,
):
    x, y, z, core = place()
    e, p = lax.axis_index("epoch"), lax.axis_index("prow")
    nz = 8

    def group(zz, cc):
        return ((zz % 4) * 2 + cc) * 2 + zz // 4

    g = group(z, core)
    barrier = pltpu.get_barrier_semaphore()
    peers = [device((x + i) % NX, z, core) for i in range(1, NX)]
    tall = [device(x, (z + i) % nz, core) for i in range(1, nz)]
    far = [device((x + i) % NX, (z + 4) % nz, core) for i in range(NX)]
    other = device(x, z, 1 - core)
    greeted = peers + tall + far[1:] + [other]
    for peer in greeted:
        pl.semaphore_signal(barrier, inc=1, device_id=peer, device_id_type=MESH)
    pl.semaphore_wait(barrier, len(greeted))

    def put(src, dst, send, recv, peer):
        copy = pltpu.make_async_remote_copy(
            src_ref=src, dst_ref=dst, send_sem=send, recv_sem=recv,
            device_id=peer, device_id_type=MESH,
        )
        copy.start()
        return copy

    def to_x(src, got, send, recv):
        return [put(src(i), got.at[i - 1], send.at[i - 1], recv.at[i - 1], peers[i - 1]) for i in range(1, NX)]

    def to_z(slab, send, recv):
        return [put(slab.at[g], slab.at[g], send.at[i - 1], recv.at[i - 1], tall[i - 1]) for i in range(1, nz)]

    def to_core(slab, send, recv, i):
        k = group((z + nz - i) % nz, core)
        return put(slab.at[k], slab.at[k], send.at[i], recv.at[i], other)

    lead_a = to_x(lambda i: la_ref, got_la, s_la, r_la)
    ridges = [
        put(ridge0_ref, ridge4.at[x], s_r.at[i - 1], r_r.at[i - 1], peers[i - 1])
        for i in range(1, NX)
    ] + [
        put(ridge0_ref, ridge_far.at[x], s_f.at[i], r_f.at[i], far[i]) for i in range(NX)
    ]
    lead_b = to_x(lambda i: lb_ref, got_lb, s_lb, r_lb)
    ridge4[x] = ridge0_ref[...]
    for copy in lead_a:
        copy.wait()
    slab_a[g] = la_ref[...] + got_la[0] + got_la[1] + got_la[2]
    z_a = to_z(slab_a, s_za, r_za)
    c_a = [to_core(slab_a, s_ca, r_ca, 0)]
    for copy in lead_b:
        copy.wait()
    slab_b[g] = (lb_ref[...] + got_lb[0] + got_lb[1] + got_lb[2]).astype(BF16)
    z_b = to_z(slab_b, s_zb, r_zb)
    c_b = [to_core(slab_b, s_cb, r_cb, 0)]
    own_a = to_x(lambda i: oa_ref.at[(x + i) % NX], got_oa, s_oa, r_oa)
    own_b = to_x(lambda i: ob_ref.at[(x + i) % NX], got_ob, s_ob, r_ob)
    for i in range(1, nz):
        z_a[i - 1].wait()
        c_a.append(to_core(slab_a, s_ca, r_ca, i))
    for copy in c_a + ridges:
        copy.wait()

    lane = lax.broadcasted_iota(jnp.int32, (64, B), 1)
    sub = lax.broadcasted_iota(jnp.int32, (64, B), 0)

    def column(row):
        return jnp.transpose(jnp.broadcast_to(row, (128, 128)))[:64, 0:1]

    lead_ridge = [column(jnp.where(z < 4, ridge4[k], ridge_far[k])) for k in range(4)]
    for k in range(4):
        rows = slab_a[4 * k : 4 * k + 4].reshape(64, B)
        mat[64 * k : 64 * k + 64, 0:B] = rows + jnp.where(lane == sub + 64 * k, lead_ridge[k], 0.0)
        mat[64 * k : 64 * k + 64, B:] = jnp.where(lane == sub + 64 * k, 1.0, 0.0).astype(F32)

    nxt_ref[...] = mat[0:NB, 0:128]
    wide = lax.broadcasted_iota(jnp.int32, (NB, B), 1)

    def block_step(j, carry):
        r0 = pl.multiple_of(j * NB, NB)
        r1 = r0 + NB
        w = block_inverse(nxt_ref[:, 0:NB])[:, 0:NB]
        rj = dot(w, mat[pl.ds(r0, NB), :])
        mat[pl.ds(r0, NB), :] = rj
        hi, mid, low = split3(rj)
        right = jnp.concatenate([hi, mid, hi, low, hi, mid], axis=0)
        hi, mid, low = split3(jnp.where(wide >= r1, rj[:, 0:B], 0.0))
        left = jnp.concatenate([hi, hi, mid, hi, low, mid], axis=0)
        mat[...] -= lax.dot_general(
            left, right, (((0,), (0,)), ((), ())), preferred_element_type=F32
        )
        r1 = pl.multiple_of(jnp.minimum(r1, B - NB), NB)
        nxt_ref[...] = pltpu.roll(mat[pl.ds(r1, NB), 0:B], B - r1, 1)[:, 0:128]
        return carry

    half = B // NB // 2
    lax.fori_loop(0, half, block_step, 0)
    for i in range(1, nz):
        z_b[i - 1].wait()
        c_b.append(to_core(slab_b, s_cb, r_cb, i))
    lax.fori_loop(half, 2 * half, block_step, 0)

    for copy in own_a:
        copy.wait()
    first = (e * 8 + p) * 64
    own_ridge = column(ridge_ref[...])
    winv = mat[:, B:]
    lead = oa_ref[x] + got_oa[0] + got_oa[1] + got_oa[2]
    lead = lead + jnp.where(lane == sub + first, own_ridge, 0.0)
    panel = dot(lead, winv, ((1,), (1,)))
    panel_ref[...] = panel
    for copy in c_b:
        copy.wait()
    for copy in own_b:
        copy.wait()
    cols = lb_ref.shape[1]
    for j0 in range(0, cols, B):
        here = slab_b[:, :, j0 : j0 + B].reshape(B, B).astype(F32)
        if j0 == 0:
            exact = [
                slab_a[4 * k : 4 * k + 4].reshape(64, B)
                + jnp.where(lane == sub + 64 * k, lead_ridge[k], 0.0)
                for k in range(4)
            ]
            here = jnp.where(y == 0, jnp.concatenate(exact, axis=0), here)
        right = dot(winv, here)
        at = slice(j0, j0 + B)
        tile = oc_ref[:, at] + got_ob[0, :, at].astype(F32)
        tile = tile + got_ob[1, :, at].astype(F32) + got_ob[2, :, at].astype(F32)
        tile = tile + jnp.where(lane + (y * cols + j0) == sub + first, own_ridge, 0.0)
        schur_ref[:, at] = tile - dot(panel, right)


def on_device(steps, harmonic, col_scale, taps, ridge):
    params = harmonic.shape[0]
    cols = params // 4
    width = cols + B
    dma = pltpu.SemaphoreType.DMA
    steps3 = steps.reshape(2, 16, 128)
    ridge_row = jnp.pad(ridge.reshape(1, -1), ((0, 0), (0, 128 - ridge.shape[0])))
    phase, ridge0 = pl.pallas_call(
        phase_kernel,
        out_shape=(
            jax.ShapeDtypeStruct((256, 128), F32),
            jax.ShapeDtypeStruct((1, 128), F32),
        ),
        in_specs=[VMEM] * 2,
        out_specs=(VMEM, VMEM),
        scratch_shapes=[
            pltpu.VMEM((8, 2, 16, 128), jnp.int32),
            pltpu.VMEM((8, 1, 128), F32),
            dma((8,)), dma((8,)), dma((8,)), dma((8,)),
        ],
        compiler_params=pltpu.CompilerParams(collective_id=0, has_side_effects=True),
        name="phases",
    )(steps3, ridge_row)
    here = 4096
    n_rows = 272
    parts = pl.pallas_call(
        tile_kernel,
        out_shape=(
            jax.ShapeDtypeStruct((16, B), F32),
            jax.ShapeDtypeStruct((16, cols), F32),
            jax.ShapeDtypeStruct((NX, 64, B), F32),
            jax.ShapeDtypeStruct((NX, 64, cols), BF16),
            jax.ShapeDtypeStruct((64, cols), F32),
        ),
        in_specs=[VMEM] * 4,
        out_specs=(VMEM,) * 5,
        scratch_shapes=[
            pltpu.VMEM((16, width), BF16),
            pltpu.VMEM((1, width), F32),
            pltpu.VMEM((n_rows, 16), BF16),
            pltpu.VMEM((n_rows, 128), F32),
            pltpu.VMEM((512, 256), BF16),
            pltpu.VMEM((128, 128), F32),
            *([pltpu.VMEM((BLK, width), BF16)] * 3),
            *([pltpu.VMEM((n_rows, BLK), BF16)] * 3),
            pltpu.VMEM((here, width), BF16),
            pltpu.VMEM((n_rows, here), BF16),
            pltpu.VMEM((256, 256), F32),
        ],
        compiler_params=pltpu.CompilerParams(vmem_limit_bytes=60 * 1024 * 1024),
        name="tile",
    )(phase, harmonic.reshape(-1, 128), col_scale.reshape(-1, 128), taps.reshape(2, 128))
    return pl.pallas_call(
        final_kernel,
        out_shape=(
            jax.ShapeDtypeStruct((64, B), F32),
            jax.ShapeDtypeStruct((64, cols), F32),
        ),
        in_specs=[VMEM] * 7,
        out_specs=(VMEM, VMEM),
        scratch_shapes=[
            pltpu.VMEM((16, 16, B), F32),
            pltpu.VMEM((16, 16, cols), BF16),
            pltpu.VMEM((NX - 1, 16, B), F32),
            pltpu.VMEM((NX - 1, 16, cols), F32),
            pltpu.VMEM((NX - 1, 64, B), F32),
            pltpu.VMEM((NX - 1, 64, cols), BF16),
            pltpu.VMEM((NX, 1, 128), F32),
            pltpu.VMEM((NX, 1, 128), F32),
            pltpu.VMEM((B, 2 * B), F32),
            pltpu.VMEM((NB, 128), F32),
            *([dma((3,))] * 10), dma((4,)), dma((4,)), *([dma((7,))] * 4), *([dma((8,))] * 4),
        ],
        compiler_params=pltpu.CompilerParams(collective_id=1, has_side_effects=True),
        name="final",
    )(*parts, ridge0, ridge_row)


def solution(mesh):
    row = P(("epoch", "prow"))
    return jax.shard_map(
        on_device,
        mesh=mesh,
        in_specs=(P(None, "epoch"), P(), P(), P(), row),
        out_specs=(P(("epoch", "prow"), None), P(("epoch", "prow"), "pcol")),
        check_vma=False,
    )
```

```python
import functools

import jax
import jax.numpy as jnp
from jax import lax
from jax.experimental import pallas as pl
from jax.experimental.pallas import tpu as pltpu
from jax.sharding import PartitionSpec as P

F32 = jnp.float32
BF16 = jnp.bfloat16
MESH = pl.DeviceIdType.MESH
HIGH = lax.Precision.HIGHEST
B = 256
BLK = 256
CHUNK = 64
PERIOD = 4096
NX = 4
WAVE = (8.88573567404434, -58.45953046181323, 115.03267724691959, -100.39492606524867)
ROUND = 12582912.0
VMEM = pl.BlockSpec(memory_space=pltpu.VMEM)


def place():
    e, p, y = (lax.axis_index(a) for a in ("epoch", "prow", "pcol"))
    core, z_lo = e % 2, e // 2
    x, z_hi = p % NX, p // NX
    return x, y, z_hi * 4 + z_lo, core


def device(x, z, core):
    return {"epoch": (z % 4) * 2 + core, "prow": (z // 4) * NX + x}


def wave(turn, scale):
    whole = (turn + ROUND) - ROUND
    z = 0.25 - jnp.abs(turn - whole)
    s = z * z
    poly = s + WAVE[2] / WAVE[3]
    for c in (WAVE[1], WAVE[0]):
        poly = poly * s + c / WAVE[3]
    return poly * (z * scale)


def halves(v):
    hi = jnp.floor(v * 64.0) * (1.0 / 64.0)
    return hi, v - hi


def dot(a, b, dims=((1,), (0,))):
    return lax.dot_general(a, b, (dims, ((), ())), precision=HIGH, preferred_element_type=F32)


def split3(v):
    hi = v.astype(BF16)
    v = v - hi.astype(F32)
    mid = v.astype(BF16)
    low = (v - mid.astype(F32)).astype(BF16)
    return hi, mid, low


NB = 32


def block_inverse(a):
    groups = NB // 8
    full = (8, 128)
    sub = lax.broadcasted_iota(jnp.int32, full, 0)
    lane = lax.broadcasted_iota(jnp.int32, full, 1)

    def spread(v, s):
        return jnp.broadcast_to(v[s : s + 1, :], full)

    col = [
        {k: jnp.broadcast_to(a[8 * k : 8 * k + 8, c : c + 1], full) for k in range(c // 8, groups)}
        for c in range(NB)
    ]
    inv = [jnp.where(lane == sub + 8 * k, 1.0, 0.0).astype(F32) for k in range(groups)]
    root = [jnp.zeros(full, F32) for _ in range(groups)]
    for i in range(NB):
        k0, s = divmod(i, 8)
        pivot = spread(col[i][k0], s)
        over = 1.0 / pivot
        root[k0] = jnp.where(sub == s, lax.rsqrt(pivot), root[k0])
        ratio = {k: col[i][k] * over for k in range(k0, groups)}
        ratio[k0] = jnp.where(sub > s, ratio[k0], 0.0)
        for c in range(i + 1, NB):
            kc, sc = divmod(c, 8)
            top = spread(col[i][kc], sc)
            for k in range(kc, groups):
                col[c][k] = col[c][k] - ratio[k] * top
        top = spread(inv[k0], s)
        for k in range(k0, groups):
            inv[k] = inv[k] - ratio[k] * top
    return jnp.concatenate([inv[k] * root[k] for k in range(groups)], axis=0)


def whole_kernel(
    steps_ref, harm_ref, scale_ref, taps_ref, ridge_ref, out_ref,
    every, every_ridge, phase_ref,
    colf, cols_s, rowf, rows_s, lowt, lowr, d0, d1, d2, e0, e1, e2, fcol, frow, held,
    la_ref, lb_ref, oa_ref, ob_ref, oc_ref,
    slab_a, slab_b, got_la, got_lb, got_oa, got_ob, ridge4, ridge_far, mat, nxt_ref,
    s_st, r_st, s_ri, r_ri,
    s_la, r_la, s_lb, r_lb, s_oa, r_oa, s_ob, r_ob, s_r, r_r, s_f, r_f,
    s_za, r_za, s_zb, r_zb, s_ca, r_ca, s_cb, r_cb,
):
    x, y, z, core = place()
    e, p = lax.axis_index("epoch"), lax.axis_index("prow")
    nz, ne = 8, 8

    def group(zz, cc):
        return ((zz % 4) * 2 + cc) * 2 + zz // 4

    g = group(z, core)
    peers = [device((x + i) % NX, z, core) for i in range(1, NX)]
    tall = [device(x, (z + i) % nz, core) for i in range(1, nz)]
    ring = [{"epoch": (e + i) % ne} for i in range(1, ne)]
    across = [device(x, (1 - z // 4) * 4 + i, core) for i in range(4)]
    other = device(x, z, 1 - core)
    barrier = pltpu.get_barrier_semaphore()
    greeted = ring + peers + across
    for peer in greeted:
        pl.semaphore_signal(barrier, inc=1, device_id=peer, device_id_type=MESH)
    pl.semaphore_wait(barrier, len(greeted))

    def put(src, dst, send, recv, peer):
        copy = pltpu.make_async_remote_copy(
            src_ref=src, dst_ref=dst, send_sem=send, recv_sem=recv,
            device_id=peer, device_id_type=MESH,
        )
        copy.start()
        return copy

    def to_x(src, got, send, recv):
        return [put(src(i), got.at[i - 1], send.at[i - 1], recv.at[i - 1], peers[i - 1]) for i in range(1, NX)]

    def to_z(slab, send, recv):
        return [put(slab.at[g], slab.at[g], send.at[i - 1], recv.at[i - 1], tall[i - 1]) for i in range(1, nz)]

    def to_core(slab, send, recv, i):
        k = group((z + nz - i) % nz, core)
        return put(slab.at[k], slab.at[k], send.at[i], recv.at[i], other)

    given = [
        put(steps_ref, every.at[e], s_st.at[i], r_st.at[i], ring[i]) for i in range(ne - 1)
    ] + [
        put(ridge_ref, every_ridge.at[e], s_ri.at[i], r_ri.at[i], ring[i]) for i in range(ne - 1)
    ]
    every[e] = steps_ref[...]
    every_ridge[e] = ridge_ref[...]
    blocks = (ne * steps_ref.shape[1] // BLK) // NX
    n_rows = rows_s.shape[0]
    n_lead = n_rows - 256
    n_tiles = colf.shape[1] // 128
    cols_here = n_tiles - 2
    dcol, drow = (d0, d1, d2), (e0, e1, e2)

    def features(k):
        h = harm_ref[pl.ds(k, 1), :]
        order = lax.shift_right_logical(h, 6).astype(F32)
        degree = (h & 63).astype(F32)
        shift = jnp.full((1, 128), -0.125, F32)
        rows = jnp.concatenate(
            [order, order, degree, degree, shift, jnp.zeros((11, 128), F32)], axis=0
        )
        return rows, scale_ref[pl.ds(k, 1), :] * WAVE[3]

    def down(row):
        return jnp.transpose(jnp.broadcast_to(row, (128, 128)))

    for jt in range(n_tiles):
        k = jt if jt < 2 else y * cols_here + (jt - 2)
        rows, scale = features(k)
        colf[:, jt * 128 : jt * 128 + 128] = rows.astype(BF16)
        cols_s[:, jt * 128 : jt * 128 + 128] = scale
    for half in range(2):
        rows, scale = features(g * 2 + half)
        rowf[half * 128 : half * 128 + 128, :] = jnp.transpose(rows).astype(BF16)
        rows_s[half * 128 : half * 128 + 128, :] = down(scale)
    per = 128 // n_lead
    rows, scale = features(g // per)
    piece = pl.ds(pl.multiple_of((g % per) * n_lead, n_lead), n_lead)
    lowr[...] = down(scale)
    rows_s[256:, :] = lowr[piece, :]
    lowr[:, 0:16] = jnp.transpose(rows)
    rowf[256:, :] = lowr[piece, 0:16].astype(BF16)

    base = jnp.concatenate([taps_ref[0:1, :], taps_ref[1:2, :], jnp.zeros((1, 256), F32)], axis=1)
    full = pltpu.roll(
        jnp.broadcast_to(base, (512, 512)), 256, 1, stride=1, stride_axis=0
    )[:, :256]
    lowt[...] = full.astype(BF16)
    low_up = jnp.transpose(full).astype(BF16)


    pairs = 2 * ne
    rows = pairs * steps_ref.shape[1] // 128
    upper = (
        lax.broadcasted_iota(jnp.int32, (128, 128), 0)
        <= lax.broadcasted_iota(jnp.int32, (128, 128), 1)
    ).astype(BF16)
    r_at = lax.broadcasted_iota(jnp.int32, (rows, rows), 0)
    s_at = lax.broadcasted_iota(jnp.int32, (rows, rows), 1)
    same = r_at % 2 == s_at % 2
    key_r = ((r_at % pairs) // 2) * rows + r_at // pairs
    key_s = ((s_at % pairs) // 2) * rows + s_at // pairs
    before = jnp.where(same & (key_s < key_r), 1.0, 0.0).astype(BF16)
    for copy in given:
        copy.wait()
    flat = every[...].astype(F32).reshape(pairs, steps_ref.shape[1])
    stack = jnp.concatenate(
        [flat[:, 128 * k : 128 * k + 128] for k in range(rows // pairs)], axis=0
    )
    inside = jnp.dot(stack.astype(BF16), upper, preferred_element_type=F32)
    totals = jnp.broadcast_to(inside[:, 127:128], (rows, 128))
    high = jnp.floor(totals * (1.0 / 64.0))
    low = totals - high * 64.0
    earlier = jnp.dot(before, high.astype(BF16), preferred_element_type=F32) * 64.0
    earlier = earlier + jnp.dot(before, low.astype(BF16), preferred_element_type=F32)
    turns = (inside + earlier) * (1.0 / PERIOD)
    phase_ref[...] = turns - jnp.floor(turns)

    def phases_of(b):
        at = jnp.maximum(x * blocks + b - 1, 0)
        row0 = (at % 8) * 32 + (at // 8) * 2
        parts = []
        for a in range(2):
            q = jnp.concatenate(
                [phase_ref[pl.ds(row0 + 16 * half + a, 1), :] for half in range(2)], axis=1
            )
            parts += list(halves(q))
        parts += [jnp.ones((1, BLK), F32), jnp.zeros((11, BLK), F32)]
        rows = jnp.concatenate(parts, axis=0)
        return rows.astype(BF16), jnp.transpose(rows).astype(BF16)

    def design(qt, slot, j0):
        scale = cols_s[:, j0 : j0 + 256]
        for r0 in range(0, BLK, CHUNK):
            turn = jnp.dot(
                qt[r0 : r0 + CHUNK, :], colf[:, j0 : j0 + 256], preferred_element_type=F32
            )
            dcol[slot][r0 : r0 + CHUNK, j0 : j0 + 256] = wave(turn, scale).astype(BF16)

    def design_rows(qf, slot):
        for r0 in range(0, n_rows, CHUNK):
            r1 = min(r0 + CHUNK, n_rows)
            turn = jnp.dot(rowf[r0:r1, :], qf, preferred_element_type=F32)
            scale = rows_s[r0:r1, :]
            d = wave(turn, jnp.concatenate([scale, scale], axis=1))
            drow[slot][r0:r1, :] = d.astype(BF16)

    def filter_cols(b, s0, s1, j0):
        both = jnp.concatenate(
            [dcol[s0][:, j0 : j0 + 256], dcol[s1][:, j0 : j0 + 256]], axis=0
        )
        f = jnp.dot(low_up, both, preferred_element_type=F32)
        fcol[pl.ds(pl.multiple_of(b * BLK, BLK), BLK), j0 : j0 + 256] = f.astype(BF16)

    def filter_rows(b, s0, s1):
        both = jnp.concatenate([drow[s0][...], drow[s1][...]], axis=1)
        f = jnp.dot(both, lowt[...], preferred_element_type=F32)
        frow[:, pl.ds(pl.multiple_of(b * BLK, BLK), BLK)] = f.astype(BF16)

    wide = range(0, n_tiles * 128, 256)
    for b in range(2):
        qf, qt = phases_of(b)
        for j0 in wide:
            design(qt, b, j0)
        design_rows(qf, b)

    @pl.when(x == 0)
    def _():
        d0[...] = jnp.zeros_like(d0)
        e0[...] = jnp.zeros_like(e0)

    @pl.loop(0, blocks // 3)
    def _(step):
        for s in range(3):
            b = step * 3 + s
            qf, qt = phases_of(b + 2)
            for j0 in wide:
                filter_cols(b, s, (s + 1) % 3, j0)
                design(qt, (s + 2) % 3, j0)
            filter_rows(b, s, (s + 1) % 3)
            design_rows(qf, (s + 2) % 3)

    for b in range(blocks // 3 * 3, blocks):
        for j0 in wide:
            filter_cols(b, b % 3, (b + 1) % 3, j0)
        filter_rows(b, b % 3, (b + 1) % 3)

    total = 1.0 / (blocks * BLK * NX)

    def product(j0):
        return jnp.dot(frow[...], fcol[:, j0 : j0 + B], preferred_element_type=F32) * total

    part = product(0)
    la_ref[...] = part[B:]
    oa_ref[...] = part[:B].reshape(NX, 64, B)
    ridge4[x] = every_ridge[0]
    lead_a = to_x(lambda i: la_ref, got_la, s_la, r_la)
    ridges = [
        put(every_ridge.at[0], ridge4.at[x], s_r.at[i - 1], r_r.at[i - 1], peers[i - 1])
        for i in range(1, NX)
    ]
    for j0 in range(0, cols_here * 128, B):
        part = product(B + j0)
        at = slice(j0, j0 + B)
        lb_ref[:, at] = part[B:]
        held[...] = part[:B]
        ob_ref[:, :, at] = part[:B].astype(BF16).reshape(NX, 64, B)
        oc_ref[:, at] = held[pl.ds(pl.multiple_of(x * 64, 64), 64), :]
    lead_b = to_x(lambda i: lb_ref, got_lb, s_lb, r_lb)
    for copy in lead_a:
        copy.wait()
    slab_a[g] = la_ref[...] + got_la[0] + got_la[1] + got_la[2]
    z_a = to_z(slab_a, s_za, r_za)
    c_a = [to_core(slab_a, s_ca, r_ca, 0)]
    for copy in ridges:
        copy.wait()
    far = put(ridge4, ridge_far, s_f, r_f, device(x, (z + 4) % nz, core))
    own_a = to_x(lambda i: oa_ref.at[(x + i) % NX], got_oa, s_oa, r_oa)
    own_b = to_x(lambda i: ob_ref.at[(x + i) % NX], got_ob, s_ob, r_ob)
    for copy in lead_b:
        copy.wait()
    slab_b[g] = (lb_ref[...] + got_lb[0] + got_lb[1] + got_lb[2]).astype(BF16)
    z_b = to_z(slab_b, s_zb, r_zb)
    c_b = [to_core(slab_b, s_cb, r_cb, 0)]
    for i in range(1, nz):
        z_a[i - 1].wait()
        c_a.append(to_core(slab_a, s_ca, r_ca, i))
    far.wait()
    for copy in c_a:
        copy.wait()

    lane = lax.broadcasted_iota(jnp.int32, (64, B), 1)
    sub = lax.broadcasted_iota(jnp.int32, (64, B), 0)

    def column(row):
        return jnp.transpose(jnp.broadcast_to(row, (128, 64)))[:, 0:1]

    lead_ridge = [column(jnp.where(z < 4, ridge4[k], ridge_far[k])) for k in range(4)]
    for k in range(4):
        rows = slab_a[4 * k : 4 * k + 4].reshape(64, B)
        mat[64 * k : 64 * k + 64, 0:B] = rows + jnp.where(lane == sub + 64 * k, lead_ridge[k], 0.0)
        mat[64 * k : 64 * k + 64, B:] = jnp.where(lane == sub + 64 * k, 1.0, 0.0).astype(F32)

    nxt_ref[...] = mat[0:NB, 0:128]
    wide = lax.broadcasted_iota(jnp.int32, (NB, B), 1)

    def block_step(j, carry):
        r0 = pl.multiple_of(j * NB, NB)
        r1 = r0 + NB
        w = block_inverse(nxt_ref[:, 0:NB])[:, 0:NB]
        rj = dot(w, mat[pl.ds(r0, NB), :])
        mat[pl.ds(r0, NB), :] = rj
        hi, mid, low = split3(rj)
        right = jnp.concatenate([hi, mid, hi, low, hi, mid], axis=0)
        hi, mid, low = split3(jnp.where(wide >= r1, rj[:, 0:B], 0.0))
        left = jnp.concatenate([hi, hi, mid, hi, low, mid], axis=0)
        mat[...] -= lax.dot_general(
            left, right, (((0,), (0,)), ((), ())), preferred_element_type=F32
        )
        r1 = pl.multiple_of(jnp.minimum(r1, B - NB), NB)
        nxt_ref[...] = pltpu.roll(mat[pl.ds(r1, NB), 0:B], B - r1, 1)[:, 0:128]
        return carry

    half = B // NB // 2
    lax.fori_loop(0, half, block_step, 0)
    for i in range(1, nz):
        z_b[i - 1].wait()
        c_b.append(to_core(slab_b, s_cb, r_cb, i))
    lax.fori_loop(half, 2 * half, block_step, 0)

    for copy in own_a:
        copy.wait()
    first = (e * 8 + p) * 64
    own_ridge = column(ridge_ref[...])
    winv = mat[:, B:]
    lead = oa_ref[x] + got_oa[0] + got_oa[1] + got_oa[2]
    lead = lead + jnp.where(lane == sub + first, own_ridge, 0.0)
    panel = dot(lead, winv, ((1,), (1,)))
    out_ref[:, 0:B] = panel
    for copy in c_b:
        copy.wait()
    for copy in own_b:
        copy.wait()
    cols = lb_ref.shape[1]
    for j0 in range(0, cols, B):
        here = slab_b[:, :, j0 : j0 + B].reshape(B, B).astype(F32)
        if j0 == 0:
            exact = [
                slab_a[4 * k : 4 * k + 4].reshape(64, B)
                + jnp.where(lane == sub + 64 * k, lead_ridge[k], 0.0)
                for k in range(4)
            ]
            here = jnp.where(y == 0, jnp.concatenate(exact, axis=0), here)
        right = dot(winv, here)
        at = slice(j0, j0 + B)
        tile = oc_ref[:, at] + got_ob[0, :, at].astype(F32)
        tile = tile + got_ob[1, :, at].astype(F32) + got_ob[2, :, at].astype(F32)
        tile = tile + jnp.where(lane + (y * cols + j0) == sub + first, own_ridge, 0.0)
        out_ref[:, B + j0 : B + j0 + B] = tile - dot(panel, right)


def split_kernel(both_ref, panel_ref, schur_ref):
    panel_ref[...] = both_ref[:, 0:B]
    schur_ref[...] = both_ref[:, B:]


def on_device(steps, harmonic, col_scale, taps, ridge):
    cols = harmonic.shape[0] // 4
    width = cols + B
    here, n_rows = 4096, 272
    dma = pltpu.SemaphoreType.DMA
    vmem = pltpu.VMEM
    both = pl.pallas_call(
        whole_kernel,
        out_shape=jax.ShapeDtypeStruct((64, width), F32),
        in_specs=[VMEM] * 5,
        out_specs=VMEM,
        scratch_shapes=[
            vmem((8, 2, steps.shape[1]), jnp.int32),
            vmem((8, 1, 64), F32),
            vmem((256, 128), F32),
            vmem((16, width), BF16),
            vmem((1, width), F32),
            vmem((n_rows, 16), BF16),
            vmem((n_rows, 128), F32),
            vmem((512, 256), BF16),
            vmem((128, 128), F32),
            *([vmem((BLK, width), BF16)] * 3),
            *([vmem((n_rows, BLK), BF16)] * 3),
            vmem((here, width), BF16),
            vmem((n_rows, here), BF16),
            vmem((256, 256), F32),
            vmem((16, B), F32),
            vmem((16, cols), F32),
            vmem((NX, 64, B), F32),
            vmem((NX, 64, cols), BF16),
            vmem((64, cols), F32),
            vmem((16, 16, B), F32),
            vmem((16, 16, cols), BF16),
            vmem((NX - 1, 16, B), F32),
            vmem((NX - 1, 16, cols), F32),
            vmem((NX - 1, 64, B), F32),
            vmem((NX - 1, 64, cols), BF16),
            vmem((NX, 1, 64), F32),
            vmem((NX, 1, 64), F32),
            vmem((B, 2 * B), F32),
            vmem((NB, 128), F32),
            *([dma((7,))] * 4), *([dma((3,))] * 10), dma, dma,
            *([dma((7,))] * 4), *([dma((8,))] * 4),
        ],
        compiler_params=pltpu.CompilerParams(
            collective_id=0, has_side_effects=True, vmem_limit_bytes=60 * 1024 * 1024
        ),
        name="whole",
    )(
        steps,
        harmonic.reshape(-1, 128),
        col_scale.reshape(-1, 128),
        taps.reshape(2, 128),
        ridge.reshape(1, -1),
    )
    return pl.pallas_call(
        split_kernel,
        out_shape=(
            jax.ShapeDtypeStruct((64, B), F32),
            jax.ShapeDtypeStruct((64, cols), F32),
        ),
        in_specs=[VMEM],
        out_specs=(VMEM, VMEM),
        name="split",
    )(both)


def solution(mesh):
    row = P(("epoch", "prow"))
    return jax.shard_map(
        on_device,
        mesh=mesh,
        in_specs=(P(None, "epoch"), P(), P(), P(), row),
        out_specs=(P(("epoch", "prow"), None), P(("epoch", "prow"), "pcol")),
        check_vma=False,
    )
```

```python
import functools

import jax
import jax.numpy as jnp
from jax import lax
from jax.experimental import pallas as pl
from jax.experimental.pallas import tpu as pltpu
from jax.sharding import PartitionSpec as P

F32 = jnp.float32
BF16 = jnp.bfloat16
MESH = pl.DeviceIdType.MESH
HIGH = lax.Precision.HIGHEST
B = 256
BLK = 256
CHUNK = 64
PERIOD = 4096
NX = 4
WAVE = (8.88573567404434, -58.45953046181323, 115.03267724691959, -100.39492606524867)
ROUND = 12582912.0
VMEM = pl.BlockSpec(memory_space=pltpu.VMEM)


def place():
    e, p, y = (lax.axis_index(a) for a in ("epoch", "prow", "pcol"))
    core, z_lo = e % 2, e // 2
    x, z_hi = p % NX, p // NX
    return x, y, z_hi * 4 + z_lo, core


def device(x, z, core):
    return {"epoch": (z % 4) * 2 + core, "prow": (z // 4) * NX + x}


def wave(turn, scale):
    whole = (turn + ROUND) - ROUND
    z = 0.25 - jnp.abs(turn - whole)
    s = z * z
    poly = s + WAVE[2] / WAVE[3]
    for c in (WAVE[1], WAVE[0]):
        poly = poly * s + c / WAVE[3]
    return poly * (z * scale)


def halves(v):
    hi = jnp.floor(v * 64.0) * (1.0 / 64.0)
    return hi, v - hi


def dot(a, b, dims=((1,), (0,))):
    return lax.dot_general(a, b, (dims, ((), ())), precision=HIGH, preferred_element_type=F32)


def split3(v):
    hi = v.astype(BF16)
    v = v - hi.astype(F32)
    mid = v.astype(BF16)
    low = (v - mid.astype(F32)).astype(BF16)
    return hi, mid, low


NB = 32


def block_inverse(a):
    groups = NB // 8
    full = (8, 128)
    sub = lax.broadcasted_iota(jnp.int32, full, 0)
    lane = lax.broadcasted_iota(jnp.int32, full, 1)

    def spread(v, s):
        return jnp.broadcast_to(v[s : s + 1, :], full)

    col = [
        {k: jnp.broadcast_to(a[8 * k : 8 * k + 8, c : c + 1], full) for k in range(c // 8, groups)}
        for c in range(NB)
    ]
    inv = [jnp.where(lane == sub + 8 * k, 1.0, 0.0).astype(F32) for k in range(groups)]
    root = [jnp.zeros(full, F32) for _ in range(groups)]
    for i in range(NB):
        k0, s = divmod(i, 8)
        pivot = spread(col[i][k0], s)
        over = 1.0 / pivot
        root[k0] = jnp.where(sub == s, lax.rsqrt(pivot), root[k0])
        ratio = {k: col[i][k] * over for k in range(k0, groups)}
        ratio[k0] = jnp.where(sub > s, ratio[k0], 0.0)
        for c in range(i + 1, NB):
            kc, sc = divmod(c, 8)
            top = spread(col[i][kc], sc)
            for k in range(kc, groups):
                col[c][k] = col[c][k] - ratio[k] * top
        top = spread(inv[k0], s)
        for k in range(k0, groups):
            inv[k] = inv[k] - ratio[k] * top
    return jnp.concatenate([inv[k] * root[k] for k in range(groups)], axis=0)


def whole_kernel(
    steps_ref, harm_ref, scale_ref, taps_ref, ridge_ref, out_ref,
    every, every_ridge, phase_ref,
    colf, cols_s, rowf, rows_s, lowt, lowr, d0, d1, d2, e0, e1, e2, fcol, frow, mine, theirs, got_p,
    la_ref, lb_ref, oa_ref, ob_ref, oc_ref,
    slab_a, slab_b, got_la, got_lb, got_oa, got_ob, ridge4, ridge_far, mat, nxt_ref,
    s_st, r_st, s_ri, r_ri, s_p, r_p,
    s_la, r_la, s_lb, r_lb, s_oa, r_oa, s_ob, r_ob, s_r, r_r, s_f, r_f,
    s_za, r_za, s_zb, r_zb, s_ca, r_ca, s_cb, r_cb,
):
    x, y, z, core = place()
    e, p = lax.axis_index("epoch"), lax.axis_index("prow")
    nz, ne = 8, 8

    def group(zz, cc):
        return ((zz % 4) * 2 + cc) * 2 + zz // 4

    g = group(z, core)
    peers = [device((x + i) % NX, z, core) for i in range(1, NX)]
    tall = [device(x, (z + i) % nz, core) for i in range(1, nz)]
    ring = [{"epoch": (e + i) % ne} for i in range(1, ne)]
    across = [device(x, (1 - z // 4) * 4 + i, core) for i in range(4)]
    other = device(x, z, 1 - core)
    barrier = pltpu.get_barrier_semaphore()
    greeted = ring + peers + across
    for peer in greeted:
        pl.semaphore_signal(barrier, inc=1, device_id=peer, device_id_type=MESH)
    pl.semaphore_wait(barrier, len(greeted))

    def put(src, dst, send, recv, peer):
        copy = pltpu.make_async_remote_copy(
            src_ref=src, dst_ref=dst, send_sem=send, recv_sem=recv,
            device_id=peer, device_id_type=MESH,
        )
        copy.start()
        return copy

    def to_x(src, got, send, recv):
        return [put(src(i), got.at[i - 1], send.at[i - 1], recv.at[i - 1], peers[i - 1]) for i in range(1, NX)]

    def to_z(slab, send, recv):
        return [put(slab.at[g], slab.at[g], send.at[i - 1], recv.at[i - 1], tall[i - 1]) for i in range(1, nz)]

    def to_core(slab, send, recv, i):
        k = group((z + nz - i) % nz, core)
        return put(slab.at[k], slab.at[k], send.at[i], recv.at[i], other)

    given = [
        put(steps_ref, every.at[e], s_st.at[i], r_st.at[i], ring[i]) for i in range(ne - 1)
    ] + [
        put(ridge_ref, every_ridge.at[e], s_ri.at[i], r_ri.at[i], ring[i]) for i in range(ne - 1)
    ]
    every[e] = steps_ref[...]
    every_ridge[e] = ridge_ref[...]
    blocks = (ne * steps_ref.shape[1] // BLK) // (2 * NX)
    n_rows = rows_s.shape[0]
    n_side = n_rows // 2
    n_lead = n_side - 256
    n_tiles = colf.shape[1] // 128
    cols_here = n_tiles - 2
    dcol, drow = (d0, d1, d2), (e0, e1, e2)

    def features(k):
        h = harm_ref[pl.ds(k, 1), :]
        order = lax.shift_right_logical(h, 6).astype(F32)
        degree = (h & 63).astype(F32)
        shift = jnp.full((1, 128), -0.125, F32)
        rows = jnp.concatenate(
            [order, order, degree, degree, shift, jnp.zeros((11, 128), F32)], axis=0
        )
        return rows, scale_ref[pl.ds(k, 1), :] * WAVE[3]

    def down(row):
        return jnp.transpose(jnp.broadcast_to(row, (128, 128)))

    for jt in range(n_tiles):
        k = jt if jt < 2 else y * cols_here + (jt - 2)
        rows, scale = features(k)
        colf[:, jt * 128 : jt * 128 + 128] = rows.astype(BF16)
        cols_s[:, jt * 128 : jt * 128 + 128] = scale
    per = 128 // n_lead
    for side, gg in enumerate((group(z, 1 - core), g)):
        top = side * n_side
        for half in range(2):
            rows, scale = features(gg * 2 + half)
            at = slice(top + half * 128, top + half * 128 + 128)
            rowf[at, :] = jnp.transpose(rows).astype(BF16)
            rows_s[at, :] = down(scale)
        rows, scale = features(gg // per)
        piece = pl.ds(pl.multiple_of((gg % per) * n_lead, n_lead), n_lead)
        at = slice(top + 256, top + n_side)
        lowr[...] = down(scale)
        rows_s[at, :] = lowr[piece, :]
        lowr[:, 0:16] = jnp.transpose(rows)
        rowf[at, :] = lowr[piece, 0:16].astype(BF16)

    base = jnp.concatenate([taps_ref[0:1, :], taps_ref[1:2, :], jnp.zeros((1, 256), F32)], axis=1)
    full = pltpu.roll(
        jnp.broadcast_to(base, (512, 512)), 256, 1, stride=1, stride_axis=0
    )[:, :256]
    lowt[...] = full.astype(BF16)
    low_up = jnp.transpose(full).astype(BF16)


    pairs = 2 * ne
    rows = pairs * steps_ref.shape[1] // 128
    upper = (
        lax.broadcasted_iota(jnp.int32, (128, 128), 0)
        <= lax.broadcasted_iota(jnp.int32, (128, 128), 1)
    ).astype(BF16)
    r_at = lax.broadcasted_iota(jnp.int32, (rows, rows), 0)
    s_at = lax.broadcasted_iota(jnp.int32, (rows, rows), 1)
    same = r_at % 2 == s_at % 2
    key_r = ((r_at % pairs) // 2) * rows + r_at // pairs
    key_s = ((s_at % pairs) // 2) * rows + s_at // pairs
    before = jnp.where(same & (key_s < key_r), 1.0, 0.0).astype(BF16)
    for copy in given:
        copy.wait()
    flat = every[...].astype(F32).reshape(pairs, steps_ref.shape[1])
    stack = jnp.concatenate(
        [flat[:, 128 * k : 128 * k + 128] for k in range(rows // pairs)], axis=0
    )
    inside = jnp.dot(stack.astype(BF16), upper, preferred_element_type=F32)
    totals = jnp.broadcast_to(inside[:, 127:128], (rows, 128))
    high = jnp.floor(totals * (1.0 / 64.0))
    low = totals - high * 64.0
    earlier = jnp.dot(before, high.astype(BF16), preferred_element_type=F32) * 64.0
    earlier = earlier + jnp.dot(before, low.astype(BF16), preferred_element_type=F32)
    turns = (inside + earlier) * (1.0 / PERIOD)
    phase_ref[...] = turns - jnp.floor(turns)

    def phases_of(b):
        at = jnp.maximum((x * 2 + core) * blocks + b - 1, 0)
        row0 = (at % 8) * 32 + (at // 8) * 2
        parts = []
        for a in range(2):
            q = jnp.concatenate(
                [phase_ref[pl.ds(row0 + 16 * half + a, 1), :] for half in range(2)], axis=1
            )
            parts += list(halves(q))
        parts += [jnp.ones((1, BLK), F32), jnp.zeros((11, BLK), F32)]
        rows = jnp.concatenate(parts, axis=0)
        return rows.astype(BF16), jnp.transpose(rows).astype(BF16)

    def design(qt, slot, j0):
        scale = cols_s[:, j0 : j0 + 256]
        for r0 in range(0, BLK, CHUNK):
            turn = jnp.dot(
                qt[r0 : r0 + CHUNK, :], colf[:, j0 : j0 + 256], preferred_element_type=F32
            )
            dcol[slot][r0 : r0 + CHUNK, j0 : j0 + 256] = wave(turn, scale).astype(BF16)

    def design_rows(qf, slot):
        for r0 in range(0, n_rows, CHUNK):
            r1 = min(r0 + CHUNK, n_rows)
            turn = jnp.dot(rowf[r0:r1, :], qf, preferred_element_type=F32)
            scale = rows_s[r0:r1, :]
            d = wave(turn, jnp.concatenate([scale, scale], axis=1))
            drow[slot][r0:r1, :] = d.astype(BF16)

    def filter_cols(b, s0, s1, j0):
        both = jnp.concatenate(
            [dcol[s0][:, j0 : j0 + 256], dcol[s1][:, j0 : j0 + 256]], axis=0
        )
        f = jnp.dot(low_up, both, preferred_element_type=F32)
        fcol[pl.ds(pl.multiple_of(b * BLK, BLK), BLK), j0 : j0 + 256] = f.astype(BF16)

    def filter_rows(b, s0, s1):
        both = jnp.concatenate([drow[s0][...], drow[s1][...]], axis=1)
        f = jnp.dot(both, lowt[...], preferred_element_type=F32)
        frow[:, pl.ds(pl.multiple_of(b * BLK, BLK), BLK)] = f.astype(BF16)

    wide = range(0, n_tiles * 128, 256)
    for b in range(2):
        qf, qt = phases_of(b)
        for j0 in wide:
            design(qt, b, j0)
        design_rows(qf, b)

    @pl.when((x == 0) & (core == 0))
    def _():
        d0[...] = jnp.zeros_like(d0)
        e0[...] = jnp.zeros_like(e0)

    def block_pass(b, s, more):
        if more:
            qf, qt = phases_of(b + 2)
        for j0 in wide:
            filter_cols(b, s, (s + 1) % 3, j0)
            if more:
                design(qt, (s + 2) % 3, j0)
        filter_rows(b, s, (s + 1) % 3)
        if more:
            design_rows(qf, (s + 2) % 3)

    trips = (blocks - 1) // 3

    @pl.loop(0, trips)
    def _(step):
        for s in range(3):
            block_pass(step * 3 + s, s, True)

    for b in range(trips * 3, blocks):
        block_pass(b, b % 3, b + 2 <= blocks)

    total = 1.0 / (blocks * BLK * 2 * NX)

    def product(j):
        at = slice(j * B, j * B + B)
        part = jnp.dot(frow[...], fcol[:, at], preferred_element_type=F32) * total
        theirs[j] = part[:n_side]
        mine[j] = part[n_side:]
        return put(theirs.at[j], got_p.at[j], s_p.at[j], r_p.at[j], other)

    swaps = [product(0), product(1)]
    swaps[0].wait()
    part = mine[0] + got_p[0]
    la_ref[...] = part[B:]
    oa_ref[...] = part[:B].reshape(NX, 64, B)
    ridge4[x] = every_ridge[0]
    lead_a = to_x(lambda i: la_ref, got_la, s_la, r_la)
    ridges = [
        put(every_ridge.at[0], ridge4.at[x], s_r.at[i - 1], r_r.at[i - 1], peers[i - 1])
        for i in range(1, NX)
    ]
    own_piece = pl.ds(pl.multiple_of(x * 64, 64), 64)
    for j in range(1, n_tiles // 2):
        if j + 1 < n_tiles // 2:
            swaps.append(product(j + 1))
        swaps[j].wait()
        part = mine[j] + got_p[j]
        at = slice(j * B - B, j * B)
        lb_ref[:, at] = part[B:]
        ob_ref[:, :, at] = part[:B].astype(BF16).reshape(NX, 64, B)
        oc_ref[:, at] = mine[j, own_piece, :] + got_p[j, own_piece, :]
    lead_b = to_x(lambda i: lb_ref, got_lb, s_lb, r_lb)
    for copy in lead_a:
        copy.wait()
    slab_a[g] = la_ref[...] + got_la[0] + got_la[1] + got_la[2]
    z_a = to_z(slab_a, s_za, r_za)
    c_a = [to_core(slab_a, s_ca, r_ca, 0)]
    for copy in ridges:
        copy.wait()
    far = put(ridge4, ridge_far, s_f, r_f, device(x, (z + 4) % nz, core))
    own_a = to_x(lambda i: oa_ref.at[(x + i) % NX], got_oa, s_oa, r_oa)
    own_b = to_x(lambda i: ob_ref.at[(x + i) % NX], got_ob, s_ob, r_ob)
    for copy in lead_b:
        copy.wait()
    slab_b[g] = (lb_ref[...] + got_lb[0] + got_lb[1] + got_lb[2]).astype(BF16)
    z_b = to_z(slab_b, s_zb, r_zb)
    c_b = [to_core(slab_b, s_cb, r_cb, 0)]
    for i in range(1, nz):
        z_a[i - 1].wait()
        c_a.append(to_core(slab_a, s_ca, r_ca, i))
    far.wait()
    for copy in c_a:
        copy.wait()

    lane = lax.broadcasted_iota(jnp.int32, (64, B), 1)
    sub = lax.broadcasted_iota(jnp.int32, (64, B), 0)

    def column(row):
        return jnp.transpose(jnp.broadcast_to(row, (128, 64)))[:, 0:1]

    lead_ridge = [column(jnp.where(z < 4, ridge4[k], ridge_far[k])) for k in range(4)]
    for k in range(4):
        rows = slab_a[4 * k : 4 * k + 4].reshape(64, B)
        mat[64 * k : 64 * k + 64, 0:B] = rows + jnp.where(lane == sub + 64 * k, lead_ridge[k], 0.0)
        mat[64 * k : 64 * k + 64, B:] = jnp.where(lane == sub + 64 * k, 1.0, 0.0).astype(F32)

    nxt_ref[...] = mat[0:NB, 0:128]
    wide = lax.broadcasted_iota(jnp.int32, (NB, B), 1)

    def block_step(j, carry):
        r0 = pl.multiple_of(j * NB, NB)
        r1 = r0 + NB
        w = block_inverse(nxt_ref[:, 0:NB])[:, 0:NB]
        rj = dot(w, mat[pl.ds(r0, NB), :])
        mat[pl.ds(r0, NB), :] = rj
        hi, mid, low = split3(rj)
        right = jnp.concatenate([hi, mid, hi, low, hi, mid], axis=0)
        hi, mid, low = split3(jnp.where(wide >= r1, rj[:, 0:B], 0.0))
        left = jnp.concatenate([hi, hi, mid, hi, low, mid], axis=0)
        mat[...] -= lax.dot_general(
            left, right, (((0,), (0,)), ((), ())), preferred_element_type=F32
        )
        r1 = pl.multiple_of(jnp.minimum(r1, B - NB), NB)
        nxt_ref[...] = pltpu.roll(mat[pl.ds(r1, NB), 0:B], B - r1, 1)[:, 0:128]
        return carry

    half = B // NB // 2
    lax.fori_loop(0, half, block_step, 0)
    for i in range(1, nz):
        z_b[i - 1].wait()
        c_b.append(to_core(slab_b, s_cb, r_cb, i))
    lax.fori_loop(half, 2 * half, block_step, 0)

    for copy in own_a:
        copy.wait()
    first = (e * 8 + p) * 64
    own_ridge = column(ridge_ref[...])
    winv = mat[:, B:]
    lead = oa_ref[x] + got_oa[0] + got_oa[1] + got_oa[2]
    lead = lead + jnp.where(lane == sub + first, own_ridge, 0.0)
    panel = dot(lead, winv, ((1,), (1,)))
    weight = dot(panel, winv)
    parts = jnp.concatenate(split3(weight), axis=0)
    out_ref[:, 0:B] = panel
    for copy in c_b:
        copy.wait()
    for copy in own_b:
        copy.wait()
    cols = lb_ref.shape[1]
    for j0 in range(0, cols, B):
        three = jnp.dot(
            parts, slab_b[:, :, j0 : j0 + B].reshape(B, B), preferred_element_type=F32
        )
        known = three[0:64] + three[64:128] + three[128:192]
        if j0 == 0:
            exact = [
                slab_a[4 * k : 4 * k + 4].reshape(64, B)
                + jnp.where(lane == sub + 64 * k, lead_ridge[k], 0.0)
                for k in range(4)
            ]
            known = jnp.where(y == 0, dot(weight, jnp.concatenate(exact, axis=0)), known)
        at = slice(j0, j0 + B)
        tile = oc_ref[:, at] + got_ob[0, :, at].astype(F32)
        tile = tile + got_ob[1, :, at].astype(F32) + got_ob[2, :, at].astype(F32)
        tile = tile + jnp.where(lane + (y * cols + j0) == sub + first, own_ridge, 0.0)
        out_ref[:, B + j0 : B + j0 + B] = tile - known


def split_kernel(both_ref, panel_ref, schur_ref):
    panel_ref[...] = both_ref[:, 0:B]
    schur_ref[...] = both_ref[:, B:]


def on_device(steps, harmonic, col_scale, taps, ridge):
    cols = harmonic.shape[0] // 4
    width = cols + B
    here, n_rows = 2048, 544
    dma = pltpu.SemaphoreType.DMA
    vmem = pltpu.VMEM
    both = pl.pallas_call(
        whole_kernel,
        out_shape=jax.ShapeDtypeStruct((64, width), F32),
        in_specs=[VMEM] * 5,
        out_specs=VMEM,
        scratch_shapes=[
            vmem((8, 2, steps.shape[1]), jnp.int32),
            vmem((8, 1, 64), F32),
            vmem((256, 128), F32),
            vmem((16, width), BF16),
            vmem((1, width), F32),
            vmem((n_rows, 16), BF16),
            vmem((n_rows, 128), F32),
            vmem((512, 256), BF16),
            vmem((128, 128), F32),
            *([vmem((BLK, width), BF16)] * 3),
            *([vmem((n_rows, BLK), BF16)] * 3),
            vmem((here, width), BF16),
            vmem((n_rows, here), BF16),
            *([vmem((width // B, n_rows // 2, B), F32)] * 3),
            vmem((16, B), F32),
            vmem((16, cols), F32),
            vmem((NX, 64, B), F32),
            vmem((NX, 64, cols), BF16),
            vmem((64, cols), F32),
            vmem((16, 16, B), F32),
            vmem((16, 16, cols), BF16),
            vmem((NX - 1, 16, B), F32),
            vmem((NX - 1, 16, cols), F32),
            vmem((NX - 1, 64, B), F32),
            vmem((NX - 1, 64, cols), BF16),
            vmem((NX, 1, 64), F32),
            vmem((NX, 1, 64), F32),
            vmem((B, 2 * B), F32),
            vmem((NB, 128), F32),
            *([dma((7,))] * 4), *([dma((5,))] * 2), *([dma((3,))] * 10), dma, dma,
            *([dma((7,))] * 4), *([dma((8,))] * 4),
        ],
        compiler_params=pltpu.CompilerParams(
            collective_id=0, has_side_effects=True, vmem_limit_bytes=60 * 1024 * 1024
        ),
        name="whole",
    )(
        steps,
        harmonic.reshape(-1, 128),
        col_scale.reshape(-1, 128),
        taps.reshape(2, 128),
        ridge.reshape(1, -1),
    )
    return pl.pallas_call(
        split_kernel,
        out_shape=(
            jax.ShapeDtypeStruct((64, B), F32),
            jax.ShapeDtypeStruct((64, cols), F32),
        ),
        in_specs=[VMEM],
        out_specs=(VMEM, VMEM),
        name="split",
    )(both)


def solution(mesh):
    row = P(("epoch", "prow"))
    return jax.shard_map(
        on_device,
        mesh=mesh,
        in_specs=(P(None, "epoch"), P(), P(), P(), row),
        out_specs=(P(("epoch", "prow"), None), P(("epoch", "prow"), "pcol")),
        check_vma=False,
    )
```

```python
import functools

import jax
import jax.numpy as jnp
from jax import lax
from jax.experimental import pallas as pl
from jax.experimental.pallas import tpu as pltpu
from jax.sharding import PartitionSpec as P

F32 = jnp.float32
BF16 = jnp.bfloat16
MESH = pl.DeviceIdType.MESH
HIGH = lax.Precision.HIGHEST
B = 256
BLK = 256
CHUNK = 64
PERIOD = 4096
NX = 4
WAVE = (8.88573567404434, -58.45953046181323, 115.03267724691959, -100.39492606524867)
ROUND = 12582912.0
VMEM = pl.BlockSpec(memory_space=pltpu.VMEM)


def place():
    e, p, y = (lax.axis_index(a) for a in ("epoch", "prow", "pcol"))
    core, z_lo = e % 2, e // 2
    x, z_hi = p % NX, p // NX
    return x, y, z_hi * 4 + z_lo, core


def device(x, z, core):
    return {"epoch": (z % 4) * 2 + core, "prow": (z // 4) * NX + x}


def wave(turn, scale):
    whole = (turn + ROUND) - ROUND
    z = 0.25 - jnp.abs(turn - whole)
    s = z * z
    poly = s + WAVE[2] / WAVE[3]
    for c in (WAVE[1], WAVE[0]):
        poly = poly * s + c / WAVE[3]
    return poly * (z * scale)


def halves(v):
    hi = jnp.floor(v * 64.0) * (1.0 / 64.0)
    return hi, v - hi


def dot(a, b, dims=((1,), (0,))):
    return lax.dot_general(a, b, (dims, ((), ())), precision=HIGH, preferred_element_type=F32)


def split3(v):
    hi = v.astype(BF16)
    v = v - hi.astype(F32)
    mid = v.astype(BF16)
    low = (v - mid.astype(F32)).astype(BF16)
    return hi, mid, low


NB = 32


def block_inverse(a):
    groups = NB // 8
    full = (8, 128)
    sub = lax.broadcasted_iota(jnp.int32, full, 0)
    lane = lax.broadcasted_iota(jnp.int32, full, 1)

    def spread(v, s):
        return jnp.broadcast_to(v[s : s + 1, :], full)

    col = [
        {k: jnp.broadcast_to(a[8 * k : 8 * k + 8, c : c + 1], full) for k in range(c // 8, groups)}
        for c in range(NB)
    ]
    inv = [jnp.where(lane == sub + 8 * k, 1.0, 0.0).astype(F32) for k in range(groups)]
    root = [jnp.zeros(full, F32) for _ in range(groups)]
    for i in range(NB):
        k0, s = divmod(i, 8)
        pivot = spread(col[i][k0], s)
        over = 1.0 / pivot
        root[k0] = jnp.where(sub == s, lax.rsqrt(pivot), root[k0])
        ratio = {k: col[i][k] * over for k in range(k0, groups)}
        ratio[k0] = jnp.where(sub > s, ratio[k0], 0.0)
        for c in range(i + 1, NB):
            kc, sc = divmod(c, 8)
            top = spread(col[i][kc], sc)
            for k in range(kc, groups):
                col[c][k] = col[c][k] - ratio[k] * top
        top = spread(inv[k0], s)
        for k in range(k0, groups):
            inv[k] = inv[k] - ratio[k] * top
    return jnp.concatenate([inv[k] * root[k] for k in range(groups)], axis=0)


def whole_kernel(
    steps_ref, harm_ref, scale_ref, taps_ref, ridge_ref, out_ref,
    every, every_ridge, phase_ref,
    colf, cols_s, rowf, rows_s, lowt, lowr, d0, d1, d2, e0, e1, e2, fcol, frow, mine, theirs, got_p, lead_own, lead_out, lead_in,
    la_ref, lb_ref, oa_ref, ob_ref, oc_ref,
    slab_a, slab_b, got_la, got_lb, got_oa, got_ob, ridge4, ridge_far, mat, nxt_ref,
    s_st, r_st, s_ri, r_ri, s_p, r_p, s_l, r_l,
    s_la, r_la, s_lb, r_lb, s_oa, r_oa, s_ob, r_ob, s_r, r_r, s_f, r_f,
    s_za, r_za, s_zb, r_zb, s_ca, r_ca, s_cb, r_cb,
):
    x, y, z, core = place()
    e, p = lax.axis_index("epoch"), lax.axis_index("prow")
    nz, ne = 8, 8

    def group(zz, cc):
        return ((zz % 4) * 2 + cc) * 2 + zz // 4

    g = group(z, core)
    peers = [device((x + i) % NX, z, core) for i in range(1, NX)]
    tall = [device(x, (z + i) % nz, core) for i in range(1, nz)]
    ring = [{"epoch": (e + i) % ne} for i in range(1, ne)]
    across = [device(x, (1 - z // 4) * 4 + i, core) for i in range(4)]
    other = device(x, z, 1 - core)
    barrier = pltpu.get_barrier_semaphore()
    greeted = ring + peers + across
    for peer in greeted:
        pl.semaphore_signal(barrier, inc=1, device_id=peer, device_id_type=MESH)
    pl.semaphore_wait(barrier, len(greeted))

    def put(src, dst, send, recv, peer):
        copy = pltpu.make_async_remote_copy(
            src_ref=src, dst_ref=dst, send_sem=send, recv_sem=recv,
            device_id=peer, device_id_type=MESH,
        )
        copy.start()
        return copy

    def to_x(src, got, send, recv):
        return [put(src(i), got.at[i - 1], send.at[i - 1], recv.at[i - 1], peers[i - 1]) for i in range(1, NX)]

    def to_z(slab, send, recv):
        return [put(slab.at[g], slab.at[g], send.at[i - 1], recv.at[i - 1], tall[i - 1]) for i in range(1, nz)]

    def to_core(slab, send, recv, i):
        k = group((z + nz - i) % nz, core)
        return put(slab.at[k], slab.at[k], send.at[i], recv.at[i], other)

    given = [
        put(steps_ref, every.at[e], s_st.at[i], r_st.at[i], ring[i]) for i in range(ne - 1)
    ] + [
        put(ridge_ref, every_ridge.at[e], s_ri.at[i], r_ri.at[i], ring[i]) for i in range(ne - 1)
    ]
    every[e] = steps_ref[...]
    every_ridge[e] = ridge_ref[...]
    blocks = (ne * steps_ref.shape[1] // BLK) // (2 * NX)
    n_rows = rows_s.shape[0]
    n_lead = (n_rows - 2 * B) // 2
    n_tiles = colf.shape[1] // 128
    cols_here = n_tiles - 2
    dcol, drow = (d0, d1, d2), (e0, e1, e2)

    def features(k):
        h = harm_ref[pl.ds(k, 1), :]
        order = lax.shift_right_logical(h, 6).astype(F32)
        degree = (h & 63).astype(F32)
        shift = jnp.full((1, 128), -0.125, F32)
        rows = jnp.concatenate(
            [order, order, degree, degree, shift, jnp.zeros((11, 128), F32)], axis=0
        )
        return rows, scale_ref[pl.ds(k, 1), :] * WAVE[3]

    def down(row):
        return jnp.transpose(jnp.broadcast_to(row, (128, 128)))

    for jt in range(n_tiles):
        k = jt if jt < 2 else y * cols_here + (jt - 2)
        rows, scale = features(k)
        colf[:, jt * 128 : jt * 128 + 128] = rows.astype(BF16)
        cols_s[:, jt * 128 : jt * 128 + 128] = scale
    per = 128 // n_lead
    for side, gg in enumerate((group(z, 1 - core), g)):
        top = 2 * n_lead + side * B
        for half in range(2):
            rows, scale = features(gg * 2 + half)
            at = slice(top + half * 128, top + half * 128 + 128)
            rowf[at, :] = jnp.transpose(rows).astype(BF16)
            rows_s[at, :] = down(scale)
        rows, scale = features(gg // per)
        piece = pl.ds(pl.multiple_of((gg % per) * n_lead, n_lead), n_lead)
        at = slice(side * n_lead, side * n_lead + n_lead)
        lowr[...] = down(scale)
        rows_s[at, :] = lowr[piece, :]
        lowr[:, 0:16] = jnp.transpose(rows)
        rowf[at, :] = lowr[piece, 0:16].astype(BF16)

    base = jnp.concatenate([taps_ref[0:1, :], taps_ref[1:2, :], jnp.zeros((1, 256), F32)], axis=1)
    full = pltpu.roll(
        jnp.broadcast_to(base, (512, 512)), 256, 1, stride=1, stride_axis=0
    )[:, :256]
    lowt[...] = full.astype(BF16)
    low_up = jnp.transpose(full).astype(BF16)


    pairs = 2 * ne
    rows = pairs * steps_ref.shape[1] // 128
    upper = (
        lax.broadcasted_iota(jnp.int32, (128, 128), 0)
        <= lax.broadcasted_iota(jnp.int32, (128, 128), 1)
    ).astype(BF16)
    r_at = lax.broadcasted_iota(jnp.int32, (rows, rows), 0)
    s_at = lax.broadcasted_iota(jnp.int32, (rows, rows), 1)
    same = r_at % 2 == s_at % 2
    key_r = ((r_at % pairs) // 2) * rows + r_at // pairs
    key_s = ((s_at % pairs) // 2) * rows + s_at // pairs
    before = jnp.where(same & (key_s < key_r), 1.0, 0.0).astype(BF16)
    for copy in given:
        copy.wait()
    flat = every[...].astype(F32).reshape(pairs, steps_ref.shape[1])
    stack = jnp.concatenate(
        [flat[:, 128 * k : 128 * k + 128] for k in range(rows // pairs)], axis=0
    )
    inside = jnp.dot(stack.astype(BF16), upper, preferred_element_type=F32)
    totals = jnp.broadcast_to(inside[:, 127:128], (rows, 128))
    high = jnp.floor(totals * (1.0 / 64.0))
    low = totals - high * 64.0
    earlier = jnp.dot(before, high.astype(BF16), preferred_element_type=F32) * 64.0
    earlier = earlier + jnp.dot(before, low.astype(BF16), preferred_element_type=F32)
    turns = (inside + earlier) * (1.0 / PERIOD)
    phase_ref[...] = turns - jnp.floor(turns)

    def phases_of(b):
        at = jnp.maximum((x * 2 + core) * blocks + b - 1, 0)
        row0 = (at % 8) * 32 + (at // 8) * 2
        parts = []
        for a in range(2):
            q = jnp.concatenate(
                [phase_ref[pl.ds(row0 + 16 * half + a, 1), :] for half in range(2)], axis=1
            )
            parts += list(halves(q))
        parts += [jnp.ones((1, BLK), F32), jnp.zeros((11, BLK), F32)]
        rows = jnp.concatenate(parts, axis=0)
        return rows.astype(BF16), jnp.transpose(rows).astype(BF16)

    def design(qt, slot, j0):
        scale = cols_s[:, j0 : j0 + 256]
        for r0 in range(0, BLK, CHUNK):
            turn = jnp.dot(
                qt[r0 : r0 + CHUNK, :], colf[:, j0 : j0 + 256], preferred_element_type=F32
            )
            dcol[slot][r0 : r0 + CHUNK, j0 : j0 + 256] = wave(turn, scale).astype(BF16)

    def design_rows(qf, slot):
        for r0 in range(0, n_rows, CHUNK):
            r1 = min(r0 + CHUNK, n_rows)
            turn = jnp.dot(rowf[r0:r1, :], qf, preferred_element_type=F32)
            scale = rows_s[r0:r1, :]
            d = wave(turn, jnp.concatenate([scale, scale], axis=1))
            drow[slot][r0:r1, :] = d.astype(BF16)

    def filter_cols(b, s0, s1, j0):
        both = jnp.concatenate(
            [dcol[s0][:, j0 : j0 + 256], dcol[s1][:, j0 : j0 + 256]], axis=0
        )
        f = jnp.dot(low_up, both, preferred_element_type=F32).astype(BF16)
        fcol[pl.ds(pl.multiple_of(b * BLK, BLK), BLK), j0 : j0 + 256] = f

    def filter_rows(b, s0, s1):
        both = jnp.concatenate([drow[s0][...], drow[s1][...]], axis=1)
        f = jnp.dot(both, lowt[...], preferred_element_type=F32).astype(BF16)
        frow[:, pl.ds(pl.multiple_of(b * BLK, BLK), BLK)] = f

    wide = range(0, n_tiles * 128, 256)
    for b in range(2):
        qf, qt = phases_of(b)
        for j0 in wide:
            design(qt, b, j0)
        design_rows(qf, b)

    @pl.when((x == 0) & (core == 0))
    def _():
        d0[...] = jnp.zeros_like(d0)
        e0[...] = jnp.zeros_like(e0)

    def block_pass(b, s, more):
        if more:
            qf, qt = phases_of(b + 2)
        for j0 in wide:
            filter_cols(b, s, (s + 1) % 3, j0)
            if more:
                design(qt, (s + 2) % 3, j0)
        filter_rows(b, s, (s + 1) % 3)
        if more:
            design_rows(qf, (s + 2) % 3)

    trips = (blocks - 1) // 3

    @pl.loop(0, trips)
    def _(step):
        for s in range(3):
            block_pass(step * 3 + s, s, True)

    for b in range(trips * 3, blocks):
        block_pass(b, b % 3, b + 2 <= blocks)

    total = 1.0 / (blocks * BLK * 2 * NX)
    leads, swaps = [], []

    def product(j):
        at = slice(j * B, j * B + B)
        part = jnp.dot(frow[...], fcol[:, at], preferred_element_type=F32) * total
        lead_out[j] = part[:n_lead]
        leads.append(put(lead_out.at[j], lead_in.at[j], s_l.at[j], r_l.at[j], other))
        lead_own[j] = part[n_lead : 2 * n_lead]
        theirs[j] = part[2 * n_lead : 2 * n_lead + B]
        swaps.append(put(theirs.at[j], got_p.at[j], s_p.at[j], r_p.at[j], other))
        mine[j] = part[2 * n_lead + B :]

    own_piece = pl.ds(pl.multiple_of(x * 64, 64), 64)

    def settle(j):
        swaps[j].wait()
        part = mine[j] + got_p[j]
        if j == 0:
            oa_ref[...] = part.reshape(NX, 64, B)
            return
        at = slice(j * B - B, j * B)
        ob_ref[:, :, at] = part.astype(BF16).reshape(NX, 64, B)
        oc_ref[:, at] = mine[j, own_piece, :] + got_p[j, own_piece, :]

    product(0)
    product(1)
    leads[0].wait()
    la_ref[...] = lead_own[0] + lead_in[0]
    lead_a = to_x(lambda i: la_ref, got_la, s_la, r_la)
    ridge4[x] = every_ridge[0]
    ridges = [
        put(every_ridge.at[0], ridge4.at[x], s_r.at[i - 1], r_r.at[i - 1], peers[i - 1])
        for i in range(1, NX)
    ]
    for j in range(2, n_tiles // 2):
        product(j)
    for j in range(1, n_tiles // 2):
        leads[j].wait()
        lb_ref[:, j * B - B : j * B] = lead_own[j] + lead_in[j]
    lead_b = to_x(lambda i: lb_ref, got_lb, s_lb, r_lb)
    settle(0)
    settle(1)
    for copy in lead_a:
        copy.wait()
    slab_a[g] = la_ref[...] + got_la[0] + got_la[1] + got_la[2]
    z_a = to_z(slab_a, s_za, r_za)
    c_a = [to_core(slab_a, s_ca, r_ca, 0)]
    for copy in ridges:
        copy.wait()
    far = put(ridge4, ridge_far, s_f, r_f, device(x, (z + 4) % nz, core))
    for j in range(2, n_tiles // 2):
        settle(j)
    own_a = to_x(lambda i: oa_ref.at[(x + i) % NX], got_oa, s_oa, r_oa)
    own_b = to_x(lambda i: ob_ref.at[(x + i) % NX], got_ob, s_ob, r_ob)
    for copy in lead_b:
        copy.wait()
    slab_b[g] = (lb_ref[...] + got_lb[0] + got_lb[1] + got_lb[2]).astype(BF16)
    z_b = to_z(slab_b, s_zb, r_zb)
    c_b = [to_core(slab_b, s_cb, r_cb, 0)]
    for i in range(1, nz):
        z_a[i - 1].wait()
        c_a.append(to_core(slab_a, s_ca, r_ca, i))
    far.wait()
    for copy in c_a:
        copy.wait()

    lane = lax.broadcasted_iota(jnp.int32, (64, B), 1)
    sub = lax.broadcasted_iota(jnp.int32, (64, B), 0)

    def column(row):
        return jnp.transpose(jnp.broadcast_to(row, (128, 64)))[:, 0:1]

    lead_ridge = [column(jnp.where(z < 4, ridge4[k], ridge_far[k])) for k in range(4)]
    for k in range(4):
        rows = slab_a[4 * k : 4 * k + 4].reshape(64, B)
        mat[64 * k : 64 * k + 64, 0:B] = rows + jnp.where(lane == sub + 64 * k, lead_ridge[k], 0.0)
        mat[64 * k : 64 * k + 64, B:] = jnp.where(lane == sub + 64 * k, 1.0, 0.0).astype(F32)

    nxt_ref[...] = mat[0:NB, 0:128]
    wide = lax.broadcasted_iota(jnp.int32, (NB, B), 1)

    def block_step(j, carry):
        r0 = pl.multiple_of(j * NB, NB)
        r1 = r0 + NB
        w = block_inverse(nxt_ref[:, 0:NB])[:, 0:NB]
        rj = dot(w, mat[pl.ds(r0, NB), :])
        mat[pl.ds(r0, NB), :] = rj
        hi, mid, low = split3(rj)
        right = jnp.concatenate([hi, mid, hi, low, hi, mid], axis=0)
        hi, mid, low = split3(jnp.where(wide >= r1, rj[:, 0:B], 0.0))
        left = jnp.concatenate([hi, hi, mid, hi, low, mid], axis=0)
        mat[...] -= lax.dot_general(
            left, right, (((0,), (0,)), ((), ())), preferred_element_type=F32
        )
        r1 = pl.multiple_of(jnp.minimum(r1, B - NB), NB)
        nxt_ref[...] = pltpu.roll(mat[pl.ds(r1, NB), 0:B], B - r1, 1)[:, 0:128]
        return carry

    blocks_a = B // NB
    early = blocks_a * 3 // 4
    lax.fori_loop(0, early, block_step, 0)
    for i in range(1, nz):
        z_b[i - 1].wait()
        c_b.append(to_core(slab_b, s_cb, r_cb, i))
    lax.fori_loop(early, blocks_a, block_step, 0)

    for copy in own_a:
        copy.wait()
    first = (e * 8 + p) * 64
    own_ridge = column(ridge_ref[...])
    winv = mat[:, B:]
    lead = oa_ref[x] + got_oa[0] + got_oa[1] + got_oa[2]
    lead = lead + jnp.where(lane == sub + first, own_ridge, 0.0)
    panel = dot(lead, winv, ((1,), (1,)))
    weight = dot(panel, winv)
    parts = jnp.concatenate(split3(weight), axis=0)
    out_ref[:, 0:B] = panel
    for copy in c_b:
        copy.wait()
    for copy in own_b:
        copy.wait()
    cols = lb_ref.shape[1]
    for j0 in range(0, cols, B):
        three = jnp.dot(
            parts, slab_b[:, :, j0 : j0 + B].reshape(B, B), preferred_element_type=F32
        )
        known = three[0:64] + three[64:128] + three[128:192]
        if j0 == 0:
            exact = [
                slab_a[4 * k : 4 * k + 4].reshape(64, B)
                + jnp.where(lane == sub + 64 * k, lead_ridge[k], 0.0)
                for k in range(4)
            ]
            known = jnp.where(y == 0, dot(weight, jnp.concatenate(exact, axis=0)), known)
        at = slice(j0, j0 + B)
        tile = oc_ref[:, at] + got_ob[0, :, at].astype(F32)
        tile = tile + got_ob[1, :, at].astype(F32) + got_ob[2, :, at].astype(F32)
        tile = tile + jnp.where(lane + (y * cols + j0) == sub + first, own_ridge, 0.0)
        out_ref[:, B + j0 : B + j0 + B] = tile - known


def split_kernel(both_ref, panel_ref, schur_ref):
    panel_ref[...] = both_ref[:, 0:B]
    schur_ref[...] = both_ref[:, B:]


def on_device(steps, harmonic, col_scale, taps, ridge):
    cols = harmonic.shape[0] // 4
    width = cols + B
    here, n_rows = 2048, 544
    dma = pltpu.SemaphoreType.DMA
    vmem = pltpu.VMEM
    both = pl.pallas_call(
        whole_kernel,
        out_shape=jax.ShapeDtypeStruct((64, width), F32),
        in_specs=[VMEM] * 5,
        out_specs=VMEM,
        scratch_shapes=[
            vmem((8, 2, steps.shape[1]), jnp.int32),
            vmem((8, 1, 64), F32),
            vmem((256, 128), F32),
            vmem((16, width), BF16),
            vmem((1, width), F32),
            vmem((n_rows, 16), BF16),
            vmem((n_rows, 128), F32),
            vmem((512, 256), BF16),
            vmem((128, 128), F32),
            *([vmem((BLK, width), BF16)] * 3),
            *([vmem((n_rows, BLK), BF16)] * 3),
            vmem((here, width), BF16),
            vmem((n_rows, here), BF16),
            *([vmem((width // B, B, B), F32)] * 3),
            *([vmem((width // B, 16, B), F32)] * 3),
            vmem((16, B), F32),
            vmem((16, cols), F32),
            vmem((NX, 64, B), F32),
            vmem((NX, 64, cols), BF16),
            vmem((64, cols), F32),
            vmem((16, 16, B), F32),
            vmem((16, 16, cols), BF16),
            vmem((NX - 1, 16, B), F32),
            vmem((NX - 1, 16, cols), F32),
            vmem((NX - 1, 64, B), F32),
            vmem((NX - 1, 64, cols), BF16),
            vmem((NX, 1, 64), F32),
            vmem((NX, 1, 64), F32),
            vmem((B, 2 * B), F32),
            vmem((NB, 128), F32),
            *([dma((7,))] * 4), *([dma((5,))] * 4), *([dma((3,))] * 10), dma, dma,
            *([dma((7,))] * 4), *([dma((8,))] * 4),
        ],
        compiler_params=pltpu.CompilerParams(
            collective_id=0, has_side_effects=True, vmem_limit_bytes=60 * 1024 * 1024
        ),
        name="whole",
    )(
        steps,
        harmonic.reshape(-1, 128),
        col_scale.reshape(-1, 128),
        taps.reshape(2, 128),
        ridge.reshape(1, -1),
    )
    return pl.pallas_call(
        split_kernel,
        out_shape=(
            jax.ShapeDtypeStruct((64, B), F32),
            jax.ShapeDtypeStruct((64, cols), F32),
        ),
        in_specs=[VMEM],
        out_specs=(VMEM, VMEM),
        name="split",
    )(both)


def solution(mesh):
    row = P(("epoch", "prow"))
    return jax.shard_map(
        on_device,
        mesh=mesh,
        in_specs=(P(None, "epoch"), P(), P(), P(), row),
        out_specs=(P(("epoch", "prow"), None), P(("epoch", "prow"), "pcol")),
        check_vma=False,
    )
```

```python
import functools

import jax
import jax.numpy as jnp
from jax import lax
from jax.experimental import pallas as pl
from jax.experimental.pallas import tpu as pltpu
from jax.sharding import PartitionSpec as P

F32 = jnp.float32
BF16 = jnp.bfloat16
MESH = pl.DeviceIdType.MESH
HIGH = lax.Precision.HIGHEST
B = 256
BLK = 256
CHUNK = 64
PERIOD = 4096
NX = 4
WAVE = (8.88573567404434, -58.45953046181323, 115.03267724691959, -100.39492606524867)
ROUND = 12582912.0
VMEM = pl.BlockSpec(memory_space=pltpu.VMEM)


def place():
    e, p, y = (lax.axis_index(a) for a in ("epoch", "prow", "pcol"))
    core, z_lo = e % 2, e // 2
    x, z_hi = p % NX, p // NX
    return x, y, z_hi * 4 + z_lo, core


def device(x, z, core):
    return {"epoch": (z % 4) * 2 + core, "prow": (z // 4) * NX + x}


def wave(turn, scale):
    whole = (turn + ROUND) - ROUND
    z = 0.25 - jnp.abs(turn - whole)
    s = z * z
    poly = s + WAVE[2] / WAVE[3]
    for c in (WAVE[1], WAVE[0]):
        poly = poly * s + c / WAVE[3]
    return poly * (z * scale)


def halves(v):
    hi = jnp.floor(v * 64.0) * (1.0 / 64.0)
    return hi, v - hi


def dot(a, b, dims=((1,), (0,))):
    return lax.dot_general(a, b, (dims, ((), ())), precision=HIGH, preferred_element_type=F32)


def split3(v):
    hi = v.astype(BF16)
    v = v - hi.astype(F32)
    mid = v.astype(BF16)
    low = (v - mid.astype(F32)).astype(BF16)
    return hi, mid, low


NB = 32


def block_inverse(a, off):
    groups = NB // 8
    full = (8, 128)
    sub = lax.broadcasted_iota(jnp.int32, full, 0)
    lane = lax.broadcasted_iota(jnp.int32, full, 1)

    def spread(v, s):
        return jnp.broadcast_to(v[s : s + 1, :], full)

    col = [
        {k: jnp.broadcast_to(a[8 * k : 8 * k + 8, off + c : off + c + 1], full) for k in range(c // 8, groups)}
        for c in range(NB)
    ]
    inv = [jnp.where(lane == sub + 8 * k, 1.0, 0.0).astype(F32) for k in range(groups)]
    root = [jnp.zeros(full, F32) for _ in range(groups)]
    for i in range(NB):
        k0, s = divmod(i, 8)
        pivot = spread(col[i][k0], s)
        over = 1.0 / pivot
        root[k0] = jnp.where(sub == s, lax.rsqrt(pivot), root[k0])
        ratio = {k: col[i][k] * over for k in range(k0, groups)}
        ratio[k0] = jnp.where(sub > s, ratio[k0], 0.0)
        for c in range(i + 1, NB):
            kc, sc = divmod(c, 8)
            top = spread(col[i][kc], sc)
            for k in range(kc, groups):
                col[c][k] = col[c][k] - ratio[k] * top
        top = spread(inv[k0], s)
        for k in range(k0, groups):
            inv[k] = inv[k] - ratio[k] * top
    return jnp.concatenate([inv[k] * root[k] for k in range(groups)], axis=0)


def whole_kernel(
    steps_ref, harm_ref, scale_ref, taps_ref, ridge_ref, out_ref,
    every, every_ridge, steps_out, phase_ref,
    colf, cols_s, rowf, rows_s, lowt, lowr, d0, d1, d2, e0, e1, e2, fcol, frow, mine, theirs, got_p, lead_own, lead_out, lead_in,
    la_ref, lb_ref, oa_ref, ob_ref, oc_ref,
    slab_a, slab_b, got_la, got_lb, got_oa, got_ob, ridge4, ridge_far, mat,
    s_st, r_st, s_ri, r_ri, s_p, r_p, s_l, r_l,
    s_la, r_la, s_lb, r_lb, s_oa, r_oa, s_ob, r_ob, s_r, r_r, s_f, r_f,
    s_za, r_za, s_zb, r_zb, s_ca, r_ca, s_cb, r_cb,
):
    x, y, z, core = place()
    e, p = lax.axis_index("epoch"), lax.axis_index("prow")
    nz, ne = 8, 8

    def group(zz, cc):
        return ((zz % 4) * 2 + cc) * 2 + zz // 4

    g = group(z, core)
    peers = [device((x + i) % NX, z, core) for i in range(1, NX)]
    tall = [device(x, (z + i) % nz, core) for i in range(1, nz)]
    ring = [{"epoch": (e + i) % ne} for i in range(1, ne)]
    across = [device(x, (1 - z // 4) * 4 + i, core) for i in range(4)]
    other = device(x, z, 1 - core)
    barrier = pltpu.get_barrier_semaphore()
    greeted = ring + peers + across
    for peer in greeted:
        pl.semaphore_signal(barrier, inc=1, device_id=peer, device_id_type=MESH)
    pl.semaphore_wait(barrier, len(greeted))

    def put(src, dst, send, recv, peer):
        copy = pltpu.make_async_remote_copy(
            src_ref=src, dst_ref=dst, send_sem=send, recv_sem=recv,
            device_id=peer, device_id_type=MESH,
        )
        copy.start()
        return copy

    def to_x(src, got, send, recv):
        return [put(src(i), got.at[i - 1], send.at[i - 1], recv.at[i - 1], peers[i - 1]) for i in range(1, NX)]

    def to_z(slab, send, recv):
        return [put(slab.at[g], slab.at[g], send.at[i - 1], recv.at[i - 1], tall[i - 1]) for i in range(1, nz)]

    def to_core(slab, send, recv, i):
        k = group((z + nz - i) % nz, core)
        return put(slab.at[k], slab.at[k], send.at[i], recv.at[i], other)

    steps_out[...] = steps_ref[...].astype(F32).astype(BF16)
    given = [
        put(steps_out, every.at[e], s_st.at[i], r_st.at[i], ring[i]) for i in range(ne - 1)
    ] + [
        put(ridge_ref, every_ridge.at[e], s_ri.at[i], r_ri.at[i], ring[i]) for i in range(ne - 1)
    ]
    every[e] = steps_out[...]
    every_ridge[e] = ridge_ref[...]
    blocks = (ne * steps_ref.shape[1] // BLK) // (2 * NX)
    n_rows = rows_s.shape[0]
    n_lead = (n_rows - 2 * B) // 2
    n_tiles = colf.shape[1] // 128
    cols_here = n_tiles - 2
    dcol, drow = (d0, d1, d2), (e0, e1, e2)

    def features(k):
        h = harm_ref[pl.ds(k, 1), :]
        order = lax.shift_right_logical(h, 6).astype(F32)
        degree = (h & 63).astype(F32)
        shift = jnp.full((1, 128), -0.125, F32)
        rows = jnp.concatenate(
            [order, order, degree, degree, shift, jnp.zeros((11, 128), F32)], axis=0
        )
        return rows, scale_ref[pl.ds(k, 1), :] * WAVE[3]

    def down(row):
        return jnp.transpose(jnp.broadcast_to(row, (128, 128)))

    for jt in range(n_tiles):
        k = jt if jt < 2 else y * cols_here + (jt - 2)
        rows, scale = features(k)
        colf[:, jt * 128 : jt * 128 + 128] = rows.astype(BF16)
        cols_s[:, jt * 128 : jt * 128 + 128] = scale
    per = 128 // n_lead
    for side, gg in enumerate((group(z, 1 - core), g)):
        top = 2 * n_lead + side * B
        for half in range(2):
            rows, scale = features(gg * 2 + half)
            at = slice(top + half * 128, top + half * 128 + 128)
            rowf[at, :] = jnp.transpose(rows).astype(BF16)
            rows_s[at, :] = down(scale)
        rows, scale = features(gg // per)
        piece = pl.ds(pl.multiple_of((gg % per) * n_lead, n_lead), n_lead)
        at = slice(side * n_lead, side * n_lead + n_lead)
        lowr[...] = down(scale)
        rows_s[at, :] = lowr[piece, :]
        lowr[:, 0:16] = jnp.transpose(rows)
        rowf[at, :] = lowr[piece, 0:16].astype(BF16)

    base = jnp.concatenate([taps_ref[0:1, :], taps_ref[1:2, :], jnp.zeros((1, 256), F32)], axis=1)
    full = pltpu.roll(
        jnp.broadcast_to(base, (512, 512)), 256, 1, stride=1, stride_axis=0
    )[:, :256]
    lowt[...] = full.astype(BF16)
    low_up = jnp.transpose(full).astype(BF16)


    pairs = 2 * ne
    rows = pairs * steps_ref.shape[1] // 128
    upper = (
        lax.broadcasted_iota(jnp.int32, (128, 128), 0)
        <= lax.broadcasted_iota(jnp.int32, (128, 128), 1)
    ).astype(BF16)
    r_at = lax.broadcasted_iota(jnp.int32, (rows, rows), 0)
    s_at = lax.broadcasted_iota(jnp.int32, (rows, rows), 1)
    same = r_at % 2 == s_at % 2
    key_r = ((r_at % pairs) // 2) * rows + r_at // pairs
    key_s = ((s_at % pairs) // 2) * rows + s_at // pairs
    before = jnp.where(same & (key_s < key_r), 1.0, 0.0).astype(BF16)
    for copy in given:
        copy.wait()
    flat = every[...].astype(F32).reshape(pairs, steps_ref.shape[1])
    stack = jnp.concatenate(
        [flat[:, 128 * k : 128 * k + 128] for k in range(rows // pairs)], axis=0
    )
    inside = jnp.dot(stack.astype(BF16), upper, preferred_element_type=F32)
    totals = jnp.broadcast_to(inside[:, 127:128], (rows, 128))
    high = jnp.floor(totals * (1.0 / 64.0))
    low = totals - high * 64.0
    earlier = jnp.dot(before, high.astype(BF16), preferred_element_type=F32) * 64.0
    earlier = earlier + jnp.dot(before, low.astype(BF16), preferred_element_type=F32)
    turns = (inside + earlier) * (1.0 / PERIOD)
    phase_ref[...] = turns - jnp.floor(turns)

    def phases_of(b):
        at = jnp.maximum((x * 2 + core) * blocks + b - 1, 0)
        row0 = (at % 8) * 32 + (at // 8) * 2
        parts = []
        for a in range(2):
            q = jnp.concatenate(
                [phase_ref[pl.ds(row0 + 16 * half + a, 1), :] for half in range(2)], axis=1
            )
            parts += list(halves(q))
        parts += [jnp.ones((1, BLK), F32), jnp.zeros((11, BLK), F32)]
        rows = jnp.concatenate(parts, axis=0)
        return rows.astype(BF16), jnp.transpose(rows).astype(BF16)

    def design(qt, slot, j0):
        scale = cols_s[:, j0 : j0 + 256]
        for r0 in range(0, BLK, CHUNK):
            turn = jnp.dot(
                qt[r0 : r0 + CHUNK, :], colf[:, j0 : j0 + 256], preferred_element_type=F32
            )
            dcol[slot][r0 : r0 + CHUNK, j0 : j0 + 256] = wave(turn, scale).astype(BF16)

    def design_rows(qf, slot):
        for r0 in range(0, n_rows, CHUNK):
            r1 = min(r0 + CHUNK, n_rows)
            turn = jnp.dot(rowf[r0:r1, :], qf, preferred_element_type=F32)
            scale = rows_s[r0:r1, :]
            d = wave(turn, jnp.concatenate([scale, scale], axis=1))
            drow[slot][r0:r1, :] = d.astype(BF16)

    def filter_cols(b, s0, s1, j0):
        both = jnp.concatenate(
            [dcol[s0][:, j0 : j0 + 256], dcol[s1][:, j0 : j0 + 256]], axis=0
        )
        f = jnp.dot(low_up, both, preferred_element_type=F32).astype(BF16)
        fcol[pl.ds(pl.multiple_of(b * BLK, BLK), BLK), j0 : j0 + 256] = f

    def filter_rows(b, s0, s1):
        both = jnp.concatenate([drow[s0][...], drow[s1][...]], axis=1)
        f = jnp.dot(both, lowt[...], preferred_element_type=F32).astype(BF16)
        frow[:, pl.ds(pl.multiple_of(b * BLK, BLK), BLK)] = f

    wide = range(0, n_tiles * 128, 256)
    for b in range(2):
        qf, qt = phases_of(b)
        for j0 in wide:
            design(qt, b, j0)
        design_rows(qf, b)

    @pl.when((x == 0) & (core == 0))
    def _():
        d0[...] = jnp.zeros_like(d0)
        e0[...] = jnp.zeros_like(e0)

    def block_pass(b, s, more):
        if more:
            qf, qt = phases_of(b + 2)
        for j0 in wide:
            filter_cols(b, s, (s + 1) % 3, j0)
            if more:
                design(qt, (s + 2) % 3, j0)
        filter_rows(b, s, (s + 1) % 3)
        if more:
            design_rows(qf, (s + 2) % 3)

    trips = (blocks - 1) // 3

    @pl.loop(0, trips)
    def _(step):
        for s in range(3):
            block_pass(step * 3 + s, s, True)

    for b in range(trips * 3, blocks):
        block_pass(b, b % 3, b + 2 <= blocks)

    total = 1.0 / (blocks * BLK * 2 * NX)
    leads, swaps = [], []

    def product(j):
        at = slice(j * B, j * B + B)
        part = jnp.dot(frow[...], fcol[:, at], preferred_element_type=F32) * total
        lead_out[j] = part[:n_lead]
        leads.append(put(lead_out.at[j], lead_in.at[j], s_l.at[j], r_l.at[j], other))
        lead_own[j] = part[n_lead : 2 * n_lead]
        theirs[j] = part[2 * n_lead : 2 * n_lead + B]
        swaps.append(put(theirs.at[j], got_p.at[j], s_p.at[j], r_p.at[j], other))
        mine[j] = part[2 * n_lead + B :]

    own_piece = pl.ds(pl.multiple_of(x * 64, 64), 64)

    def settle(j):
        swaps[j].wait()
        part = mine[j] + got_p[j]
        if j == 0:
            oa_ref[...] = part.reshape(NX, 64, B)
            return
        at = slice(j * B - B, j * B)
        ob_ref[:, :, at] = part.astype(BF16).reshape(NX, 64, B)
        oc_ref[:, at] = mine[j, own_piece, :] + got_p[j, own_piece, :]

    product(0)
    product(1)
    leads[0].wait()
    la_ref[...] = lead_own[0] + lead_in[0]
    lead_a = to_x(lambda i: la_ref, got_la, s_la, r_la)
    ridge4[x] = every_ridge[0]
    ridges = [
        put(every_ridge.at[0], ridge4.at[x], s_r.at[i - 1], r_r.at[i - 1], peers[i - 1])
        for i in range(1, NX)
    ]
    for j in range(2, n_tiles // 2):
        product(j)
    for j in range(1, n_tiles // 2):
        leads[j].wait()
        lb_ref[:, j * B - B : j * B] = lead_own[j] + lead_in[j]
    lead_b = to_x(lambda i: lb_ref, got_lb, s_lb, r_lb)
    settle(0)
    settle(1)
    for copy in lead_a:
        copy.wait()
    slab_a[g] = la_ref[...] + got_la[0] + got_la[1] + got_la[2]
    z_a = to_z(slab_a, s_za, r_za)
    c_a = [to_core(slab_a, s_ca, r_ca, 0)]
    for copy in ridges:
        copy.wait()
    far = put(ridge4, ridge_far, s_f, r_f, device(x, (z + 4) % nz, core))
    for j in range(2, n_tiles // 2):
        settle(j)
    own_a = to_x(lambda i: oa_ref.at[(x + i) % NX], got_oa, s_oa, r_oa)
    own_b = to_x(lambda i: ob_ref.at[(x + i) % NX], got_ob, s_ob, r_ob)
    for copy in lead_b:
        copy.wait()
    slab_b[g] = (lb_ref[...] + got_lb[0] + got_lb[1] + got_lb[2]).astype(BF16)
    z_b = to_z(slab_b, s_zb, r_zb)
    c_b = [to_core(slab_b, s_cb, r_cb, 0)]
    for i in range(1, nz):
        z_a[i - 1].wait()
        c_a.append(to_core(slab_a, s_ca, r_ca, i))
    far.wait()
    for copy in c_a:
        copy.wait()

    lane = lax.broadcasted_iota(jnp.int32, (64, B), 1)
    sub = lax.broadcasted_iota(jnp.int32, (64, B), 0)

    def column(row):
        return jnp.transpose(jnp.broadcast_to(row, (128, 64)))[:, 0:1]

    lead_ridge = [column(jnp.where(z < 4, ridge4[k], ridge_far[k])) for k in range(4)]
    for k in range(4):
        rows = slab_a[4 * k : 4 * k + 4].reshape(64, B)
        mat[64 * k : 64 * k + 64, 0:B] = rows + jnp.where(lane == sub + 64 * k, lead_ridge[k], 0.0)
        mat[64 * k : 64 * k + 64, B:] = jnp.where(lane == sub + 64 * k, 1.0, 0.0).astype(F32)

    turned = (((0,), (0,)), ((), ()))
    following, off = mat[0:NB, 0:128], 0
    for r0 in range(0, B, NB):
        r1 = r0 + NB
        if r0 == B * 3 // 4:
            for i in range(1, nz):
                z_b[i - 1].wait()
                c_b.append(to_core(slab_b, s_cb, r_cb, i))
        w = block_inverse(following, off)[:, 0:NB]
        if r1 == B:
            mat[r0:r1, B:] = dot(w, mat[r0:r1, B:])
            break
        c0, w1 = r1 // 128 * 128, B + (r1 + 127) // 128 * 128
        rj = dot(w, mat[r0:r1, c0:w1])
        mat[r0:r1, B:w1] = rj[:, B - c0 :]
        hi, mid, low = split3(rj)
        left = jnp.concatenate([hi, hi, mid, hi, low, mid], axis=0)
        right = jnp.concatenate([hi, mid, hi, low, hi, mid], axis=0)
        off = r1 - c0
        near = lax.dot_general(
            left[:, 0:128], right[:, 0:128], turned, preferred_element_type=F32
        )
        following = mat[r1 : r1 + NB, c0 : c0 + 128] - near[off : off + NB, :]
        step = lax.dot_general(left[:, : B - c0], right, turned, preferred_element_type=F32)
        mat[r1:B, c0:w1] -= step[off:, :]

    for copy in own_a:
        copy.wait()
    first = (e * 8 + p) * 64
    own_ridge = column(ridge_ref[...])
    winv = mat[:, B:]
    lead = oa_ref[x] + got_oa[0] + got_oa[1] + got_oa[2]
    lead = lead + jnp.where(lane == sub + first, own_ridge, 0.0)
    panel = dot(lead, winv, ((1,), (1,)))
    weight = dot(panel, winv)
    parts = jnp.concatenate(split3(weight), axis=0)
    out_ref[:, 0:B] = panel
    for copy in c_b:
        copy.wait()
    for copy in own_b:
        copy.wait()
    cols = lb_ref.shape[1]
    for j0 in range(0, cols, B):
        three = jnp.dot(
            parts, slab_b[:, :, j0 : j0 + B].reshape(B, B), preferred_element_type=F32
        )
        known = three[0:64] + three[64:128] + three[128:192]
        if j0 == 0:
            exact = [
                slab_a[4 * k : 4 * k + 4].reshape(64, B)
                + jnp.where(lane == sub + 64 * k, lead_ridge[k], 0.0)
                for k in range(4)
            ]
            known = jnp.where(y == 0, dot(weight, jnp.concatenate(exact, axis=0)), known)
        at = slice(j0, j0 + B)
        tile = oc_ref[:, at] + got_ob[0, :, at].astype(F32)
        tile = tile + got_ob[1, :, at].astype(F32) + got_ob[2, :, at].astype(F32)
        tile = tile + jnp.where(lane + (y * cols + j0) == sub + first, own_ridge, 0.0)
        out_ref[:, B + j0 : B + j0 + B] = tile - known


def split_kernel(both_ref, panel_ref, schur_ref):
    panel_ref[...] = both_ref[:, 0:B]
    schur_ref[...] = both_ref[:, B:]


def on_device(steps, harmonic, col_scale, taps, ridge):
    cols = harmonic.shape[0] // 4
    width = cols + B
    here, n_rows = 2048, 544
    dma = pltpu.SemaphoreType.DMA
    vmem = pltpu.VMEM
    both = pl.pallas_call(
        whole_kernel,
        out_shape=jax.ShapeDtypeStruct((64, width), F32),
        in_specs=[VMEM] * 5,
        out_specs=VMEM,
        scratch_shapes=[
            vmem((8, 2, steps.shape[1]), BF16),
            vmem((8, 1, 64), F32),
            vmem((2, steps.shape[1]), BF16),
            vmem((256, 128), F32),
            vmem((16, width), BF16),
            vmem((1, width), F32),
            vmem((n_rows, 16), BF16),
            vmem((n_rows, 128), F32),
            vmem((512, 256), BF16),
            vmem((128, 128), F32),
            *([vmem((BLK, width), BF16)] * 3),
            *([vmem((n_rows, BLK), BF16)] * 3),
            vmem((here, width), BF16),
            vmem((n_rows, here), BF16),
            *([vmem((width // B, B, B), F32)] * 3),
            *([vmem((width // B, 16, B), F32)] * 3),
            vmem((16, B), F32),
            vmem((16, cols), F32),
            vmem((NX, 64, B), F32),
            vmem((NX, 64, cols), BF16),
            vmem((64, cols), F32),
            vmem((16, 16, B), F32),
            vmem((16, 16, cols), BF16),
            vmem((NX - 1, 16, B), F32),
            vmem((NX - 1, 16, cols), F32),
            vmem((NX - 1, 64, B), F32),
            vmem((NX - 1, 64, cols), BF16),
            vmem((NX, 1, 64), F32),
            vmem((NX, 1, 64), F32),
            vmem((B, 2 * B), F32),
            *([dma((7,))] * 4), *([dma((5,))] * 4), *([dma((3,))] * 10), dma, dma,
            *([dma((7,))] * 4), *([dma((8,))] * 4),
        ],
        compiler_params=pltpu.CompilerParams(
            collective_id=0, has_side_effects=True, vmem_limit_bytes=60 * 1024 * 1024
        ),
        name="whole",
    )(
        steps,
        harmonic.reshape(-1, 128),
        col_scale.reshape(-1, 128),
        taps.reshape(2, 128),
        ridge.reshape(1, -1),
    )
    return pl.pallas_call(
        split_kernel,
        out_shape=(
            jax.ShapeDtypeStruct((64, B), F32),
            jax.ShapeDtypeStruct((64, cols), F32),
        ),
        in_specs=[VMEM],
        out_specs=(VMEM, VMEM),
        name="split",
    )(both)


def solution(mesh):
    row = P(("epoch", "prow"))
    return jax.shard_map(
        on_device,
        mesh=mesh,
        in_specs=(P(None, "epoch"), P(), P(), P(), row),
        out_specs=(P(("epoch", "prow"), None), P(("epoch", "prow"), "pcol")),
        check_vma=False,
    )
```

```python
import functools

import jax
import jax.numpy as jnp
from jax import lax
from jax.experimental import pallas as pl
from jax.experimental.pallas import tpu as pltpu
from jax.sharding import PartitionSpec as P

F32 = jnp.float32
BF16 = jnp.bfloat16
MESH = pl.DeviceIdType.MESH
HIGH = lax.Precision.HIGHEST
B = 256
BLK = 256
CHUNK = 64
PERIOD = 4096
NX = 4
WAVE = (8.88573567404434, -58.45953046181323, 115.03267724691959, -100.39492606524867)
ROUND = 12582912.0
VMEM = pl.BlockSpec(memory_space=pltpu.VMEM)


def place():
    e, p, y = (lax.axis_index(a) for a in ("epoch", "prow", "pcol"))
    core, z_lo = e % 2, e // 2
    x, z_hi = p % NX, p // NX
    return x, y, z_hi * 4 + z_lo, core


def device(x, z, core):
    return {"epoch": (z % 4) * 2 + core, "prow": (z // 4) * NX + x}


def wave(turn, scale):
    whole = (turn + ROUND) - ROUND
    z = 0.25 - jnp.abs(turn - whole)
    s = z * z
    poly = s + WAVE[2] / WAVE[3]
    for c in (WAVE[1], WAVE[0]):
        poly = poly * s + c / WAVE[3]
    return poly * (z * scale)


def halves(v):
    hi = jnp.floor(v * 64.0) * (1.0 / 64.0)
    return hi, v - hi


def dot(a, b, dims=((1,), (0,))):
    return lax.dot_general(a, b, (dims, ((), ())), precision=HIGH, preferred_element_type=F32)


def split3(v):
    hi = v.astype(BF16)
    v = v - hi.astype(F32)
    mid = v.astype(BF16)
    low = (v - mid.astype(F32)).astype(BF16)
    return hi, mid, low


NB = 32


def block_inverse(a, off):
    groups = NB // 8
    full = (8, 128)
    sub = lax.broadcasted_iota(jnp.int32, full, 0)
    lane = lax.broadcasted_iota(jnp.int32, full, 1)

    def spread(v, s):
        return jnp.broadcast_to(v[s : s + 1, :], full)

    col = [
        {k: jnp.broadcast_to(a[8 * k : 8 * k + 8, off + c : off + c + 1], full) for k in range(c // 8, groups)}
        for c in range(NB)
    ]
    inv = [jnp.where(lane == sub + 8 * k, 1.0, 0.0).astype(F32) for k in range(groups)]
    root = [jnp.zeros(full, F32) for _ in range(groups)]
    for i in range(NB):
        k0, s = divmod(i, 8)
        pivot = spread(col[i][k0], s)
        over = 1.0 / pivot
        root[k0] = jnp.where(sub == s, lax.rsqrt(pivot), root[k0])
        ratio = {k: col[i][k] * over for k in range(k0, groups)}
        ratio[k0] = jnp.where(sub > s, ratio[k0], 0.0)
        for c in range(i + 1, NB):
            kc, sc = divmod(c, 8)
            top = spread(col[i][kc], sc)
            for k in range(kc, groups):
                col[c][k] = col[c][k] - ratio[k] * top
        top = spread(inv[k0], s)
        for k in range(k0, groups):
            inv[k] = inv[k] - ratio[k] * top
    return jnp.concatenate([inv[k] * root[k] for k in range(groups)], axis=0)


def whole_kernel(
    steps_ref, harm_ref, scale_ref, taps_ref, ridge_ref, out_ref,
    every, every_ridge, steps_out, phase_ref,
    colf, cols_s, rowf, rows_s, lowt, lowr, d0, d1, d2, e0, e1, e2, fcol, frow, mine, theirs, got_p, lead_own, lead_out, lead_in,
    la_ref, lb_ref, oa_ref, ob_ref, oc_ref,
    slab_a, slab_b, got_la, got_lb, got_oa, got_ob, ridge4, ridge_far, mat,
    s_st, r_st, s_ri, r_ri, s_p, r_p, s_l, r_l,
    s_la, r_la, s_lb, r_lb, s_oa, r_oa, s_ob, r_ob, s_r, r_r, s_f, r_f,
    s_za, r_za, s_zb, r_zb, s_ca, r_ca, s_cb, r_cb,
):
    x, y, z, core = place()
    e, p = lax.axis_index("epoch"), lax.axis_index("prow")
    nz, ne = 8, 8

    def group(zz, cc):
        return ((zz % 4) * 2 + cc) * 2 + zz // 4

    g = group(z, core)
    peers = [device((x + i) % NX, z, core) for i in range(1, NX)]
    tall = [device(x, (z + i) % nz, core) for i in range(1, nz)]
    ring = [{"epoch": (e + i) % ne} for i in range(1, ne)]
    across = [device(x, (1 - z // 4) * 4 + i, core) for i in range(4)]
    other = device(x, z, 1 - core)
    barrier = pltpu.get_barrier_semaphore()
    cross = [device((x + i) % NX, z, 1 - core) for i in range(1, NX)]
    greeted = ring + peers + cross + across
    for peer in greeted:
        pl.semaphore_signal(barrier, inc=1, device_id=peer, device_id_type=MESH)
    pl.semaphore_wait(barrier, len(greeted))

    def put(src, dst, send, recv, peer):
        copy = pltpu.make_async_remote_copy(
            src_ref=src, dst_ref=dst, send_sem=send, recv_sem=recv,
            device_id=peer, device_id_type=MESH,
        )
        copy.start()
        return copy

    def to_x(src, got, send, recv):
        return [put(src(i), got.at[i - 1], send.at[i - 1], recv.at[i - 1], peers[i - 1]) for i in range(1, NX)]

    def to_z(slab, send, recv):
        return [put(slab.at[g], slab.at[g], send.at[i - 1], recv.at[i - 1], tall[i - 1]) for i in range(1, nz)]

    def to_core(slab, send, recv, i):
        k = group((z + nz - i) % nz, core)
        return put(slab.at[k], slab.at[k], send.at[i], recv.at[i], other)

    steps_out[...] = steps_ref[...].astype(F32).astype(BF16)
    given = [
        put(steps_out, every.at[e], s_st.at[i], r_st.at[i], ring[i]) for i in range(ne - 1)
    ] + [
        put(ridge_ref, every_ridge.at[e], s_ri.at[i], r_ri.at[i], ring[i]) for i in range(ne - 1)
    ]
    every[e] = steps_out[...]
    every_ridge[e] = ridge_ref[...]
    blocks = (ne * steps_ref.shape[1] // BLK) // (2 * NX)
    n_rows = rows_s.shape[0]
    n_lead = (n_rows - 2 * B) // 2
    n_tiles = colf.shape[1] // 128
    cols_here = n_tiles - 2
    dcol, drow = (d0, d1, d2), (e0, e1, e2)

    def features(k):
        h = harm_ref[pl.ds(k, 1), :]
        order = lax.shift_right_logical(h, 6).astype(F32)
        degree = (h & 63).astype(F32)
        shift = jnp.full((1, 128), -0.125, F32)
        rows = jnp.concatenate(
            [order, order, degree, degree, shift, jnp.zeros((11, 128), F32)], axis=0
        )
        return rows, scale_ref[pl.ds(k, 1), :] * WAVE[3]

    def down(row):
        return jnp.transpose(jnp.broadcast_to(row, (128, 128)))

    for jt in range(n_tiles):
        k = jt if jt < 2 else y * cols_here + (jt - 2)
        rows, scale = features(k)
        colf[:, jt * 128 : jt * 128 + 128] = rows.astype(BF16)
        cols_s[:, jt * 128 : jt * 128 + 128] = scale
    per = 128 // n_lead
    for side, gg in enumerate((group(z, 1 - core), g)):
        top = 2 * n_lead + side * B
        for half in range(2):
            rows, scale = features(gg * 2 + half)
            at = slice(top + half * 128, top + half * 128 + 128)
            rowf[at, :] = jnp.transpose(rows).astype(BF16)
            rows_s[at, :] = down(scale)
        rows, scale = features(gg // per)
        piece = pl.ds(pl.multiple_of((gg % per) * n_lead, n_lead), n_lead)
        at = slice(side * n_lead, side * n_lead + n_lead)
        lowr[...] = down(scale)
        rows_s[at, :] = lowr[piece, :]
        lowr[:, 0:16] = jnp.transpose(rows)
        rowf[at, :] = lowr[piece, 0:16].astype(BF16)

    base = jnp.concatenate([taps_ref[0:1, :], taps_ref[1:2, :], jnp.zeros((1, 256), F32)], axis=1)
    full = pltpu.roll(
        jnp.broadcast_to(base, (512, 512)), 256, 1, stride=1, stride_axis=0
    )[:, :256]
    lowt[...] = full.astype(BF16)
    low_up = jnp.transpose(full).astype(BF16)


    pairs = 2 * ne
    rows = pairs * steps_ref.shape[1] // 128
    upper = (
        lax.broadcasted_iota(jnp.int32, (128, 128), 0)
        <= lax.broadcasted_iota(jnp.int32, (128, 128), 1)
    ).astype(BF16)
    r_at = lax.broadcasted_iota(jnp.int32, (rows, rows), 0)
    s_at = lax.broadcasted_iota(jnp.int32, (rows, rows), 1)
    same = r_at % 2 == s_at % 2
    key_r = ((r_at % pairs) // 2) * rows + r_at // pairs
    key_s = ((s_at % pairs) // 2) * rows + s_at // pairs
    before = jnp.where(same & (key_s < key_r), 1.0, 0.0).astype(BF16)
    for copy in given:
        copy.wait()
    flat = every[...].astype(F32).reshape(pairs, steps_ref.shape[1])
    stack = jnp.concatenate(
        [flat[:, 128 * k : 128 * k + 128] for k in range(rows // pairs)], axis=0
    )
    inside = jnp.dot(stack.astype(BF16), upper, preferred_element_type=F32)
    totals = jnp.broadcast_to(inside[:, 127:128], (rows, 128))
    high = jnp.floor(totals * (1.0 / 64.0))
    low = totals - high * 64.0
    earlier = jnp.dot(before, high.astype(BF16), preferred_element_type=F32) * 64.0
    earlier = earlier + jnp.dot(before, low.astype(BF16), preferred_element_type=F32)
    turns = (inside + earlier) * (1.0 / PERIOD)
    phase_ref[...] = turns - jnp.floor(turns)

    def phases_of(b):
        at = jnp.maximum((x * 2 + core) * blocks + b - 1, 0)
        row0 = (at % 8) * 32 + (at // 8) * 2
        parts = []
        for a in range(2):
            q = jnp.concatenate(
                [phase_ref[pl.ds(row0 + 16 * half + a, 1), :] for half in range(2)], axis=1
            )
            parts += list(halves(q))
        parts += [jnp.ones((1, BLK), F32), jnp.zeros((11, BLK), F32)]
        rows = jnp.concatenate(parts, axis=0)
        return rows.astype(BF16), jnp.transpose(rows).astype(BF16)

    def design(qt, slot, j0):
        scale = cols_s[:, j0 : j0 + 256]
        for r0 in range(0, BLK, CHUNK):
            turn = jnp.dot(
                qt[r0 : r0 + CHUNK, :], colf[:, j0 : j0 + 256], preferred_element_type=F32
            )
            dcol[slot][r0 : r0 + CHUNK, j0 : j0 + 256] = wave(turn, scale).astype(BF16)

    def design_rows(qf, slot):
        for r0 in range(0, n_rows, CHUNK):
            r1 = min(r0 + CHUNK, n_rows)
            turn = jnp.dot(rowf[r0:r1, :], qf, preferred_element_type=F32)
            scale = rows_s[r0:r1, :]
            d = wave(turn, jnp.concatenate([scale, scale], axis=1))
            drow[slot][r0:r1, :] = d.astype(BF16)

    def filter_cols(b, s0, s1, j0):
        both = jnp.concatenate(
            [dcol[s0][:, j0 : j0 + 256], dcol[s1][:, j0 : j0 + 256]], axis=0
        )
        f = jnp.dot(low_up, both, preferred_element_type=F32).astype(BF16)
        fcol[pl.ds(pl.multiple_of(b * BLK, BLK), BLK), j0 : j0 + 256] = f

    def filter_rows(b, s0, s1):
        both = jnp.concatenate([drow[s0][...], drow[s1][...]], axis=1)
        f = jnp.dot(both, lowt[...], preferred_element_type=F32).astype(BF16)
        frow[:, pl.ds(pl.multiple_of(b * BLK, BLK), BLK)] = f

    wide = range(0, n_tiles * 128, 256)
    for b in range(2):
        qf, qt = phases_of(b)
        for j0 in wide:
            design(qt, b, j0)
        design_rows(qf, b)

    @pl.when((x == 0) & (core == 0))
    def _():
        d0[...] = jnp.zeros_like(d0)
        e0[...] = jnp.zeros_like(e0)

    def block_pass(b, s, more):
        if more:
            qf, qt = phases_of(b + 2)
        for j0 in wide:
            filter_cols(b, s, (s + 1) % 3, j0)
            if more:
                design(qt, (s + 2) % 3, j0)
        filter_rows(b, s, (s + 1) % 3)
        if more:
            design_rows(qf, (s + 2) % 3)

    trips = (blocks - 1) // 3

    @pl.loop(0, trips)
    def _(step):
        for s in range(3):
            block_pass(step * 3 + s, s, True)

    for b in range(trips * 3, blocks):
        block_pass(b, b % 3, b + 2 <= blocks)

    total = 1.0 / (blocks * BLK * 2 * NX)
    swaps = []

    def leading(j):
        part = jnp.dot(
            frow[: 2 * n_lead, :], fcol[:, j * B : j * B + B], preferred_element_type=F32
        )
        return part[:n_lead] * total, part[n_lead:] * total

    def product(j):
        part = jnp.dot(
            frow[2 * n_lead :, :], fcol[:, j * B : j * B + B], preferred_element_type=F32
        )
        theirs[j] = part[:B] * total
        swaps.append(put(theirs.at[j], got_p.at[j], s_p.at[j], r_p.at[j], other))
        mine[j] = part[B:] * total

    own_piece = pl.ds(pl.multiple_of(x * 64, 64), 64)

    def settle(j):
        swaps[j].wait()
        part = mine[j] + got_p[j]
        if j == 0:
            oa_ref[...] = part.reshape(NX, 64, B)
            return
        at = slice(j * B - B, j * B)
        ob_ref[:, :, at] = part.astype(BF16).reshape(NX, 64, B)
        oc_ref[:, at] = mine[j, own_piece, :] + got_p[j, own_piece, :]

    given_a, own_a0 = leading(0)
    la_ref[1 - core] = given_a
    la_ref[core] = own_a0
    lead_a = []
    for i, peer in enumerate([other] + peers + cross):
        side = core if 1 <= i < NX else 1 - core
        lead_a.append(put(la_ref.at[side], got_la.at[i], s_la.at[i], r_la.at[i], peer))
    ridge4[x] = every_ridge[0]
    ridges = [
        put(every_ridge.at[0], ridge4.at[x], s_r.at[i - 1], r_r.at[i - 1], peers[i - 1])
        for i in range(1, NX)
    ]
    for j in range(1, n_tiles // 2):
        at = slice(j * B - B, j * B)
        lead_out[:, at], lead_own[:, at] = leading(j)
    lead_swap = put(lead_out, lead_in, s_l, r_l, other)
    product(0)
    product(1)
    lead_swap.wait()
    lb_ref[...] = lead_own[...] + lead_in[...]
    lead_b = to_x(lambda i: lb_ref, got_lb, s_lb, r_lb)
    product(2)
    for copy in lead_a:
        copy.wait()
    block = la_ref[core]
    for i in range(2 * NX - 1):
        block = block + got_la[i]
    slab_a[g] = block
    z_a = to_z(slab_a, s_za, r_za)
    c_a = [to_core(slab_a, s_ca, r_ca, 0)]
    for copy in ridges:
        copy.wait()
    far = put(ridge4, ridge_far, s_f, r_f, device(x, (z + 4) % nz, core))
    product(3)
    settle(0)
    product(4)
    settle(1)
    for copy in lead_b:
        copy.wait()
    slab_b[g] = (lb_ref[...] + got_lb[0] + got_lb[1] + got_lb[2]).astype(BF16)
    z_b = to_z(slab_b, s_zb, r_zb)
    c_b = [to_core(slab_b, s_cb, r_cb, 0)]
    for j in range(2, n_tiles // 2):
        settle(j)
    own_a = to_x(lambda i: oa_ref.at[(x + i) % NX], got_oa, s_oa, r_oa)
    own_b = to_x(lambda i: ob_ref.at[(x + i) % NX], got_ob, s_ob, r_ob)
    for i in range(1, nz):
        z_a[i - 1].wait()
        c_a.append(to_core(slab_a, s_ca, r_ca, i))
    far.wait()
    for copy in c_a:
        copy.wait()

    lane = lax.broadcasted_iota(jnp.int32, (64, B), 1)
    sub = lax.broadcasted_iota(jnp.int32, (64, B), 0)

    def column(row):
        return jnp.transpose(jnp.broadcast_to(row, (128, 64)))[:, 0:1]

    lead_ridge = [column(jnp.where(z < 4, ridge4[k], ridge_far[k])) for k in range(4)]
    for k in range(4):
        rows = slab_a[4 * k : 4 * k + 4].reshape(64, B)
        mat[64 * k : 64 * k + 64, 0:B] = rows + jnp.where(lane == sub + 64 * k, lead_ridge[k], 0.0)
        mat[64 * k : 64 * k + 64, B:] = jnp.where(lane == sub + 64 * k, 1.0, 0.0).astype(F32)

    turned = (((0,), (0,)), ((), ()))
    following, off = mat[0:NB, 0:128], 0
    for r0 in range(0, B, NB):
        r1 = r0 + NB
        if r0 == B * 3 // 4:
            for i in range(1, nz):
                z_b[i - 1].wait()
                c_b.append(to_core(slab_b, s_cb, r_cb, i))
        w = block_inverse(following, off)[:, 0:NB]
        if r1 == B:
            mat[r0:r1, B:] = dot(w, mat[r0:r1, B:])
            break
        c0, w1 = r1 // 128 * 128, B + (r1 + 127) // 128 * 128
        rj = dot(w, mat[r0:r1, c0:w1])
        mat[r0:r1, B:w1] = rj[:, B - c0 :]
        hi, mid, low = split3(rj)
        left = jnp.concatenate([hi, hi, mid, hi, low, mid], axis=0)
        right = jnp.concatenate([hi, mid, hi, low, hi, mid], axis=0)
        off = r1 - c0
        near = lax.dot_general(
            left[:, 0:128], right[:, 0:128], turned, preferred_element_type=F32
        )
        following = mat[r1 : r1 + NB, c0 : c0 + 128] - near[off : off + NB, :]
        step = lax.dot_general(left[:, : B - c0], right, turned, preferred_element_type=F32)
        mat[r1:B, c0:w1] -= step[off:, :]

    for copy in own_a:
        copy.wait()
    first = (e * 8 + p) * 64
    own_ridge = column(ridge_ref[...])
    winv = mat[:, B:]
    lead = oa_ref[x] + got_oa[0] + got_oa[1] + got_oa[2]
    lead = lead + jnp.where(lane == sub + first, own_ridge, 0.0)
    panel = dot(lead, winv, ((1,), (1,)))
    weight = dot(panel, winv)
    parts = jnp.concatenate(split3(weight), axis=0)
    out_ref[:, 0:B] = panel
    for copy in c_b:
        copy.wait()
    for copy in own_b:
        copy.wait()
    cols = lb_ref.shape[1]
    for j0 in range(0, cols, B):
        three = jnp.dot(
            parts, slab_b[:, :, j0 : j0 + B].reshape(B, B), preferred_element_type=F32
        )
        known = three[0:64] + three[64:128] + three[128:192]
        if j0 == 0:
            exact = [
                slab_a[4 * k : 4 * k + 4].reshape(64, B)
                + jnp.where(lane == sub + 64 * k, lead_ridge[k], 0.0)
                for k in range(4)
            ]
            known = jnp.where(y == 0, dot(weight, jnp.concatenate(exact, axis=0)), known)
        at = slice(j0, j0 + B)
        tile = oc_ref[:, at] + got_ob[0, :, at].astype(F32)
        tile = tile + got_ob[1, :, at].astype(F32) + got_ob[2, :, at].astype(F32)
        tile = tile + jnp.where(lane + (y * cols + j0) == sub + first, own_ridge, 0.0)
        out_ref[:, B + j0 : B + j0 + B] = tile - known


def split_kernel(both_ref, panel_ref, schur_ref):
    panel_ref[...] = both_ref[:, 0:B]
    schur_ref[...] = both_ref[:, B:]


def on_device(steps, harmonic, col_scale, taps, ridge):
    cols = harmonic.shape[0] // 4
    width = cols + B
    here, n_rows = 2048, 544
    dma = pltpu.SemaphoreType.DMA
    vmem = pltpu.VMEM
    both = pl.pallas_call(
        whole_kernel,
        out_shape=jax.ShapeDtypeStruct((64, width), F32),
        in_specs=[VMEM] * 5,
        out_specs=VMEM,
        scratch_shapes=[
            vmem((8, 2, steps.shape[1]), BF16),
            vmem((8, 1, 64), F32),
            vmem((2, steps.shape[1]), BF16),
            vmem((256, 128), F32),
            vmem((16, width), BF16),
            vmem((1, width), F32),
            vmem((n_rows, 16), BF16),
            vmem((n_rows, 128), F32),
            vmem((512, 256), BF16),
            vmem((128, 128), F32),
            *([vmem((BLK, width), BF16)] * 3),
            *([vmem((n_rows, BLK), BF16)] * 3),
            vmem((here, width), BF16),
            vmem((n_rows, here), BF16),
            *([vmem((width // B, B, B), F32)] * 3),
            *([vmem((16, cols), F32)] * 3),
            vmem((2, 16, B), F32),
            vmem((16, cols), F32),
            vmem((NX, 64, B), F32),
            vmem((NX, 64, cols), BF16),
            vmem((64, cols), F32),
            vmem((16, 16, B), F32),
            vmem((16, 16, cols), BF16),
            vmem((2 * NX - 1, 16, B), F32),
            vmem((NX - 1, 16, cols), F32),
            vmem((NX - 1, 64, B), F32),
            vmem((NX - 1, 64, cols), BF16),
            vmem((NX, 1, 64), F32),
            vmem((NX, 1, 64), F32),
            vmem((B, 2 * B), F32),
            *([dma((7,))] * 4), *([dma((5,))] * 2), dma, dma, *([dma((7,))] * 2), *([dma((3,))] * 8), dma, dma,
            *([dma((7,))] * 4), *([dma((8,))] * 4),
        ],
        compiler_params=pltpu.CompilerParams(
            collective_id=0, has_side_effects=True, vmem_limit_bytes=60 * 1024 * 1024
        ),
        name="whole",
    )(
        steps,
        harmonic.reshape(-1, 128),
        col_scale.reshape(-1, 128),
        taps.reshape(2, 128),
        ridge.reshape(1, -1),
    )
    return pl.pallas_call(
        split_kernel,
        out_shape=(
            jax.ShapeDtypeStruct((64, B), F32),
            jax.ShapeDtypeStruct((64, cols), F32),
        ),
        in_specs=[VMEM],
        out_specs=(VMEM, VMEM),
        name="split",
    )(both)


def solution(mesh):
    row = P(("epoch", "prow"))
    return jax.shard_map(
        on_device,
        mesh=mesh,
        in_specs=(P(None, "epoch"), P(), P(), P(), row),
        out_specs=(P(("epoch", "prow"), None), P(("epoch", "prow"), "pcol")),
        check_vma=False,
    )
```

```python
import functools

import jax
import jax.numpy as jnp
from jax import lax
from jax.experimental import pallas as pl
from jax.experimental.pallas import tpu as pltpu
from jax.sharding import PartitionSpec as P

F32 = jnp.float32
BF16 = jnp.bfloat16
MESH = pl.DeviceIdType.MESH
HIGH = lax.Precision.HIGHEST
B = 256
BLK = 256
CHUNK = 64
PERIOD = 4096
NX = 4
FAR_FIRST = (4, 3, 5, 2, 6, 1, 7)
WAVE = (8.88573567404434, -58.45953046181323, 115.03267724691959, -100.39492606524867)
ROUND = 12582912.0
VMEM = pl.BlockSpec(memory_space=pltpu.VMEM)


def place():
    e, p, y = (lax.axis_index(a) for a in ("epoch", "prow", "pcol"))
    core, z_lo = e % 2, e // 2
    x, z_hi = p % NX, p // NX
    return x, y, z_hi * 4 + z_lo, core


def device(x, z, core):
    return {"epoch": (z % 4) * 2 + core, "prow": (z // 4) * NX + x}


def wave(turn, scale):
    whole = (turn + ROUND) - ROUND
    z = 0.25 - jnp.abs(turn - whole)
    s = z * z
    poly = s + WAVE[2] / WAVE[3]
    for c in (WAVE[1], WAVE[0]):
        poly = poly * s + c / WAVE[3]
    return poly * (z * scale)


def halves(v):
    hi = jnp.floor(v * 64.0) * (1.0 / 64.0)
    return hi, v - hi


def dot(a, b, dims=((1,), (0,))):
    return lax.dot_general(a, b, (dims, ((), ())), precision=HIGH, preferred_element_type=F32)


def split3(v):
    hi = v.astype(BF16)
    v = v - hi.astype(F32)
    mid = v.astype(BF16)
    low = (v - mid.astype(F32)).astype(BF16)
    return hi, mid, low


NB = 32


def block_inverse(a, off):
    groups = NB // 8
    full = (8, 128)
    sub = lax.broadcasted_iota(jnp.int32, full, 0)
    lane = lax.broadcasted_iota(jnp.int32, full, 1)

    def spread(v, s):
        return jnp.broadcast_to(v[s : s + 1, :], full)

    col = [
        {k: jnp.broadcast_to(a[8 * k : 8 * k + 8, off + c : off + c + 1], full) for k in range(c // 8, groups)}
        for c in range(NB)
    ]
    inv = [jnp.where(lane == sub + 8 * k, 1.0, 0.0).astype(F32) for k in range(groups)]
    root = [jnp.zeros(full, F32) for _ in range(groups)]
    for i in range(NB):
        k0, s = divmod(i, 8)
        pivot = spread(col[i][k0], s)
        over = 1.0 / pivot
        root[k0] = jnp.where(sub == s, lax.rsqrt(pivot), root[k0])
        ratio = {k: col[i][k] * over for k in range(k0, groups)}
        ratio[k0] = jnp.where(sub > s, ratio[k0], 0.0)
        for c in range(i + 1, NB):
            kc, sc = divmod(c, 8)
            top = spread(col[i][kc], sc)
            for k in range(kc, groups):
                col[c][k] = col[c][k] - ratio[k] * top
        top = spread(inv[k0], s)
        for k in range(k0, groups):
            inv[k] = inv[k] - ratio[k] * top
    return jnp.concatenate([inv[k] * root[k] for k in range(groups)], axis=0)


def whole_kernel(
    steps_hbm, harm_hbm, scale_hbm, taps_hbm, ridge_hbm, out_ref,
    steps_ref, harm_ref, scale_ref, taps_ref, ridge_ref, s_in,
    every, every_ridge, steps_out, phase_ref,
    colf, cols_s, rowf, rows_s, lowt, lowr, d0, d1, d2, e0, e1, e2, fcol, frow, mine, theirs, got_p, lead_own, lead_out, lead_in,
    la_ref, lb_ref, oa_ref, ob_ref, oc_ref,
    slab_a, slab_b, got_la, got_lb, got_oa, got_ob, ridge4, ridge_far, mat,
    s_st, r_st, s_ri, r_ri, s_p, r_p, s_l, r_l,
    s_la, r_la, s_lb, r_lb, s_oa, r_oa, s_ob, r_ob, s_r, r_r, s_f, r_f,
    s_za, r_za, s_zb, r_zb, s_ca, r_ca, s_cb, r_cb,
):
    x, y, z, core = place()
    e, p = lax.axis_index("epoch"), lax.axis_index("prow")
    nz, ne = 8, 8
    fetches = []
    for i, (src, dst) in enumerate((
        (steps_hbm, steps_ref), (ridge_hbm, ridge_ref), (harm_hbm, harm_ref),
        (scale_hbm, scale_ref), (taps_hbm, taps_ref),
    )):
        fetches.append(pltpu.make_async_copy(src, dst, s_in.at[i]))
        fetches[-1].start()

    def group(zz, cc):
        return ((zz % 4) * 2 + cc) * 2 + zz // 4

    g = group(z, core)
    peers = [device((x + i) % NX, z, core) for i in range(1, NX)]
    tall = [device(x, (z + i) % nz, core) for i in range(1, nz)]
    ring = [{"epoch": (e + i) % ne} for i in range(1, ne)]
    across = [device(x, (1 - z // 4) * 4 + i, core) for i in range(4)]
    other = device(x, z, 1 - core)
    barrier = pltpu.get_barrier_semaphore()
    cross = [device((x + i) % NX, z, 1 - core) for i in range(1, NX)]
    greeted = ring + peers + cross + across
    for peer in greeted:
        pl.semaphore_signal(barrier, inc=1, device_id=peer, device_id_type=MESH)
    pl.semaphore_wait(barrier, len(greeted))
    for fetch in fetches:
        fetch.wait()

    def put(src, dst, send, recv, peer):
        copy = pltpu.make_async_remote_copy(
            src_ref=src, dst_ref=dst, send_sem=send, recv_sem=recv,
            device_id=peer, device_id_type=MESH,
        )
        copy.start()
        return copy

    def to_x(src, got, send, recv):
        return [put(src(i), got.at[i - 1], send.at[i - 1], recv.at[i - 1], peers[i - 1]) for i in range(1, NX)]

    def to_z(slab, send, recv):
        sent = {}
        for i in FAR_FIRST:
            sent[i - 1] = put(slab.at[g], slab.at[g], send.at[i - 1], recv.at[i - 1], tall[i - 1])
        return sent

    def to_core(slab, send, recv, i):
        k = group((z + nz - i) % nz, core)
        return put(slab.at[k], slab.at[k], send.at[i], recv.at[i], other)

    steps_out[...] = steps_ref[...].astype(F32).astype(BF16)
    given = [
        put(steps_out, every.at[e], s_st.at[i], r_st.at[i], ring[i]) for i in range(ne - 1)
    ] + [
        put(ridge_ref, every_ridge.at[e], s_ri.at[i], r_ri.at[i], ring[i]) for i in range(ne - 1)
    ]
    every[e] = steps_out[...]
    every_ridge[e] = ridge_ref[...]
    blocks = (ne * steps_ref.shape[1] // BLK) // (2 * NX)
    n_rows = rows_s.shape[0]
    n_lead = (n_rows - 2 * B) // 2
    n_tiles = colf.shape[1] // 128
    cols_here = n_tiles - 2
    dcol, drow = (d0, d1, d2), (e0, e1, e2)

    def features(k):
        h = harm_ref[pl.ds(k, 1), :]
        order = lax.shift_right_logical(h, 6).astype(F32)
        degree = (h & 63).astype(F32)
        shift = jnp.full((1, 128), -0.125, F32)
        rows = jnp.concatenate(
            [order, order, degree, degree, shift, jnp.zeros((11, 128), F32)], axis=0
        )
        return rows, scale_ref[pl.ds(k, 1), :] * WAVE[3]

    def down(row):
        return jnp.transpose(jnp.broadcast_to(row, (128, 128)))

    for jt in range(n_tiles):
        k = jt if jt < 2 else y * cols_here + (jt - 2)
        rows, scale = features(k)
        colf[:, jt * 128 : jt * 128 + 128] = rows.astype(BF16)
        cols_s[:, jt * 128 : jt * 128 + 128] = scale
    per = 128 // n_lead
    for side, gg in enumerate((group(z, 1 - core), g)):
        top = 2 * n_lead + side * B
        for half in range(2):
            rows, scale = features(gg * 2 + half)
            at = slice(top + half * 128, top + half * 128 + 128)
            rowf[at, :] = jnp.transpose(rows).astype(BF16)
            rows_s[at, :] = down(scale)
        rows, scale = features(gg // per)
        piece = pl.ds(pl.multiple_of((gg % per) * n_lead, n_lead), n_lead)
        at = slice(side * n_lead, side * n_lead + n_lead)
        lowr[...] = down(scale)
        rows_s[at, :] = lowr[piece, :]
        lowr[:, 0:16] = jnp.transpose(rows)
        rowf[at, :] = lowr[piece, 0:16].astype(BF16)

    base = jnp.concatenate([taps_ref[0:1, :], taps_ref[1:2, :], jnp.zeros((1, 256), F32)], axis=1)
    full = pltpu.roll(
        jnp.broadcast_to(base, (512, 512)), 256, 1, stride=1, stride_axis=0
    )[:, :256]
    lowt[...] = full.astype(BF16)
    low_up = jnp.transpose(full).astype(BF16)


    pairs = 2 * ne
    rows = pairs * steps_ref.shape[1] // 128
    upper = (
        lax.broadcasted_iota(jnp.int32, (128, 128), 0)
        <= lax.broadcasted_iota(jnp.int32, (128, 128), 1)
    ).astype(BF16)
    r_at = lax.broadcasted_iota(jnp.int32, (rows, rows), 0)
    s_at = lax.broadcasted_iota(jnp.int32, (rows, rows), 1)
    same = r_at % 2 == s_at % 2
    key_r = ((r_at % pairs) // 2) * rows + r_at // pairs
    key_s = ((s_at % pairs) // 2) * rows + s_at // pairs
    before = jnp.where(same & (key_s < key_r), 1.0, 0.0).astype(BF16)
    for copy in given:
        copy.wait()
    flat = every[...].astype(F32).reshape(pairs, steps_ref.shape[1])
    stack = jnp.concatenate(
        [flat[:, 128 * k : 128 * k + 128] for k in range(rows // pairs)], axis=0
    )
    inside = jnp.dot(stack.astype(BF16), upper, preferred_element_type=F32)
    totals = jnp.broadcast_to(inside[:, 127:128], (rows, 128))
    high = jnp.floor(totals * (1.0 / 64.0))
    low = totals - high * 64.0
    earlier = jnp.dot(before, high.astype(BF16), preferred_element_type=F32) * 64.0
    earlier = earlier + jnp.dot(before, low.astype(BF16), preferred_element_type=F32)
    turns = (inside + earlier) * (1.0 / PERIOD)
    phase_ref[...] = turns - jnp.floor(turns)

    def phases_of(b):
        at = jnp.maximum((x * 2 + core) * blocks + b - 1, 0)
        row0 = (at % 8) * 32 + (at // 8) * 2
        parts = []
        for a in range(2):
            q = jnp.concatenate(
                [phase_ref[pl.ds(row0 + 16 * half + a, 1), :] for half in range(2)], axis=1
            )
            parts += list(halves(q))
        parts += [jnp.ones((1, BLK), F32), jnp.zeros((11, BLK), F32)]
        rows = jnp.concatenate(parts, axis=0)
        return rows.astype(BF16), jnp.transpose(rows).astype(BF16)

    def design(qt, slot, j0):
        scale = cols_s[:, j0 : j0 + 256]
        for r0 in range(0, BLK, CHUNK):
            turn = jnp.dot(
                qt[r0 : r0 + CHUNK, :], colf[:, j0 : j0 + 256], preferred_element_type=F32
            )
            dcol[slot][r0 : r0 + CHUNK, j0 : j0 + 256] = wave(turn, scale).astype(BF16)

    def design_rows(qf, slot):
        for r0 in range(0, n_rows, CHUNK):
            r1 = min(r0 + CHUNK, n_rows)
            turn = jnp.dot(rowf[r0:r1, :], qf, preferred_element_type=F32)
            scale = rows_s[r0:r1, :]
            d = wave(turn, jnp.concatenate([scale, scale], axis=1))
            drow[slot][r0:r1, :] = d.astype(BF16)

    def filter_cols(b, s0, s1, j0):
        both = jnp.concatenate(
            [dcol[s0][:, j0 : j0 + 256], dcol[s1][:, j0 : j0 + 256]], axis=0
        )
        f = jnp.dot(low_up, both, preferred_element_type=F32).astype(BF16)
        fcol[pl.ds(pl.multiple_of(b * BLK, BLK), BLK), j0 : j0 + 256] = f

    def filter_rows(b, s0, s1):
        both = jnp.concatenate([drow[s0][...], drow[s1][...]], axis=1)
        f = jnp.dot(both, lowt[...], preferred_element_type=F32).astype(BF16)
        frow[:, pl.ds(pl.multiple_of(b * BLK, BLK), BLK)] = f

    wide = range(0, n_tiles * 128, 256)
    for b in range(2):
        qf, qt = phases_of(b)
        for j0 in wide:
            design(qt, b, j0)
        design_rows(qf, b)

    @pl.when((x == 0) & (core == 0))
    def _():
        d0[...] = jnp.zeros_like(d0)
        e0[...] = jnp.zeros_like(e0)

    def block_pass(b, s, more):
        if more:
            qf, qt = phases_of(b + 2)
        for j0 in wide:
            filter_cols(b, s, (s + 1) % 3, j0)
            if more:
                design(qt, (s + 2) % 3, j0)
        filter_rows(b, s, (s + 1) % 3)
        if more:
            design_rows(qf, (s + 2) % 3)

    trips = (blocks - 1) // 3

    @pl.loop(0, trips)
    def _(step):
        for s in range(3):
            block_pass(step * 3 + s, s, True)

    for b in range(trips * 3, blocks):
        block_pass(b, b % 3, b + 2 <= blocks)

    total = 1.0 / (blocks * BLK * 2 * NX)
    swaps = []

    def leading(j):
        part = jnp.dot(
            frow[: 2 * n_lead, :], fcol[:, j * B : j * B + B], preferred_element_type=F32
        )
        return part[:n_lead] * total, part[n_lead:] * total

    def product(j):
        part = jnp.dot(
            frow[2 * n_lead :, :], fcol[:, j * B : j * B + B], preferred_element_type=F32
        )
        theirs[j] = part[:B] * total
        swaps.append(put(theirs.at[j], got_p.at[j], s_p.at[j], r_p.at[j], other))
        mine[j] = part[B:] * total

    own_piece = pl.ds(pl.multiple_of(x * 64, 64), 64)

    def settle(j):
        swaps[j].wait()
        part = mine[j] + got_p[j]
        if j == 0:
            oa_ref[...] = part.reshape(NX, 64, B)
            return
        at = slice(j * B - B, j * B)
        ob_ref[:, :, at] = part.astype(BF16).reshape(NX, 64, B)
        oc_ref[:, at] = mine[j, own_piece, :] + got_p[j, own_piece, :]

    given_a, own_a0 = leading(0)
    la_ref[1 - core] = given_a
    la_ref[core] = own_a0
    lead_a = []
    row = [other] + peers + cross
    for i in (2, 5, 1, 3, 4, 6, 0):
        peer = row[i]
        side = core if 1 <= i < NX else 1 - core
        lead_a.append(put(la_ref.at[side], got_la.at[i], s_la.at[i], r_la.at[i], peer))
    ridge4[x] = every_ridge[0]
    ridges = [
        put(every_ridge.at[0], ridge4.at[x], s_r.at[i - 1], r_r.at[i - 1], peers[i - 1])
        for i in range(1, NX)
    ]
    for j in range(1, n_tiles // 2):
        at = slice(j * B - B, j * B)
        lead_out[:, at], lead_own[:, at] = leading(j)
    lead_swap = put(lead_out, lead_in, s_l, r_l, other)
    product(0)
    product(1)
    lead_swap.wait()
    lb_ref[...] = lead_own[...] + lead_in[...]
    lead_b = to_x(lambda i: lb_ref, got_lb, s_lb, r_lb)
    product(2)
    for copy in lead_a:
        copy.wait()
    block = la_ref[core]
    for i in range(2 * NX - 1):
        block = block + got_la[i]
    slab_a[g] = block
    z_a = to_z(slab_a, s_za, r_za)
    c_a = [to_core(slab_a, s_ca, r_ca, 0)]
    for copy in ridges:
        copy.wait()
    far = put(ridge4, ridge_far, s_f, r_f, device(x, (z + 4) % nz, core))
    product(3)
    settle(0)
    product(4)
    settle(1)
    for copy in lead_b:
        copy.wait()
    slab_b[g] = (lb_ref[...] + got_lb[0] + got_lb[1] + got_lb[2]).astype(BF16)
    z_b = to_z(slab_b, s_zb, r_zb)
    c_b = [to_core(slab_b, s_cb, r_cb, 0)]
    for j in range(2, n_tiles // 2):
        settle(j)
    own_a = to_x(lambda i: oa_ref.at[(x + i) % NX], got_oa, s_oa, r_oa)
    own_b = to_x(lambda i: ob_ref.at[(x + i) % NX], got_ob, s_ob, r_ob)
    for i in reversed(FAR_FIRST):
        z_a[i - 1].wait()
        c_a.append(to_core(slab_a, s_ca, r_ca, i))
    far.wait()
    for copy in c_a:
        copy.wait()

    lane = lax.broadcasted_iota(jnp.int32, (64, B), 1)
    sub = lax.broadcasted_iota(jnp.int32, (64, B), 0)

    def column(row):
        return jnp.transpose(jnp.broadcast_to(row, (128, 64)))[:, 0:1]

    lead_ridge = [column(jnp.where(z < 4, ridge4[k], ridge_far[k])) for k in range(4)]
    for k in range(4):
        rows = slab_a[4 * k : 4 * k + 4].reshape(64, B)
        mat[64 * k : 64 * k + 64, 0:B] = rows + jnp.where(lane == sub + 64 * k, lead_ridge[k], 0.0)
        mat[64 * k : 64 * k + 64, B:] = jnp.where(lane == sub + 64 * k, 1.0, 0.0).astype(F32)

    turned = (((0,), (0,)), ((), ()))
    following, off = mat[0:NB, 0:128], 0
    for r0 in range(0, B, NB):
        r1 = r0 + NB
        if r0 == B * 3 // 4:
            for i in reversed(FAR_FIRST):
                z_b[i - 1].wait()
                c_b.append(to_core(slab_b, s_cb, r_cb, i))
        w = block_inverse(following, off)[:, 0:NB]
        if r1 == B:
            mat[r0:r1, B:] = dot(w, mat[r0:r1, B:])
            break
        c0, w1 = r1 // 128 * 128, B + (r1 + 127) // 128 * 128
        rj = dot(w, mat[r0:r1, c0:w1])
        mat[r0:r1, B:w1] = rj[:, B - c0 :]
        hi, mid, low = split3(rj)
        left = jnp.concatenate([hi, hi, mid, hi, low, mid], axis=0)
        right = jnp.concatenate([hi, mid, hi, low, hi, mid], axis=0)
        off = r1 - c0
        near = lax.dot_general(
            left[:, 0:128], right[:, 0:128], turned, preferred_element_type=F32
        )
        following = mat[r1 : r1 + NB, c0 : c0 + 128] - near[off : off + NB, :]
        step = lax.dot_general(left[:, : B - c0], right, turned, preferred_element_type=F32)
        mat[r1:B, c0:w1] -= step[off:, :]

    for copy in own_a:
        copy.wait()
    first = (e * 8 + p) * 64
    own_ridge = column(ridge_ref[...])
    winv = mat[:, B:]
    lead = oa_ref[x] + got_oa[0] + got_oa[1] + got_oa[2]
    lead = lead + jnp.where(lane == sub + first, own_ridge, 0.0)
    panel = dot(lead, winv, ((1,), (1,)))
    weight = dot(panel, winv)
    parts = jnp.concatenate(split3(weight), axis=0)
    out_ref[:, 0:B] = panel
    for copy in c_b:
        copy.wait()
    for copy in own_b:
        copy.wait()
    cols = lb_ref.shape[1]
    for j0 in range(0, cols, B):
        three = jnp.dot(
            parts, slab_b[:, :, j0 : j0 + B].reshape(B, B), preferred_element_type=F32
        )
        known = three[0:64] + three[64:128] + three[128:192]
        if j0 == 0:
            exact = [
                slab_a[4 * k : 4 * k + 4].reshape(64, B)
                + jnp.where(lane == sub + 64 * k, lead_ridge[k], 0.0)
                for k in range(4)
            ]
            known = jnp.where(y == 0, dot(weight, jnp.concatenate(exact, axis=0)), known)
        at = slice(j0, j0 + B)
        tile = oc_ref[:, at] + got_ob[0, :, at].astype(F32)
        tile = tile + got_ob[1, :, at].astype(F32) + got_ob[2, :, at].astype(F32)
        tile = tile + jnp.where(lane + (y * cols + j0) == sub + first, own_ridge, 0.0)
        out_ref[:, B + j0 : B + j0 + B] = tile - known


def split_kernel(both_ref, panel_ref, schur_ref):
    panel_ref[...] = both_ref[:, 0:B]
    schur_ref[...] = both_ref[:, B:]


def on_device(steps, harmonic, col_scale, taps, ridge):
    cols = harmonic.shape[0] // 4
    width = cols + B
    here, n_rows = 2048, 544
    dma = pltpu.SemaphoreType.DMA
    vmem = pltpu.VMEM
    both = pl.pallas_call(
        whole_kernel,
        out_shape=jax.ShapeDtypeStruct((64, width), F32),
        in_specs=[pl.BlockSpec(memory_space=pltpu.HBM)] * 5,
        out_specs=VMEM,
        scratch_shapes=[
            vmem(steps.shape, jnp.int32),
            vmem((32, 128), jnp.int32),
            vmem((32, 128), F32),
            vmem((2, 128), F32),
            vmem((1, 64), F32),
            dma((5,)),
            vmem((8, 2, steps.shape[1]), BF16),
            vmem((8, 1, 64), F32),
            vmem((2, steps.shape[1]), BF16),
            vmem((256, 128), F32),
            vmem((16, width), BF16),
            vmem((1, width), F32),
            vmem((n_rows, 16), BF16),
            vmem((n_rows, 128), F32),
            vmem((512, 256), BF16),
            vmem((128, 128), F32),
            *([vmem((BLK, width), BF16)] * 3),
            *([vmem((n_rows, BLK), BF16)] * 3),
            vmem((here, width), BF16),
            vmem((n_rows, here), BF16),
            *([vmem((width // B, B, B), F32)] * 3),
            *([vmem((16, cols), F32)] * 3),
            vmem((2, 16, B), F32),
            vmem((16, cols), F32),
            vmem((NX, 64, B), F32),
            vmem((NX, 64, cols), BF16),
            vmem((64, cols), F32),
            vmem((16, 16, B), F32),
            vmem((16, 16, cols), BF16),
            vmem((2 * NX - 1, 16, B), F32),
            vmem((NX - 1, 16, cols), F32),
            vmem((NX - 1, 64, B), F32),
            vmem((NX - 1, 64, cols), BF16),
            vmem((NX, 1, 64), F32),
            vmem((NX, 1, 64), F32),
            vmem((B, 2 * B), F32),
            *([dma((7,))] * 4), *([dma((5,))] * 2), dma, dma, *([dma((7,))] * 2), *([dma((3,))] * 8), dma, dma,
            *([dma((7,))] * 4), *([dma((8,))] * 4),
        ],
        compiler_params=pltpu.CompilerParams(
            collective_id=0, has_side_effects=True, vmem_limit_bytes=60 * 1024 * 1024
        ),
        name="whole",
    )(
        steps,
        harmonic.reshape(-1, 128),
        col_scale.reshape(-1, 128),
        taps.reshape(2, 128),
        ridge.reshape(1, -1),
    )
    return pl.pallas_call(
        split_kernel,
        out_shape=(
            jax.ShapeDtypeStruct((64, B), F32),
            jax.ShapeDtypeStruct((64, cols), F32),
        ),
        in_specs=[VMEM],
        out_specs=(VMEM, VMEM),
        name="split",
    )(both)


def solution(mesh):
    row = P(("epoch", "prow"))
    return jax.shard_map(
        on_device,
        mesh=mesh,
        in_specs=(P(None, "epoch"), P(), P(), P(), row),
        out_specs=(P(("epoch", "prow"), None), P(("epoch", "prow"), "pcol")),
        check_vma=False,
    )
```

```python
import functools

import jax
import jax.numpy as jnp
from jax import lax
from jax.experimental import pallas as pl
from jax.experimental.pallas import tpu as pltpu
from jax.sharding import PartitionSpec as P

F32 = jnp.float32
BF16 = jnp.bfloat16
MESH = pl.DeviceIdType.MESH
HIGH = lax.Precision.HIGHEST
B = 256
BLK = 256
CHUNK = 64
PERIOD = 4096
NX = 4
FAR_FIRST = (4, 3, 5, 2, 6, 1, 7)
WAVE = (8.88573567404434, -58.45953046181323, 115.03267724691959, -100.39492606524867)
ROUND = 12582912.0
VMEM = pl.BlockSpec(memory_space=pltpu.VMEM)


def place():
    e, p, y = (lax.axis_index(a) for a in ("epoch", "prow", "pcol"))
    core, z_lo = e % 2, e // 2
    x, z_hi = p % NX, p // NX
    return x, y, z_hi * 4 + z_lo, core


def device(x, z, core):
    return {"epoch": (z % 4) * 2 + core, "prow": (z // 4) * NX + x}


def wave(turn, scale):
    whole = (turn + ROUND) - ROUND
    z = 0.25 - jnp.abs(turn - whole)
    s = z * z
    poly = s + WAVE[2] / WAVE[3]
    for c in (WAVE[1], WAVE[0]):
        poly = poly * s + c / WAVE[3]
    return poly * (z * scale)


def halves(v):
    hi = jnp.floor(v * 64.0) * (1.0 / 64.0)
    return hi, v - hi


def dot(a, b, dims=((1,), (0,))):
    return lax.dot_general(a, b, (dims, ((), ())), precision=HIGH, preferred_element_type=F32)


def split3(v):
    hi = v.astype(BF16)
    v = v - hi.astype(F32)
    mid = v.astype(BF16)
    low = (v - mid.astype(F32)).astype(BF16)
    return hi, mid, low


NB = 32


def block_inverse(a, off):
    groups = NB // 8
    full = (8, 128)
    sub = lax.broadcasted_iota(jnp.int32, full, 0)
    lane = lax.broadcasted_iota(jnp.int32, full, 1)

    def spread(v, s):
        return jnp.broadcast_to(v[s : s + 1, :], full)

    col = [
        {k: jnp.broadcast_to(a[8 * k : 8 * k + 8, off + c : off + c + 1], full) for k in range(c // 8, groups)}
        for c in range(NB)
    ]
    inv = [jnp.where(lane == sub + 8 * k, 1.0, 0.0).astype(F32) for k in range(groups)]
    root = [jnp.zeros(full, F32) for _ in range(groups)]
    for i in range(NB):
        k0, s = divmod(i, 8)
        pivot = spread(col[i][k0], s)
        over = 1.0 / pivot
        root[k0] = jnp.where(sub == s, lax.rsqrt(pivot), root[k0])
        ratio = {k: col[i][k] * over for k in range(k0, groups)}
        ratio[k0] = jnp.where(sub > s, ratio[k0], 0.0)
        for c in range(i + 1, NB):
            kc, sc = divmod(c, 8)
            top = spread(col[i][kc], sc)
            for k in range(kc, groups):
                col[c][k] = col[c][k] - ratio[k] * top
        top = spread(inv[k0], s)
        for k in range(k0, groups):
            inv[k] = inv[k] - ratio[k] * top
    return jnp.concatenate([inv[k] * root[k] for k in range(groups)], axis=0)


def whole_kernel(
    steps_hbm, harm_hbm, scale_hbm, taps_hbm, ridge_hbm, out_ref,
    steps_ref, harm_ref, scale_ref, taps_ref, ridge_ref, s_in,
    every, every_ridge, steps_out, phase_ref,
    colf, cols_s, rowf, rows_s, lowt, lowr, d0, d1, d2, e0, e1, e2, fcol, frow, mine, theirs, got_p, lead_own, lead_out, lead_in,
    la_ref, lb_ref, oa_ref, ob_ref, oc_ref,
    slab_a, slab_b, got_la, got_lb, got_oa, got_ob, ridge4, ridge_far, mat,
    s_st, r_st, s_ri, r_ri, s_p, r_p, s_l, r_l,
    s_la, r_la, s_lb, r_lb, s_oa, r_oa, s_ob, r_ob, s_r, r_r, s_f, r_f,
    s_za, r_za, s_zb, r_zb, s_ca, r_ca, s_cb, r_cb,
):
    x, y, z, core = place()
    e, p = lax.axis_index("epoch"), lax.axis_index("prow")
    nz, ne = 8, 8
    fetches = []
    for i, (src, dst) in enumerate((
        (steps_hbm, steps_ref), (ridge_hbm, ridge_ref), (harm_hbm, harm_ref),
        (scale_hbm, scale_ref), (taps_hbm, taps_ref),
    )):
        fetches.append(pltpu.make_async_copy(src, dst, s_in.at[i]))
        fetches[-1].start()

    def group(zz, cc):
        return ((zz % 4) * 2 + cc) * 2 + zz // 4

    g = group(z, core)
    peers = [device((x + i) % NX, z, core) for i in range(1, NX)]
    tall = [device(x, (z + i) % nz, core) for i in range(1, nz)]
    ring = [{"epoch": (e + i) % ne} for i in range(1, ne)]
    across = [device(x, (1 - z // 4) * 4 + i, core) for i in range(4)]
    other = device(x, z, 1 - core)
    barrier = pltpu.get_barrier_semaphore()
    cross = [device((x + i) % NX, z, 1 - core) for i in range(1, NX)]
    greeted = ring + peers + cross + across
    for peer in greeted:
        pl.semaphore_signal(barrier, inc=1, device_id=peer, device_id_type=MESH)
    pl.semaphore_wait(barrier, len(greeted))
    for fetch in fetches:
        fetch.wait()

    def put(src, dst, send, recv, peer):
        copy = pltpu.make_async_remote_copy(
            src_ref=src, dst_ref=dst, send_sem=send, recv_sem=recv,
            device_id=peer, device_id_type=MESH,
        )
        copy.start()
        return copy

    def to_x(src, got, send, recv):
        return [put(src(i), got.at[i - 1], send.at[i - 1], recv.at[i - 1], peers[i - 1]) for i in range(1, NX)]

    def to_z(slab, send, recv):
        sent = {}
        for i in FAR_FIRST:
            sent[i - 1] = put(slab.at[g], slab.at[g], send.at[i - 1], recv.at[i - 1], tall[i - 1])
        return sent

    def to_core(slab, send, recv, i):
        k = group((z + nz - i) % nz, core)
        return put(slab.at[k], slab.at[k], send.at[i], recv.at[i], other)

    steps_out[...] = steps_ref[...].astype(F32).astype(BF16)
    given = [
        put(steps_out, every.at[e], s_st.at[i], r_st.at[i], ring[i]) for i in range(ne - 1)
    ] + [
        put(ridge_ref, every_ridge.at[e], s_ri.at[i], r_ri.at[i], ring[i]) for i in range(ne - 1)
    ]
    every[e] = steps_out[...]
    every_ridge[e] = ridge_ref[...]
    blocks = (ne * steps_ref.shape[1] // BLK) // (2 * NX)
    n_rows = rows_s.shape[0]
    n_lead = (n_rows - 2 * B) // 2
    n_tiles = colf.shape[1] // 128
    cols_here = n_tiles - 2
    dcol, drow = (d0, d1, d2), (e0, e1, e2)

    def features(k):
        h = harm_ref[pl.ds(k, 1), :]
        order = lax.shift_right_logical(h, 6).astype(F32)
        degree = (h & 63).astype(F32)
        shift = jnp.full((1, 128), -0.125, F32)
        rows = jnp.concatenate(
            [order, order, degree, degree, shift, jnp.zeros((11, 128), F32)], axis=0
        )
        return rows, scale_ref[pl.ds(k, 1), :] * WAVE[3]

    def down(row):
        return jnp.transpose(jnp.broadcast_to(row, (128, 128)))

    for jt in range(n_tiles):
        k = jt if jt < 2 else y * cols_here + (jt - 2)
        rows, scale = features(k)
        colf[:, jt * 128 : jt * 128 + 128] = rows.astype(BF16)
        cols_s[:, jt * 128 : jt * 128 + 128] = scale
    per = 128 // n_lead
    for side, gg in enumerate((group(z, 1 - core), g)):
        top = 2 * n_lead + side * B
        for half in range(2):
            rows, scale = features(gg * 2 + half)
            at = slice(top + half * 128, top + half * 128 + 128)
            rowf[at, :] = jnp.transpose(rows).astype(BF16)
            rows_s[at, :] = down(scale)
        rows, scale = features(gg // per)
        piece = pl.ds(pl.multiple_of((gg % per) * n_lead, n_lead), n_lead)
        at = slice(side * n_lead, side * n_lead + n_lead)
        lowr[...] = down(scale)
        rows_s[at, :] = lowr[piece, :]
        lowr[:, 0:16] = jnp.transpose(rows)
        rowf[at, :] = lowr[piece, 0:16].astype(BF16)

    base = jnp.concatenate([taps_ref[0:1, :], taps_ref[1:2, :], jnp.zeros((1, 256), F32)], axis=1)
    full = pltpu.roll(
        jnp.broadcast_to(base, (512, 512)), 256, 1, stride=1, stride_axis=0
    )[:, :256]
    lowt[...] = full.astype(BF16)
    low_up = jnp.transpose(full).astype(BF16)


    pairs = 2 * ne
    rows = pairs * steps_ref.shape[1] // 128
    upper = (
        lax.broadcasted_iota(jnp.int32, (128, 128), 0)
        <= lax.broadcasted_iota(jnp.int32, (128, 128), 1)
    ).astype(BF16)
    r_at = lax.broadcasted_iota(jnp.int32, (rows, rows), 0)
    s_at = lax.broadcasted_iota(jnp.int32, (rows, rows), 1)
    same = r_at % 2 == s_at % 2
    key_r = ((r_at % pairs) // 2) * rows + r_at // pairs
    key_s = ((s_at % pairs) // 2) * rows + s_at // pairs
    before = jnp.where(same & (key_s < key_r), 1.0, 0.0).astype(BF16)
    for copy in given:
        copy.wait()
    flat = every[...].astype(F32).reshape(pairs, steps_ref.shape[1])
    stack = jnp.concatenate(
        [flat[:, 128 * k : 128 * k + 128] for k in range(rows // pairs)], axis=0
    )
    inside = jnp.dot(stack.astype(BF16), upper, preferred_element_type=F32)
    totals = jnp.broadcast_to(inside[:, 127:128], (rows, 128))
    high = jnp.floor(totals * (1.0 / 64.0))
    low = totals - high * 64.0
    earlier = jnp.dot(before, high.astype(BF16), preferred_element_type=F32) * 64.0
    earlier = earlier + jnp.dot(before, low.astype(BF16), preferred_element_type=F32)
    turns = (inside + earlier) * (1.0 / PERIOD)
    phase_ref[...] = turns - jnp.floor(turns)

    def phases_of(b):
        at = jnp.maximum((x * 2 + core) * blocks + b - 1, 0)
        row0 = (at % 8) * 32 + (at // 8) * 2
        parts = []
        for a in range(2):
            q = jnp.concatenate(
                [phase_ref[pl.ds(row0 + 16 * half + a, 1), :] for half in range(2)], axis=1
            )
            parts += list(halves(q))
        parts += [jnp.ones((1, BLK), F32), jnp.zeros((11, BLK), F32)]
        rows = jnp.concatenate(parts, axis=0)
        return rows.astype(BF16), jnp.transpose(rows).astype(BF16)

    def design(qt, slot, j0):
        scale = cols_s[:, j0 : j0 + 256]
        for r0 in range(0, BLK, CHUNK):
            turn = jnp.dot(
                qt[r0 : r0 + CHUNK, :], colf[:, j0 : j0 + 256], preferred_element_type=F32
            )
            dcol[slot][r0 : r0 + CHUNK, j0 : j0 + 256] = wave(turn, scale).astype(BF16)

    def design_rows(qf, slot):
        for r0 in range(0, n_rows, CHUNK):
            r1 = min(r0 + CHUNK, n_rows)
            turn = jnp.dot(rowf[r0:r1, :], qf, preferred_element_type=F32)
            scale = rows_s[r0:r1, :]
            d = wave(turn, jnp.concatenate([scale, scale], axis=1))
            drow[slot][r0:r1, :] = d.astype(BF16)

    def filter_cols(b, s0, s1, j0):
        both = jnp.concatenate(
            [dcol[s0][:, j0 : j0 + 256], dcol[s1][:, j0 : j0 + 256]], axis=0
        )
        f = jnp.dot(low_up, both, preferred_element_type=F32).astype(BF16)
        fcol[pl.ds(pl.multiple_of(b * BLK, BLK), BLK), j0 : j0 + 256] = f

    def filter_rows(b, s0, s1):
        both = jnp.concatenate([drow[s0][...], drow[s1][...]], axis=1)
        f = jnp.dot(both, lowt[...], preferred_element_type=F32).astype(BF16)
        frow[:, pl.ds(pl.multiple_of(b * BLK, BLK), BLK)] = f

    wide = range(0, n_tiles * 128, 256)
    for b in range(2):
        qf, qt = phases_of(b)
        for j0 in wide:
            design(qt, b, j0)
        design_rows(qf, b)

    @pl.when((x == 0) & (core == 0))
    def _():
        d0[...] = jnp.zeros_like(d0)
        e0[...] = jnp.zeros_like(e0)

    def block_pass(b, s, more):
        if more:
            qf, qt = phases_of(b + 2)
        for j0 in wide:
            filter_cols(b, s, (s + 1) % 3, j0)
            if more:
                design(qt, (s + 2) % 3, j0)
        filter_rows(b, s, (s + 1) % 3)
        if more:
            design_rows(qf, (s + 2) % 3)

    trips = (blocks - 1) // 3

    @pl.loop(0, trips)
    def _(step):
        for s in range(3):
            block_pass(step * 3 + s, s, True)

    for b in range(trips * 3, blocks):
        block_pass(b, b % 3, b + 2 <= blocks)

    total = 1.0 / (blocks * BLK * 2 * NX)
    swaps = []

    def leading(j):
        part = jnp.dot(
            frow[: 2 * n_lead, :], fcol[:, j * B : j * B + B], preferred_element_type=F32
        )
        return part[:n_lead] * total, part[n_lead:] * total

    def product(j):
        part = jnp.dot(
            frow[2 * n_lead :, :], fcol[:, j * B : j * B + B], preferred_element_type=F32
        )
        theirs[j] = part[:B] * total
        swaps.append(put(theirs.at[j], got_p.at[j], s_p.at[j], r_p.at[j], other))
        mine[j] = part[B:] * total

    own_piece = pl.ds(pl.multiple_of(x * 64, 64), 64)

    def settle(j):
        swaps[j].wait()
        part = mine[j] + got_p[j]
        if j == 0:
            oa_ref[...] = part.reshape(NX, 64, B)
            return
        at = slice(j * B - B, j * B)
        ob_ref[:, :, at] = part.astype(BF16).reshape(NX, 64, B)
        oc_ref[:, at] = mine[j, own_piece, :] + got_p[j, own_piece, :]

    given_a, own_a0 = leading(0)
    la_ref[1 - core] = given_a
    la_ref[core] = own_a0
    lead_a = []
    row = [other] + peers + cross
    for i in (2, 5, 1, 3, 4, 6, 0):
        peer = row[i]
        side = core if 1 <= i < NX else 1 - core
        lead_a.append(put(la_ref.at[side], got_la.at[i], s_la.at[i], r_la.at[i], peer))
    ridge4[x] = every_ridge[0]
    ridges = [
        put(every_ridge.at[0], ridge4.at[x], s_r.at[i - 1], r_r.at[i - 1], peers[i - 1])
        for i in range(1, NX)
    ]
    for j in range(1, n_tiles // 2):
        at = slice(j * B - B, j * B)
        lead_out[:, at], lead_own[:, at] = leading(j)
    lead_swap = put(lead_out, lead_in, s_l, r_l, other)
    product(0)
    product(1)
    lead_swap.wait()
    lb_ref[...] = lead_own[...] + lead_in[...]
    lead_b = to_x(lambda i: lb_ref, got_lb, s_lb, r_lb)
    product(2)
    for copy in lead_a:
        copy.wait()
    block = la_ref[core]
    for i in range(2 * NX - 1):
        block = block + got_la[i]
    slab_a[g] = block
    z_a = to_z(slab_a, s_za, r_za)
    c_a = [to_core(slab_a, s_ca, r_ca, 0)]
    for copy in ridges:
        copy.wait()
    far = put(ridge4, ridge_far, s_f, r_f, device(x, (z + 4) % nz, core))
    product(3)
    settle(0)
    product(4)
    settle(1)
    for copy in lead_b:
        copy.wait()
    slab_b[g] = (lb_ref[...] + got_lb[0] + got_lb[1] + got_lb[2]).astype(BF16)
    z_b = to_z(slab_b, s_zb, r_zb)
    c_b = [to_core(slab_b, s_cb, r_cb, 0)]
    for j in range(2, n_tiles // 2):
        settle(j)
    own_a = to_x(lambda i: oa_ref.at[(x + i) % NX], got_oa, s_oa, r_oa)
    own_b = to_x(lambda i: ob_ref.at[(x + i) % NX], got_ob, s_ob, r_ob)
    for i in reversed(FAR_FIRST):
        z_a[i - 1].wait()
        c_a.append(to_core(slab_a, s_ca, r_ca, i))
    far.wait()

    lane = lax.broadcasted_iota(jnp.int32, (64, B), 1)
    sub = lax.broadcasted_iota(jnp.int32, (64, B), 0)

    def column(row):
        return jnp.transpose(jnp.broadcast_to(row, (128, 64)))[:, 0:1]

    lead_ridge = [column(jnp.where(z < 4, ridge4[k], ridge_far[k])) for k in range(4)]
    for k in range(4):
        mat[64 * k : 64 * k + 64, B:] = jnp.where(lane == sub + 64 * k, 1.0, 0.0).astype(F32)
    for copy in c_a:
        copy.wait()
    for k in range(4):
        rows = slab_a[4 * k : 4 * k + 4].reshape(64, B)
        mat[64 * k : 64 * k + 64, 0:B] = rows + jnp.where(lane == sub + 64 * k, lead_ridge[k], 0.0)

    turned = (((0,), (0,)), ((), ()))
    following, off = mat[0:NB, 0:128], 0
    for r0 in range(0, B, NB):
        r1 = r0 + NB
        if r0 == B * 3 // 4:
            for i in reversed(FAR_FIRST):
                z_b[i - 1].wait()
                c_b.append(to_core(slab_b, s_cb, r_cb, i))
        w = block_inverse(following, off)[:, 0:NB]
        if r1 == B:
            mat[r0:r1, B:] = dot(w, mat[r0:r1, B:])
            break
        c0, w1 = r1 // 128 * 128, B + (r1 + 127) // 128 * 128
        rj = dot(w, mat[r0:r1, c0:w1])
        mat[r0:r1, B:w1] = rj[:, B - c0 :]
        hi, mid, low = split3(rj)
        left = jnp.concatenate([hi, hi, mid, hi, low, mid], axis=0)
        right = jnp.concatenate([hi, mid, hi, low, hi, mid], axis=0)
        off = r1 - c0
        near = lax.dot_general(
            left[:, 0:128], right[:, 0:128], turned, preferred_element_type=F32
        )
        following = mat[r1 : r1 + NB, c0 : c0 + 128] - near[off : off + NB, :]
        step = lax.dot_general(left[:, : B - c0], right, turned, preferred_element_type=F32)
        mat[r1:B, c0:w1] -= step[off:, :]

    for copy in own_a:
        copy.wait()
    first = (e * 8 + p) * 64
    own_ridge = column(ridge_ref[...])
    winv = mat[:, B:]
    lead = oa_ref[x] + got_oa[0] + got_oa[1] + got_oa[2]
    lead = lead + jnp.where(lane == sub + first, own_ridge, 0.0)
    panel = dot(lead, winv, ((1,), (1,)))
    weight = dot(panel, winv)
    parts = jnp.concatenate(split3(weight), axis=0)
    out_ref[:, 0:B] = panel
    for copy in c_b:
        copy.wait()
    for copy in own_b:
        copy.wait()
    cols = lb_ref.shape[1]
    for j0 in range(0, cols, B):
        three = jnp.dot(
            parts, slab_b[:, :, j0 : j0 + B].reshape(B, B), preferred_element_type=F32
        )
        known = three[0:64] + three[64:128] + three[128:192]
        if j0 == 0:
            exact = [
                slab_a[4 * k : 4 * k + 4].reshape(64, B)
                + jnp.where(lane == sub + 64 * k, lead_ridge[k], 0.0)
                for k in range(4)
            ]
            known = jnp.where(y == 0, dot(weight, jnp.concatenate(exact, axis=0)), known)
        at = slice(j0, j0 + B)
        tile = oc_ref[:, at] + got_ob[0, :, at].astype(F32)
        tile = tile + got_ob[1, :, at].astype(F32) + got_ob[2, :, at].astype(F32)
        tile = tile + jnp.where(lane + (y * cols + j0) == sub + first, own_ridge, 0.0)
        out_ref[:, B + j0 : B + j0 + B] = tile - known


def split_kernel(both_ref, panel_ref, schur_ref):
    panel_ref[...] = both_ref[:, 0:B]
    schur_ref[...] = both_ref[:, B:]


def on_device(steps, harmonic, col_scale, taps, ridge):
    cols = harmonic.shape[0] // 4
    width = cols + B
    here, n_rows = 2048, 544
    dma = pltpu.SemaphoreType.DMA
    vmem = pltpu.VMEM
    both = pl.pallas_call(
        whole_kernel,
        out_shape=jax.ShapeDtypeStruct((64, width), F32),
        in_specs=[pl.BlockSpec(memory_space=pltpu.HBM)] * 5,
        out_specs=VMEM,
        scratch_shapes=[
            vmem(steps.shape, jnp.int32),
            vmem((32, 128), jnp.int32),
            vmem((32, 128), F32),
            vmem((2, 128), F32),
            vmem((1, 64), F32),
            dma((5,)),
            vmem((8, 2, steps.shape[1]), BF16),
            vmem((8, 1, 64), F32),
            vmem((2, steps.shape[1]), BF16),
            vmem((256, 128), F32),
            vmem((16, width), BF16),
            vmem((1, width), F32),
            vmem((n_rows, 16), BF16),
            vmem((n_rows, 128), F32),
            vmem((512, 256), BF16),
            vmem((128, 128), F32),
            *([vmem((BLK, width), BF16)] * 3),
            *([vmem((n_rows, BLK), BF16)] * 3),
            vmem((here, width), BF16),
            vmem((n_rows, here), BF16),
            *([vmem((width // B, B, B), F32)] * 3),
            *([vmem((16, cols), F32)] * 3),
            vmem((2, 16, B), F32),
            vmem((16, cols), F32),
            vmem((NX, 64, B), F32),
            vmem((NX, 64, cols), BF16),
            vmem((64, cols), F32),
            vmem((16, 16, B), F32),
            vmem((16, 16, cols), BF16),
            vmem((2 * NX - 1, 16, B), F32),
            vmem((NX - 1, 16, cols), F32),
            vmem((NX - 1, 64, B), F32),
            vmem((NX - 1, 64, cols), BF16),
            vmem((NX, 1, 64), F32),
            vmem((NX, 1, 64), F32),
            vmem((B, 2 * B), F32),
            *([dma((7,))] * 4), *([dma((5,))] * 2), dma, dma, *([dma((7,))] * 2), *([dma((3,))] * 8), dma, dma,
            *([dma((7,))] * 4), *([dma((8,))] * 4),
        ],
        compiler_params=pltpu.CompilerParams(
            collective_id=0, has_side_effects=True, vmem_limit_bytes=60 * 1024 * 1024
        ),
        name="whole",
    )(
        steps,
        harmonic.reshape(-1, 128),
        col_scale.reshape(-1, 128),
        taps.reshape(2, 128),
        ridge.reshape(1, -1),
    )
    return pl.pallas_call(
        split_kernel,
        out_shape=(
            jax.ShapeDtypeStruct((64, B), F32),
            jax.ShapeDtypeStruct((64, cols), F32),
        ),
        in_specs=[VMEM],
        out_specs=(VMEM, VMEM),
        name="split",
    )(both)


def solution(mesh):
    row = P(("epoch", "prow"))
    return jax.shard_map(
        on_device,
        mesh=mesh,
        in_specs=(P(None, "epoch"), P(), P(), P(), row),
        out_specs=(P(("epoch", "prow"), None), P(("epoch", "prow"), "pcol")),
        check_vma=False,
    )
```
